32 devices in a mesh: dp: 8 (over z, y), seq: 4 (over x, core).
Axes of the slice: x: 2, y: 2, z: 4, core: 2. Of those that a mesh axis runs over, the one named last changes fastest.
Arguments:
- tokens: bfloat16 [8, 2048, 768], P('dp', 'seq'), may hold values from -6 to 6
- lengths: int32 [8], P('dp'), may hold values from 512 to 2048, as said below
- qkv_weight: bfloat16 [768, 576], P('dp'), may hold values from -0.4375 to 0.4375
- qv_bias: bfloat16 [1536], P('dp'), may hold values from -0.75 to 0.75
- out_weight: bfloat16 [768, 768], P('dp'), may hold values from -4 to 4
- out_bias: bfloat16 [768], P('dp'), may hold values from -4 to 4
- norm_gain: bfloat16 [768], P('dp'), may hold values from 0.5 to 1.5
- norm_shift: bfloat16 [768], P('dp'), may hold values from -4 to 4
- up_weight: bfloat16 [768, 768], P('dp'), may hold values from -0.4375 to 0.4375
- up_bias: bfloat16 [3072], P('dp'), may hold values from -6 to 6
- down_weight: bfloat16 [3072, 192], P('dp'), may hold values from -0.21875 to 0.21875
- down_bias: bfloat16 [768], P('dp'), may hold values from -4 to 4
- final_gain: bfloat16 [768], P('dp'), may hold values from 0.5 to 1.5
- final_shift: bfloat16 [768], P('dp'), may hold values from -4 to 4
- grad_output: bfloat16 [8, 2048, 768], P('dp', 'seq'), may hold values from -6 to 6
Outputs:
- output: bfloat16 [8, 2048, 768], P('dp', 'seq')
- grad_tokens: bfloat16 [8, 2048, 768], P('dp', 'seq')
- grad_qkv_weight: float32 [768, 576], P('dp')
- grad_qv_bias: float32 [1536], P('dp')
- grad_out_weight: float32 [768, 768], P('dp')
- grad_out_bias: float32 [768], P('dp')
- grad_norm_gain: float32 [768], P('dp')
- grad_norm_shift: float32 [768], P('dp')
- grad_up_weight: float32 [768, 768], P('dp')
- grad_up_bias: float32 [3072], P('dp')
- grad_down_weight: float32 [3072, 192], P('dp')
- grad_down_bias: float32 [768], P('dp')
- grad_final_gain: float32 [768], P('dp')
- grad_final_shift: float32 [768], P('dp')
The draws below stay inside these ranges and needn't reach their ends.
Inputs may be any that keep to these rules, and one draw needn't show every extreme that they name: `lengths`: tokens at positions below the length are valid, the rest of the 2048 slots are padding; some sequence is full and some has 512.
All inputs are finite; a program needn't handle non-finite values.
Results may differ from the reference program's by a relative error of at most 0.015.
Values may be sent and summed in bfloat16 or wider, within the bound.
A program may use at most 128 MiB of HBM per device.

```python
import jax
import jax.numpy as jnp
from jax import lax

D = 768
FF = 3072
H = 12
GROUPS = 4
SLOT = 2048
HD = 64
QB = 512
BATCH = 8


def draw_lengths(key, part):
    key_one, key_two, key_three = jax.random.split(jax.random.fold_in(key, 17), 3)
    counts = jax.random.randint(key_one, (BATCH,), SLOT // 4, SLOT + 1)
    longest = jax.random.randint(key_two, (), 0, BATCH)
    shortest = (longest + 1 + jax.random.randint(key_three, (), 0, BATCH - 1)) % BATCH
    counts = counts.at[longest].set(SLOT).at[shortest].set(SLOT // 4)
    return counts.astype(jnp.int32)


def block_levels(own_key, extent, shards, smallest, largest):
    def one(axis_at, shards_of):
        draws = jax.random.uniform(jax.random.fold_in(jax.random.fold_in(own_key, 6), axis_at), (shards_of,), jnp.float32, smallest / len(shards), largest / len(shards))
        return jnp.repeat(jnp.exp(draws), extent[axis_at] // shards_of).reshape((-1,) + (1,) * (len(extent) - axis_at - 1))

    factor_of = one(*shards[0])
    for cut in shards[1:]:
        factor_of = factor_of * one(*cut)
    return factor_of


def scatter_about(key, extent, deviation, reach, cuts=(), kind=jnp.bfloat16):
    loudness = block_levels(key, extent, cuts, -0.22, 0.18) if cuts else 1.0
    array = jax.random.normal(key, extent, jnp.float32) * deviation * loudness
    return jnp.minimum(jnp.maximum(array, -reach), reach).astype(kind)


def setup_inputs(seed: int = 0) -> dict:
    splits = jax.random.split(jax.random.key(seed), 16)
    tokens = scatter_about(splits[0], (BATCH, SLOT, D), 1.0, 6.0, ((0, 8), (1, 4)))
    lengths = draw_lengths(jax.random.fold_in(splits[15], 71), 0)
    qkv_weight = scatter_about(splits[2], (D, 3 * D // GROUPS), (D // GROUPS) ** -0.5, 0.4375, ((0, 8),))
    qv_bias = scatter_about(splits[3], (2 * D,), 0.05, 0.75, ((0, 8),))
    out_weight = scatter_about(splits[4], (D, D), 2 ** -0.5, 4.0, ((0, 8),))
    out_bias = scatter_about(splits[5], (D,), 0.3, 4.0, ((0, 8),))
    norm_gain = jnp.clip(1.0 + 0.1 * jax.random.normal(splits[6], (D,), jnp.float32), 0.5, 1.5).astype(jnp.bfloat16)
    norm_shift = scatter_about(splits[7], (D,), 0.3, 4.0, ((0, 8),))
    up_weight = scatter_about(splits[8], (D, FF // GROUPS), (D // GROUPS) ** -0.5, 0.4375, ((0, 8),))
    up_bias = scatter_about(splits[9], (FF,), 0.5, 6.0, ((0, 8),))
    down_weight = scatter_about(splits[10], (FF, D // GROUPS), (FF // GROUPS) ** -0.5, 0.21875, ((0, 8),))
    down_bias = scatter_about(splits[11], (D,), 0.3, 4.0, ((0, 8),))
    final_gain = jnp.clip(1.0 + 0.1 * jax.random.normal(splits[12], (D,), jnp.float32), 0.5, 1.5).astype(jnp.bfloat16)
    final_shift = scatter_about(splits[13], (D,), 0.3, 4.0, ((0, 8),))
    grad_output = scatter_about(splits[14], (BATCH, SLOT, D), 1.0, 6.0, ((0, 8), (1, 4)))
    return {"tokens": tokens, "lengths": lengths, "qkv_weight": qkv_weight, "qv_bias": qv_bias, "out_weight": out_weight, "out_bias": out_bias, "norm_gain": norm_gain, "norm_shift": norm_shift, "up_weight": up_weight, "up_bias": up_bias, "down_weight": down_weight, "down_bias": down_bias, "final_gain": final_gain, "final_shift": final_shift, "grad_output": grad_output}


@jax.custom_vjp
def low(v):
    return lax.optimization_barrier(v.astype(jnp.bfloat16)).astype(jnp.float32)

@jax.custom_vjp
def low_back(v):
    return v

def low_keep(v):
    return (low(v), None)

def low_pass(kept, grad):
    return (grad,)

def back_keep(v):
    return (v, None)

def back_low(kept, grad):
    return (low(grad),)
low.defvjp(low_keep, low_pass)
low_back.defvjp(back_keep, back_low)
epsilon = 1e-05
masked_score = -1000000000.0
highest = lax.Precision.HIGHEST

def norm_rows(values, scales, shifts):
    row_mean = lax.optimization_barrier(jnp.mean(values, axis=-1, keepdims=True))
    centred = values - row_mean
    row_var = lax.optimization_barrier(jnp.mean(centred * centred, axis=-1, keepdims=True))
    return centred * lax.rsqrt(row_var + epsilon) * scales + shifts

def grouped(values, matrix):
    tok_rows = values.shape[0]
    split_rows = values.reshape(tok_rows, GROUPS, -1)
    split_matrix = matrix.reshape(GROUPS, split_rows.shape[2], -1)
    result = jnp.einsum('ngi,gio->ngo', split_rows, split_matrix, precision=highest)
    return result.reshape(tok_rows, -1)

def layer(values, length, qkv_weight, qv_bias, out_weight, out_bias, norm_gain, norm_shift, up_weight, up_bias, down_weight, down_bias, final_gain, final_shift):
    tok_rows, model_width = values.shape
    group_width = model_width // GROUPS
    mixed_qkv = grouped(values, qkv_weight).reshape(tok_rows, GROUPS, 3, group_width)
    bias_block = jnp.stack([qv_bias[:model_width].reshape(GROUPS, group_width), jnp.zeros((GROUPS, group_width), jnp.float32), qv_bias[model_width:].reshape(GROUPS, group_width)], axis=1)
    projected = low_back(low(mixed_qkv + bias_block))
    query_rows = projected[:, :, 0].reshape(tok_rows, H, HD)
    key_rows = projected[:, :, 1].reshape(tok_rows, H, HD)
    value_rows = projected[:, :, 2].reshape(tok_rows, H, HD)
    valid_keys = jnp.arange(tok_rows) < length
    score_scale = HD ** (-0.5)

    def attend_block(block_start):
        block_query = lax.dynamic_slice_in_dim(query_rows, block_start, QB, 0)
        raw_scores = jnp.einsum('qhd,khd->hqk', block_query, key_rows, precision=highest)
        scores = low_back(raw_scores * score_scale)
        scores = jnp.where(valid_keys[None, None, :], scores, masked_score)
        row_max = lax.optimization_barrier(jnp.max(scores, axis=-1, keepdims=True))
        exponent = jnp.exp(scores - row_max)
        weights = low(exponent / lax.optimization_barrier(jnp.sum(exponent, axis=-1, keepdims=True)))
        return jnp.einsum('hqk,khd->qhd', weights, value_rows, precision=highest)
    block_starts = (jnp.arange(tok_rows // QB) * QB).astype(jnp.int32)
    context = lax.map(jax.checkpoint(attend_block), block_starts)
    context = low_back(low(context.reshape(tok_rows, model_width)))
    attended = low_back(jnp.dot(context, out_weight, precision=highest)) + out_bias
    mixed = norm_rows(values + attended, norm_gain, norm_shift)
    upper = low_back(grouped(low(mixed), up_weight)) + up_bias
    active = low(jax.nn.gelu(upper, approximate=False))
    lowered = low_back(grouped(active, down_weight)) + down_bias
    normed = norm_rows(mixed + lowered, final_gain, final_shift)
    return normed * valid_keys[:, None].astype(jnp.float32)

def reference(tokens, lengths, qkv_weight, qv_bias, out_weight, out_bias, norm_gain, norm_shift, up_weight, up_bias, down_weight, down_bias, final_gain, final_shift, grad_output):
    params = tuple((param.astype(jnp.float32) for param in (qkv_weight, qv_bias, out_weight, out_bias, norm_gain, norm_shift, up_weight, up_bias, down_weight, down_bias, final_gain, final_shift)))
    zeroed = tuple((jnp.zeros_like(param) for param in params))

    def one_sequence(carried, sequence):
        seq_tokens, seq_length, seq_grad = sequence

        def forward(values, *weights):
            return layer(values, seq_length, *weights)
        result, pull_back = jax.vjp(forward, seq_tokens.astype(jnp.float32), *params)
        grads = pull_back(seq_grad.astype(jnp.float32))
        carried = tuple((total + grad for total, grad in zip(carried, grads[1:])))
        return (carried, (result.astype(jnp.bfloat16), grads[0].astype(jnp.bfloat16)))
    totals, (outputs, grad_inputs) = lax.scan(one_sequence, zeroed, (tokens, lengths, grad_output))
    return (outputs, grad_inputs, totals[0], totals[1], totals[2], totals[3], totals[4], totals[5], totals[6], totals[7], totals[8], totals[9], totals[10], totals[11])
```

```python
import functools

import jax
import jax.numpy as jnp
from jax import lax
from jax.experimental import pallas as pl
from jax.experimental.pallas import tpu as pltpu
from jax.sharding import PartitionSpec as P

H = 12
GROUPS = 4
HD = 64
epsilon = 1e-05
LOG2E = 1.4426950408889634
MASKED = -1e30
F32 = jnp.float32
BF16 = jnp.bfloat16


def mm(a, b):
    return jnp.dot(a, b, preferred_element_type=F32)


def mm_nt(a, b):
    return lax.dot_general(a, b, (((1,), (1,)), ((), ())), preferred_element_type=F32)


def mm_tn(a, b):
    return lax.dot_general(a, b, (((0,), (0,)), ((), ())), preferred_element_type=F32)


def pad_rows(w, half):
    zeros = jnp.zeros((64, w.shape[1]), w.dtype)
    return jnp.concatenate([w, zeros] if half == 0 else [zeros, w], axis=0)


def pad_lanes(w, half):
    zeros = jnp.zeros((w.shape[0], 64), w.dtype)
    return jnp.concatenate([w, zeros] if half == 0 else [zeros, w], axis=1)


def window(half):
    return slice(half * 128, half * 128 + 256)


def attend_kernel(len_ref, x_ref, w_ref, b_ref, ctx_ref, linv_ref, e_ref, k_out, qT_out, vT_out, qe, ke, ve):
    heads = qe.shape[0]
    sources, rows, _ = x_ref.shape
    gw = heads * HD
    slot = sources * 2 * rows

    @pl.when(pl.program_id(0) == 0)
    def _():
        scale = HD ** (-0.5) * LOG2E
        lane = lax.broadcasted_iota(jnp.int32, (slot, 128), 1)
        ones_lane = jnp.where(lane == 0, 1.0, 0.0).astype(BF16)
        key_pos = lax.broadcasted_iota(jnp.int32, (128, slot), 1)
        key_row = lax.broadcasted_iota(jnp.int32, (128, slot), 0)
        bias = jnp.where((key_row == 0) & (key_pos >= len_ref[0]), MASKED, 0.0).astype(BF16)
        for h in range(heads):
            qe[h, :, 128:256] = ones_lane
            ke[h, 128:256, :] = bias
        for s in range(sources):
            for half in range(2):
                at = (s * 2 + half) * rows
                w = pad_rows(w_ref[...], half)
                qkv = (mm(x_ref[s, :, window(half)], w) + b_ref[...]).astype(BF16)
                q = qkv[:, :gw]
                k = qkv[:, gw : 2 * gw]
                v = qkv[:, 2 * gw :]
                k_out[at : at + rows, :] = k
                qT_out[:, at : at + rows] = q.T
                vT_out[:, at : at + rows] = v.T
                kT = k.T
                scaled = q.astype(F32) * scale
                hi = scaled.astype(BF16)
                lo = (scaled - hi.astype(F32)).astype(BF16)
                ones = jnp.ones((rows, HD), BF16)
                for h in range(heads):
                    c = slice(h * HD, (h + 1) * HD)
                    qe[h, at : at + rows, 0:128] = jnp.concatenate([hi[:, c], lo[:, c]], axis=1)
                    ke[h, 0:HD, at : at + rows] = kT[c, :]
                    ke[h, HD : 2 * HD, at : at + rows] = kT[c, :]
                    ve[h, at : at + rows, :] = jnp.concatenate([v[:, c], ones], axis=1)

    s = pl.program_id(0)
    parts = []
    for half in range(2):
        inverse = []
        at = pl.multiple_of((s * 2 + half) * rows, rows)
        for h in range(heads):
            scores = mm(qe[h, pl.ds(at, rows), :], ke[h])
            top = jnp.max(scores, axis=1, keepdims=True)
            e = jnp.exp2(scores - top).astype(BF16)
            e_ref[h, half * rows : (half + 1) * rows, :] = e
            o = mm(e, ve[h])
            inv = 1.0 / o[:, HD:]
            inverse.append(inv)
            parts.append((o[:, :HD] * inv).astype(BF16))
        linv_ref[0, half] = jnp.concatenate(inverse, axis=1)
    ctx_ref[0] = jnp.concatenate(parts, axis=1)


def attend(length, x, w, b):
    sources, rows, _ = x.shape
    gw = w.shape[0]
    heads = gw // HD
    slot = sources * 2 * rows
    whole = lambda *shape: pl.BlockSpec(shape, lambda s: (0,) * len(shape))
    return pl.pallas_call(
        attend_kernel,
        grid=(sources,),
        in_specs=[
            pl.BlockSpec(memory_space=pltpu.SMEM),
            whole(*x.shape),
            whole(*w.shape),
            whole(*b.shape),
        ],
        out_specs=[
            pl.BlockSpec((1, rows, 2 * gw), lambda s: (s, 0, 0)),
            pl.BlockSpec((1, 2, rows, gw), lambda s: (s, 0, 0, 0)),
            pl.BlockSpec((heads, 2 * rows, slot), lambda s: (0, s, 0)),
            whole(slot, gw),
            whole(gw, slot),
            whole(gw, slot),
        ],
        out_shape=[
            jax.ShapeDtypeStruct((sources, rows, 2 * gw), BF16),
            jax.ShapeDtypeStruct((sources, 2, rows, gw), F32),
            jax.ShapeDtypeStruct((heads, slot, slot), BF16),
            jax.ShapeDtypeStruct((slot, gw), BF16),
            jax.ShapeDtypeStruct((gw, slot), BF16),
            jax.ShapeDtypeStruct((gw, slot), BF16),
        ],
        scratch_shapes=[
            pltpu.VMEM((heads, slot, 256), BF16),
            pltpu.VMEM((heads, 256, slot), BF16),
            pltpu.VMEM((heads, slot, 128), BF16),
        ],
        compiler_params=pltpu.CompilerParams(vmem_limit_bytes=60 << 20),
        name="attend",
    )(length, x, w, b)


def revisit_kernel(
    e_ref, gctx_ref, ctx_ref, linv_ref, qT_ref, vT_ref, k_ref, x_ref, w_ref,
    gi_ref, gw_ref, gb_ref, vTe, kn, dkT, dvT, gT,
):
    heads = kn.shape[0]
    sources, rows, _ = x_ref.shape
    gw = heads * HD
    slot = sources * 2 * rows
    s = pl.program_id(0)

    @pl.when(s == 0)
    def _():
        dkT[...] = jnp.zeros_like(dkT)
        dvT[...] = jnp.zeros_like(dvT)
        row = lax.broadcasted_iota(jnp.int32, (HD, slot), 0)
        ones_rows = jnp.where(row < 2, 1.0, 0.0).astype(BF16)
        for h in range(heads):
            c = slice(h * HD, (h + 1) * HD)
            vTe[h, 0:HD, :] = vT_ref[c, :]
            vTe[h, HD:, :] = ones_rows
            kn[h] = k_ref[:, c]

    lane = lax.broadcasted_iota(jnp.int32, (rows, HD), 1)
    for half in range(2):
        at = pl.multiple_of((s * 2 + half) * rows, rows)
        lanes = slice(half * gw, (half + 1) * gw)
        g = gctx_ref[0, :, lanes].astype(F32) * linv_ref[0, half]
        g_low = g.astype(BF16)
        gT_low = g_low.T
        prod = g * ctx_ref[0, :, lanes].astype(F32)
        dqs = []
        for h in range(heads):
            c = slice(h * HD, (h + 1) * HD)
            delta = -jnp.sum(prod[:, c], axis=1, keepdims=True)
            d_hi = delta.astype(BF16)
            d_lo = (delta - d_hi.astype(F32)).astype(BF16)
            tail = jnp.where(lane == 0, d_hi, jnp.where(lane == 1, d_lo, jnp.zeros((), BF16)))
            ge = jnp.concatenate([g_low[:, c], tail], axis=1)
            e = e_ref[h, half * rows : (half + 1) * rows, :]
            ds = (e.astype(F32) * mm(ge, vTe[h])).astype(BF16)
            dvT[c, :] += mm(gT_low[c, :], e)
            dkT[c, :] += mm(qT_ref[c, half * rows : (half + 1) * rows], ds)
            dqs.append((mm(ds, kn[h]) * (HD ** (-0.5))).astype(BF16))
        gT[0:gw, pl.ds(at, rows)] = jnp.concatenate(dqs, axis=1).T

    @pl.when(s == sources - 1)
    def _():
        gT[gw : 2 * gw, :] = (dkT[...] * (HD ** (-0.5))).astype(BF16)
        gT[2 * gw :, :] = dvT[...].astype(BF16)
        gb_ref[...] = mm_nt(jnp.ones((8, slot), BF16), gT[...])
        sums = [None, None]
        for t in range(sources):
            packed = []
            for half in range(2):
                cols = slice((t * 2 + half) * rows, (t * 2 + half + 1) * rows)
                part = mm(gT[:, cols], x_ref[t, :, window(half)])
                sums[half] = part if sums[half] is None else sums[half] + part
                packed.append(mm(w_ref[...], gT[:, cols]).T.astype(BF16))
            gi_ref[t] = jnp.concatenate(packed, axis=1)
        gw_ref[...] = (sums[0][:, :gw] + sums[1][:, 64:]).T


def revisit(e, gctx, ctx, linv, qT, vT, k, x, w):
    sources, rows, _ = x.shape
    gw = w.shape[0]
    heads = gw // HD
    slot = sources * 2 * rows
    whole = lambda *shape: pl.BlockSpec(shape, lambda s: (0,) * len(shape))
    return pl.pallas_call(
        revisit_kernel,
        grid=(sources,),
        in_specs=[
            pl.BlockSpec((heads, 2 * rows, slot), lambda s: (0, s, 0)),
            pl.BlockSpec((1, rows, 2 * gw), lambda s: (s, 0, 0)),
            pl.BlockSpec((1, rows, 2 * gw), lambda s: (s, 0, 0)),
            pl.BlockSpec((1, 2, rows, gw), lambda s: (s, 0, 0, 0)),
            pl.BlockSpec((gw, 2 * rows), lambda s: (0, s)),
            whole(*vT.shape),
            whole(*k.shape),
            whole(*x.shape),
            whole(*w.shape),
        ],
        out_specs=[whole(*x.shape), whole(gw, 3 * gw), whole(8, 3 * gw)],
        out_shape=[
            jax.ShapeDtypeStruct(x.shape, BF16),
            jax.ShapeDtypeStruct((gw, 3 * gw), F32),
            jax.ShapeDtypeStruct((8, 3 * gw), F32),
        ],
        scratch_shapes=[
            pltpu.VMEM((heads, 2 * HD, slot), BF16),
            pltpu.VMEM((heads, slot, HD), BF16),
            pltpu.VMEM((gw, slot), F32),
            pltpu.VMEM((gw, slot), F32),
            pltpu.VMEM((3 * gw, slot), BF16),
        ],
        compiler_params=pltpu.CompilerParams(vmem_limit_bytes=60 << 20),
        name="revisit",
    )(e, gctx, ctx, linv, qT, vT, k, x, w)


def split_rows(values):
    mean = jnp.mean(values, axis=-1, keepdims=True)
    centred = values - mean
    var = jnp.mean(centred * centred, axis=-1, keepdims=True)
    return centred, lax.rsqrt(var + epsilon)


def norm_back(grad, unit, inverse, gain):
    g = grad * gain
    m1 = jnp.mean(g, axis=-1, keepdims=True)
    m2 = jnp.mean(g * unit, axis=-1, keepdims=True)
    return inverse * (g - m1 - unit * m2)


def join_windows(parts):
    tiles = []
    for even, odd in zip(parts[0::2], parts[1::2]):
        tiles += [even[:, :128], even[:, 128:] + odd[:, :128], odd[:, 128:]]
    return jnp.concatenate(tiles, axis=1)


def group_window(g):
    at = (g // 2) * 384 + (g % 2) * 128
    return slice(at, at + 256)


def middle_kernel(
    pos_ref, ctx_ref, tok_ref, gout_ref, wo_ref, wu_ref, wd_ref, vec_ref, ub_ref,
    out_ref, gctx_ref, gres_ref, gwo_ref, gwu_ref, gwd_ref, small_ref, upad, dpad, gelu_low,
):
    rows = ctx_ref.shape[1]
    gw = ctx_ref.shape[2] // 2
    width = tok_ref.shape[1]
    hidden = wu_ref.shape[1]
    obias, gain1, shift1, dbias, gain2, shift2 = (vec_ref[i : i + 1, :].astype(F32) for i in range(6))
    for g in range(GROUPS):
        upad[g] = pad_rows(wu_ref[g * gw : (g + 1) * gw, :], g % 2)
        dpad[g] = pad_lanes(wd_ref[g * hidden : (g + 1) * hidden, :], g % 2)
    packed = [[] for _ in range(GROUPS)]
    for half in range(2):
        first = half == 0

        def keep(ref, at, value):
            if first:
                ref[at] = value
            else:
                ref[at] += value

        r = slice(half * rows, (half + 1) * rows)
        x = tok_ref[r, :].astype(F32) + obias
        for g in range(GROUPS):
            x += mm(ctx_ref[g, :, window(half)], pad_rows(wo_ref[g * gw : (g + 1) * gw, :], half))
        c1, i1 = split_rows(x)
        n1 = c1 * i1
        mixed = n1 * gain1 + shift1
        low = mixed.astype(BF16)
        lowered = []
        slopes = []
        actives = []
        for g in range(GROUPS):
            u = mm(low[:, group_window(g)], upad[g]) + ub_ref[g : g + 1, :].astype(F32)
            phi = 0.5 + 0.5 * lax.erf(u * (0.5 ** 0.5))
            slope = phi + u * (jnp.exp(u * u * -0.5) * 0.3989422804014327)
            act = (u * phi).astype(BF16)
            actives.append(act)
            slopes.append(slope)
            lowered.append(mm(act, dpad[g]))
        x = mixed + join_windows(lowered) + dbias
        c2, i2 = split_rows(x)
        n2 = c2 * i2
        row = lax.broadcasted_iota(jnp.int32, (rows, 1), 0) + (pos_ref[1] + half * rows)
        valid = jnp.where(row < pos_ref[0], 1.0, 0.0)
        out_ref[r, :] = (valid * (n2 * gain2 + shift2)).astype(BF16)
        gy = gout_ref[r, :].astype(F32) * valid
        d2 = norm_back(gy, n2, i2, gain2)
        keep(small_ref, slice(4, 5), jnp.sum(gy * n2, axis=0, keepdims=True))
        keep(small_ref, slice(5, 6), jnp.sum(gy, axis=0, keepdims=True))
        keep(small_ref, slice(3, 4), jnp.sum(d2, axis=0, keepdims=True))
        d2_low = d2.astype(BF16)
        backs = []
        for g in range(GROUPS):
            win = d2_low[:, group_window(g)]
            keep(gwd_ref, g, mm_tn(actives[g], win))
            gu = mm_nt(win, dpad[g]) * slopes[g]
            keep(small_ref, slice(6 + g, 7 + g), jnp.sum(gu, axis=0, keepdims=True))
            gu_low = gu.astype(BF16)
            keep(gwu_ref, g, mm_tn(low[:, group_window(g)], gu_low))
            backs.append(mm_nt(gu_low, upad[g]))
        gm = join_windows(backs) + d2
        d1 = norm_back(gm, n1, i1, gain1)
        keep(small_ref, slice(1, 2), jnp.sum(gm * n1, axis=0, keepdims=True))
        keep(small_ref, slice(2, 3), jnp.sum(gm, axis=0, keepdims=True))
        keep(small_ref, slice(0, 1), jnp.sum(d1, axis=0, keepdims=True))
        gres_ref[r, :] = d1
        d1_low = d1.astype(BF16)
        for g in range(GROUPS):
            part = mm_tn(ctx_ref[g, :, window(half)], d1_low)
            keep(gwo_ref, slice(g * gw, (g + 1) * gw), part[64 * half : 64 * half + gw])
        back = mm_nt(d1_low, wo_ref[...]).astype(BF16)
        for g in range(GROUPS):
            packed[g].append(back[:, g * gw : (g + 1) * gw])
    small_ref[10:16, :] = jnp.zeros((6, width), F32)
    for g in range(GROUPS):
        gctx_ref[g] = jnp.concatenate(packed[g], axis=1)


def middle(pos, ctx, tok, gout, wo, wu, wd, vec, ub):
    hidden = wu.shape[1]
    width = tok.shape[1]
    vmem = pl.BlockSpec(memory_space=pltpu.VMEM)
    return pl.pallas_call(
        middle_kernel,
        in_specs=[pl.BlockSpec(memory_space=pltpu.SMEM)] + [vmem] * 8,
        out_specs=[vmem] * 7,
        out_shape=[
            jax.ShapeDtypeStruct(tok.shape, BF16),
            jax.ShapeDtypeStruct(ctx.shape, BF16),
            jax.ShapeDtypeStruct(tok.shape, F32),
            jax.ShapeDtypeStruct(wo.shape, F32),
            jax.ShapeDtypeStruct((GROUPS, 256, hidden), F32),
            jax.ShapeDtypeStruct((GROUPS, hidden, 256), F32),
            jax.ShapeDtypeStruct((16, width), F32),
        ],
        scratch_shapes=[
            pltpu.VMEM((GROUPS, 256, hidden), BF16),
            pltpu.VMEM((GROUPS, hidden, 256), BF16),
            pltpu.VMEM((8, 128), F32),
        ],
        compiler_params=pltpu.CompilerParams(vmem_limit_bytes=62 << 20),
        name="middle",
    )(pos, ctx, tok, gout, wo, wu, wd, vec, ub)


def on_device(
    tokens, lengths, qkv_weight, qv_bias, out_weight, out_bias, norm_gain, norm_shift,
    up_weight, up_bias, down_weight, down_bias, final_gain, final_shift, grad_output,
):
    _, piece_rows, width = tokens.shape
    gw = width // GROUPS
    half = piece_rows // 2
    hidden = up_weight.shape[1]
    me = lax.axis_index("seq")
    gather = lambda a: lax.all_gather(a, "dp", axis=0, tiled=True)
    qkv_full, qv_full = gather(qkv_weight), gather(qv_bias)
    wo, wu, wd = gather(out_weight), gather(up_weight), gather(down_weight)
    vec = jnp.stack([gather(a) for a in (out_bias, norm_gain, norm_shift, down_bias, final_gain, final_shift)])
    vec = jnp.concatenate([vec, jnp.zeros((2, width), BF16)])
    ub = gather(up_bias).reshape(GROUPS, hidden)
    w = lax.dynamic_slice_in_dim(qkv_full, me * gw, gw, 0)
    bias = qv_full.astype(F32).reshape(2, GROUPS, gw)
    bias = lax.dynamic_index_in_dim(bias, me, 1, keepdims=False)
    b = jnp.concatenate([bias[0], jnp.zeros((gw,), F32), bias[1]])[None, :]

    def pack(t):
        return t.reshape(2, half, GROUPS, gw).transpose(2, 1, 0, 3).reshape(GROUPS, half, 2 * gw)

    def unpack(t):
        return t.reshape(GROUPS, half, 2, gw).transpose(2, 1, 0, 3).reshape(piece_rows, width)

    def swap(t):
        return lax.all_to_all(t, "seq", split_axis=0, concat_axis=0, tiled=True)

    x = swap(pack(tokens))
    ctx, linv, e, k, qT, vT = attend(lengths, x, w, b)
    pos = jnp.stack([lengths[0], (me * piece_rows).astype(jnp.int32)])
    ctx_pos = swap(ctx)
    output, gctx, gres, gwo, gwu, gwd, small = middle(
        pos, ctx_pos, tokens[0], grad_output[0], wo, wu, wd, vec, ub
    )
    gi, gwt, gb = revisit(e, swap(gctx), ctx, linv, qT, vT, k, x, w)
    grad_tokens = (unpack(swap(gi)).astype(F32) + gres).astype(BF16)[None]
    gwu = jnp.concatenate([gwu[g, 64 * (g % 2) : 64 * (g % 2) + gw] for g in range(GROUPS)], axis=0)
    gwd = jnp.concatenate([gwd[g, :, 64 * (g % 2) : 64 * (g % 2) + gw] for g in range(GROUPS)], axis=0)
    gqkv = lax.dynamic_update_slice_in_dim(jnp.zeros((width, 3 * gw), F32), gwt, me * gw, 0)
    gqv = jnp.zeros((2, GROUPS, gw), F32)
    gqv = lax.dynamic_update_slice(gqv, jnp.stack([gb[0, :gw], gb[0, 2 * gw :]])[:, None], (0, me, 0))

    def total(a):
        return lax.psum(lax.psum_scatter(a, "dp", scatter_dimension=0, tiled=True), "seq")

    return (
        output[None], grad_tokens, total(gqkv), total(gqv.reshape(-1)), total(gwo), total(small[0]),
        total(small[1]), total(small[2]), total(gwu), total(small[6:10].reshape(-1)), total(gwd),
        total(small[3]), total(small[4]), total(small[5]),
    )


def solution(mesh):
    rows = P("dp", "seq", None)
    mat = P("dp", None)
    vec = P("dp")
    in_specs = (rows, vec, mat, vec, mat, vec, vec, vec, mat, vec, mat, vec, vec, vec, rows)
    out_specs = (rows, rows, mat, vec, mat, vec, vec, vec, mat, vec, mat, vec, vec, vec)
    return jax.shard_map(on_device, mesh=mesh, in_specs=in_specs, out_specs=out_specs, check_vma=False)
```

```python
import functools

import jax
import jax.numpy as jnp
from jax import lax
from jax.experimental import pallas as pl
from jax.experimental.pallas import tpu as pltpu
from jax.sharding import PartitionSpec as P

H = 12
GROUPS = 4
HD = 64
epsilon = 1e-05
LOG2E = 1.4426950408889634
MASKED = -1e30
F32 = jnp.float32
BF16 = jnp.bfloat16


def mm(a, b):
    return jnp.dot(a, b, preferred_element_type=F32)


def mm_nt(a, b):
    return lax.dot_general(a, b, (((1,), (1,)), ((), ())), preferred_element_type=F32)


def mm_tn(a, b):
    return lax.dot_general(a, b, (((0,), (0,)), ((), ())), preferred_element_type=F32)


def pad_rows(w, half):
    zeros = jnp.zeros((64, w.shape[1]), w.dtype)
    return jnp.concatenate([w, zeros] if half == 0 else [zeros, w], axis=0)


def pad_lanes(w, half):
    zeros = jnp.zeros((w.shape[0], 64), w.dtype)
    return jnp.concatenate([w, zeros] if half == 0 else [zeros, w], axis=1)


def window(half):
    return slice(half * 128, half * 128 + 256)


MESH = pl.DeviceIdType.MESH


def remote(src, dst, send_sem, recv_sem, dp, seq):
    return pltpu.make_async_remote_copy(
        src_ref=src, dst_ref=dst, send_sem=send_sem, recv_sem=recv_sem,
        device_id={"dp": dp, "seq": seq}, device_id_type=MESH,
    )


def greet(n, group, i, s):
    barrier = pltpu.get_barrier_semaphore()
    for d in range(1, n):
        pl.semaphore_signal(barrier, inc=1, device_id={"dp": lax.rem(i + d, n), "seq": s}, device_id_type=MESH)
    for d in range(1, group):
        pl.semaphore_signal(barrier, inc=1, device_id={"dp": i, "seq": lax.rem(s + d, group)}, device_id_type=MESH)
    pl.semaphore_wait(barrier, n + group - 2)


def other(index):
    return index + 1 - 2 * lax.rem(index, 2)


def half_of(ref, lead, c):
    if len(ref.shape) == len(lead) + 3:
        return ref.at[lead + (c,)]
    lanes = ref.shape[-1] // 2
    at = pl.multiple_of(c * lanes, 128) if lanes % 128 == 0 else c * lanes
    return ref.at[lead + (slice(None), pl.ds(at, lanes))]


def stack_rows(pieces):
    if len(pieces) == 1:
        return pieces[0]
    if pieces[0].shape[0] % 16 == 0:
        return jnp.concatenate(pieces, axis=0)
    return jnp.concatenate([p.astype(F32) for p in pieces], axis=0).astype(pieces[0].dtype)


def join_lanes(pieces):
    return pieces[0] if len(pieces) == 1 else jnp.concatenate(pieces, axis=1)


def attend_kernel(
    n, per, len_ref, x_in, wq_in, vec_in, wo_in, wu_in, wd_in,
    ctx_ref, linv_ref, e_ref, k_out, qT_out, vT_out, w_out, vec_out, x_out, ctx_pos, wo_out, wu_out, wd_out,
    qe, ke, ve, x_buf, ctx_buf, wq_buf, vec_buf,
    x_send, x_recv, c_send, c_recv, q_send, q_recv, v_send, v_recv, z_send, z_recv, y_send, y_recv, p_send, p_recv, own, local,
):
    heads = qe.shape[0]
    sources, rows, _ = x_buf.shape
    gw = heads * HD
    slot = sources * 2 * rows
    parts_q = wq_buf.shape[0]
    t = pl.program_id(0)
    i = lax.axis_index("dp")
    me = lax.axis_index("seq")
    c = lax.rem(me, 2)
    y = lax.rem(i, 2)
    k = i // 2
    depth = n // 2
    weights = ((wo_in, wo_out), (wu_in, wu_out), (wd_in, wd_out))

    def x_copy(d):
        peer = lax.rem(me + d, sources)
        return remote(x_in.at[peer], x_buf.at[sources - 1 - d], x_send.at[d - 1], x_recv.at[d - 1], i, peer)

    def ctx_copy(d):
        peer = lax.rem(me + d, sources)
        return remote(ctx_buf.at[d - 1], ctx_pos.at[me], c_send.at[d - 1], c_recv.at[d - 1], i, peer)

    def q_copy(d):
        piece = jnp.clip(i - me * parts_q, 0, parts_q - 1)
        return remote(wq_in, wq_buf.at[piece], q_send.at[d - 1], q_recv.at[piece], lax.rem(i + d, n), me)

    def v_copy(d):
        return remote(vec_in, vec_buf.at[i], v_send.at[d - 1], v_recv.at[d - 1], lax.rem(i + d, n), me)

    def z_copy(w, d):
        src, dst = weights[w]
        to = lax.rem(k + d, depth)
        return remote(
            half_of(src, (), c), half_of(dst, (k, y), c), z_send.at[w, d - 1], z_recv.at[w, d - 1], to * 2 + y, me
        )

    def own_copy(w):
        src, dst = weights[w]
        return pltpu.make_async_copy(half_of(src, (), c), half_of(dst, (k, y), c), own.at[w])

    def y_copy(w):
        part = half_of(weights[w][1], (slice(None), y), c)
        return remote(part, part, y_send.at[w], y_recv.at[w], other(i), me)

    def p_copy(w):
        part = half_of(weights[w][1], (slice(None), slice(None)), c)
        return remote(part, part, p_send.at[w], p_recv.at[w], i, other(me))

    x_own = pltpu.make_async_copy(x_in.at[me], x_buf.at[sources - 1], local.at[0])
    x_keep = pltpu.make_async_copy(x_buf, x_out, local.at[1])
    v_own = pltpu.make_async_copy(vec_in, vec_buf.at[i], local.at[2])
    ctx_own = pltpu.make_async_copy(ctx_buf.at[sources - 1], ctx_pos.at[me], local.at[3])
    sender = i // parts_q == me

    @pl.when(t == 0)
    def _():
        greet(n, sources, i, me)
        for d in (2, 1, 3):
            x_copy(d).start()
        x_own.start()

        @pl.when(sender)
        def _():
            for d in range(1, n):
                q_copy(d).start()
            pltpu.make_async_copy(wq_in, wq_buf.at[jnp.clip(i - me * parts_q, 0, parts_q - 1)], local.at[4]).start()

        v_own.start()
        for d in range(1, n):
            v_copy(d).start()
        for w in range(3):
            for d in range(1, depth):
                z_copy(w, d).start()
            own_copy(w).start()

        scale = HD ** (-0.5) * LOG2E
        lane = lax.broadcasted_iota(jnp.int32, (slot, 128), 1)
        ones_lane = jnp.where(lane == 0, 1.0, 0.0).astype(BF16)
        key_row = lax.broadcasted_iota(jnp.int32, (128, 2 * rows), 0)
        for h in range(heads):
            qe[h, :, 128:256] = ones_lane
        for j in range(sources):
            first = lax.rem(me + 1 + j, sources) * (2 * rows)
            key_pos = lax.broadcasted_iota(jnp.int32, (128, 2 * rows), 1) + first
            bias = jnp.where((key_row == 0) & (key_pos >= len_ref[0]), MASKED, 0.0).astype(BF16)
            for h in range(heads):
                ke[h, 128:256, j * 2 * rows : (j + 1) * 2 * rows] = bias

        for piece in range(parts_q):
            @pl.when(jnp.logical_not(jnp.logical_and(sender, i - me * parts_q == piece)))
            def _():
                remote(wq_in, wq_buf.at[piece], q_send.at[0], q_recv.at[piece], other(i), me).wait_recv()

        @pl.when(sender)
        def _():
            pltpu.make_async_copy(wq_in, wq_buf.at[jnp.clip(i - me * parts_q, 0, parts_q - 1)], local.at[4]).wait()

        v_own.wait()
        for d in range(1, n):
            v_copy(d).wait_recv()
        vec_out[...] = vec_buf[...]
        count = gw // per
        q_bias = join_lanes([vec_buf[me * count + u, 0:1, 0:per] for u in range(count)])
        v_bias = join_lanes([vec_buf[(GROUPS + me) * count + u, 0:1, 0:per] for u in range(count)])
        b = jnp.concatenate([q_bias, jnp.zeros((1, gw), F32), v_bias], axis=1)
        weight = stack_rows([wq_buf[u] for u in range(parts_q)])
        w_out[...] = weight
        x_own.wait()
        for j in (3, 0, 2, 1):
            if j < sources - 1:
                x_copy(sources - 1 - j).wait_recv()
            for half in range(2):
                at = (j * 2 + half) * rows
                w = pad_rows(weight, half)
                qkv = (mm(x_buf[j, :, window(half)], w) + b).astype(BF16)
                q = qkv[:, :gw]
                kk = qkv[:, gw : 2 * gw]
                v = qkv[:, 2 * gw :]
                k_out[at : at + rows, :] = kk
                qT_out[:, at : at + rows] = q.T
                vT_out[:, at : at + rows] = v.T
                kT = kk.T
                scaled = q.astype(F32) * scale
                hi = scaled.astype(BF16)
                lo = (scaled - hi.astype(F32)).astype(BF16)
                ones = jnp.ones((rows, HD), BF16)
                for h in range(heads):
                    cols = slice(h * HD, (h + 1) * HD)
                    qe[h, at : at + rows, 0:128] = jnp.concatenate([hi[:, cols], lo[:, cols]], axis=1)
                    ke[h, 0:HD, at : at + rows] = kT[cols, :]
                    ke[h, HD : 2 * HD, at : at + rows] = kT[cols, :]
                    ve[h, at : at + rows, :] = jnp.concatenate([v[:, cols], ones], axis=1)
        x_keep.start()

    def step_y(w):
        own_copy(w).wait()
        for d in range(1, depth):
            z_copy(w, d).wait_recv()
        y_copy(w).start()

    def step_p(w):
        y_copy(w).wait_recv()
        p_copy(w).start()

    plan = {
        (0, 0): [(step_y, 0)], (0, 4): [(step_y, 1)], (1, 2): [(step_p, 0)], (1, 4): [(step_y, 2)],
        (2, 3): [(step_p, 1)], (3, 2): [(step_p, 2)],
    }

    parts = []
    for half in range(2):
        inverse = []
        at = pl.multiple_of((t * 2 + half) * rows, rows)
        for h in range(heads):
            for (when_t, point), actions in plan.items():
                if point == half * heads + h:
                    @pl.when(t == when_t)
                    def _(actions=actions):
                        for fn, w in actions:
                            fn(w)
            if half == 0 and h == 1:
                for d in range(1, sources):
                    @pl.when(t == d)
                    def _(d=d):
                        ctx_copy(d).start()
            scores = mm(qe[h, pl.ds(at, rows), :], ke[h])
            top = jnp.max(scores, axis=1, keepdims=True)
            e = jnp.exp2(scores - top).astype(BF16)
            e_ref[h, half * rows : (half + 1) * rows, :] = e
            o = mm(e, ve[h])
            inv = 1.0 / o[:, HD:]
            inverse.append(inv)
            parts.append((o[:, :HD] * inv).astype(BF16))
        linv_ref[0, half] = jnp.concatenate(inverse, axis=1)
    block = jnp.concatenate(parts, axis=1)
    ctx_ref[0] = block
    ctx_buf[t] = block

    @pl.when(t == sources - 1)
    def _():
        ctx_own.start()
        for d in range(1, sources):
            x_copy(d).wait_send()
            ctx_copy(d).wait_send()
            ctx_copy(d).wait_recv()

        @pl.when(sender)
        def _():
            for d in range(1, n):
                q_copy(d).wait_send()

        for d in range(1, n):
            v_copy(d).wait_send()
        for w in range(3):
            for d in range(1, depth):
                z_copy(w, d).wait_send()
            y_copy(w).wait_send()
            p_copy(w).wait()
        x_keep.wait()
        ctx_own.wait()


def attend(n, per, length, x, wq, vec, wo, wu, wd):
    sources, rows, _ = x.shape
    gw = wq.shape[1] // 3
    heads = gw // HD
    slot = sources * 2 * rows
    parts_q = n // GROUPS
    depth = n // 2
    whole = lambda *shape: pl.BlockSpec(shape, lambda s: (0,) * len(shape), pipeline_mode=pl.Buffered(1))
    out_whole = lambda *shape: pl.BlockSpec(shape, lambda s: (0,) * len(shape))
    anywhere = pl.BlockSpec(memory_space=pl.ANY)
    dma = lambda *shape: pltpu.SemaphoreType.DMA(shape)
    return pl.pallas_call(
        functools.partial(attend_kernel, n, per),
        grid=(sources,),
        in_specs=[
            pl.BlockSpec(memory_space=pltpu.SMEM), anywhere, anywhere, whole(*vec.shape),
            whole(*wo.shape), whole(*wu.shape), whole(*wd.shape),
        ],
        out_specs=[
            pl.BlockSpec((1, rows, 2 * gw), lambda s: (s, 0, 0)),
            pl.BlockSpec((1, 2, rows, gw), lambda s: (s, 0, 0, 0)),
            pl.BlockSpec((heads, 2 * rows, slot), lambda s: (0, s, 0)),
            out_whole(slot, gw),
            out_whole(gw, slot),
            out_whole(gw, slot),
            out_whole(gw, 3 * gw),
            out_whole(n, *vec.shape),
            anywhere, anywhere, anywhere, anywhere, anywhere,
        ],
        out_shape=[
            jax.ShapeDtypeStruct((sources, rows, 2 * gw), BF16),
            jax.ShapeDtypeStruct((sources, 2, rows, gw), F32),
            jax.ShapeDtypeStruct((heads, slot, slot), BF16),
            jax.ShapeDtypeStruct((slot, gw), BF16),
            jax.ShapeDtypeStruct((gw, slot), BF16),
            jax.ShapeDtypeStruct((gw, slot), BF16),
            jax.ShapeDtypeStruct((gw, 3 * gw), BF16),
            jax.ShapeDtypeStruct((n,) + vec.shape, F32),
            jax.ShapeDtypeStruct(x.shape, BF16),
            jax.ShapeDtypeStruct(x.shape, BF16),
            jax.ShapeDtypeStruct((depth, 2) + wo.shape, BF16),
            jax.ShapeDtypeStruct((depth, 2) + wu.shape, BF16),
            jax.ShapeDtypeStruct((depth, 2) + wd.shape, BF16),
        ],
        scratch_shapes=[
            pltpu.VMEM((heads, slot, 256), BF16),
            pltpu.VMEM((heads, 256, slot), BF16),
            pltpu.VMEM((heads, slot, 128), BF16),
            pltpu.VMEM(x.shape, BF16),
            pltpu.VMEM(x.shape, BF16),
            pltpu.VMEM((parts_q,) + wq.shape, BF16),
            pltpu.VMEM((n,) + vec.shape, F32),
            dma(3), dma(3), dma(3), dma(3), dma(n - 1), dma(parts_q), dma(n - 1), dma(n - 1),
            dma(3, depth - 1), dma(3, depth - 1), dma(3), dma(3), dma(3), dma(3), dma(3), dma(5),
        ],
        compiler_params=pltpu.CompilerParams(vmem_limit_bytes=60 << 20, collective_id=1, has_side_effects=True),
        name="attend",
    )(length, x, wq, vec, wo, wu, wd)


def revisit_kernel(
    n, per,
    e_ref, ctx_ref, linv_ref, qT_ref, vT_ref, k_ref, x_ref, w_ref, gres_ref, gctx_in, gwo_in, gwu_in, gwd_in, sm_in,
    gt_ref, gqkv_ref, gqv_ref, gwo_ref, gwu_ref, gwd_ref, sm_ref,
    vTe, kn, dkT, dvT, gT, gc_buf, gi_buf, gi_pos, sm_buf, sm_seq, gb_buf, gqv_buf, gq_buf, gq_got, gq_fin,
    mine0, mine1, mine2, core0, core1, core2, yb0, yb1, yb2, zb0, zb1, zb2, xm0, xm1, xm2, xb0, xb1, xb2, f0, f1, f2, fb0, fb1, fb2,
    g_send, g_recv, i_send, i_recv, sm_send, sm_recv, ss_send, ss_recv, b_send, b_recv, bs_send, bs_recv,
    q_send, q_recv, qs_send, qs_recv, c_send, c_recv, y_send, y_recv, z_send, z_recv, xs_send, xs_recv, p_send, p_recv, own, local,
):
    heads = kn.shape[0]
    sources, rows, _ = x_ref.shape
    gw = heads * HD
    slot = sources * 2 * rows
    parts_q = gq_buf.shape[0]
    u = pl.program_id(0)
    i = lax.axis_index("dp")
    me = lax.axis_index("seq")
    c = lax.rem(me, 2)
    y = lax.rem(i, 2)
    k = i // 2
    depth = n // 2
    across = lax.rem(me + 2, sources)
    every = slice(None)
    inputs = (gwo_in, gwu_in, gwd_in)
    outputs = (gwo_ref, gwu_ref, gwd_ref)
    mine, core, ybuf, zbuf = (mine0, mine1, mine2), (core0, core1, core2), (yb0, yb1, yb2), (zb0, zb1, zb2)
    xmine, xbuf, final, fbuf = (xm0, xm1, xm2), (xb0, xb1, xb2), (f0, f1, f2), (fb0, fb1, fb2)

    def g_copy(d):
        peer = lax.rem(me + d, sources)
        return remote(gctx_in.at[peer], gc_buf.at[sources - 1 - d], g_send.at[d - 1], g_recv.at[d - 1], i, peer)

    def i_copy(d):
        return remote(gi_buf.at[d - 1], gi_pos.at[me], i_send.at[d - 1], i_recv.at[d - 1], i, lax.rem(me + d, sources))

    def sm_copy(d):
        to = lax.rem(i + d, n)
        return remote(sm_in.at[to], sm_buf.at[d - 1], sm_send.at[d - 1], sm_recv.at[d - 1], to, me)

    def ss_copy(d):
        return remote(sm_seq.at[me], sm_seq.at[me], ss_send.at[d - 1], ss_recv.at[d - 1], i, lax.rem(me + d, sources))

    def b_copy(d):
        return remote(gb_buf.at[i], gb_buf.at[i], b_send.at[d - 1], b_recv.at[d - 1], lax.rem(i + d, n), me)

    def bs_copy(d):
        return remote(gqv_buf, gqv_buf, bs_send.at[d - 1], bs_recv, i, lax.rem(me + d, sources))

    def q_copy(piece):
        to = me * parts_q + piece
        d = lax.rem(to - i + n, n)
        at = jnp.maximum(d, 1) - 1
        return d, remote(gq_buf.at[piece], gq_got.at[at], q_send.at[piece], q_recv.at[at], to, me)

    def qs_copy(d):
        return remote(gq_fin, gq_fin, qs_send.at[d - 1], qs_recv, i, lax.rem(me + d, sources))

    def own_copy(w):
        return pltpu.make_async_copy(half_of(inputs[w], (every, every), c), mine[w], own.at[w])

    def c_copy(w):
        return remote(half_of(inputs[w], (every, every), 1 - c), core[w], c_send.at[w], c_recv.at[w], i, other(me))

    def y_copy(w):
        return remote(mine[w].at[:, 1 - y], ybuf[w], y_send.at[w], y_recv.at[w], other(i), me)

    def z_copy(w, d):
        to = lax.rem(k + d, depth)
        return remote(mine[w].at[to, y], zbuf[w].at[d - 1], z_send.at[w, d - 1], z_recv.at[w, d - 1], to * 2 + y, me)

    def x_copy(w):
        return remote(xmine[w], xbuf[w], xs_send.at[w], xs_recv.at[w], i, across)

    def p_copy(w):
        return remote(final[w], fbuf[w], p_send.at[w], p_recv.at[w], i, other(me))

    g_own = pltpu.make_async_copy(gctx_in.at[me], gc_buf.at[sources - 1], local.at[0])
    sm_own = pltpu.make_async_copy(sm_in.at[i], sm_buf.at[n - 1], local.at[1])
    owner = i // parts_q == me
    count = gw // per
    bias_owner = lax.rem(i // count, GROUPS) == me

    def add(a, b):
        return (a.astype(F32) + b.astype(F32)).astype(BF16)

    def step_y(w):
        own_copy(w).wait()
        c_copy(w).wait_recv()
        mine[w][:, 1 - y] = add(mine[w][:, 1 - y], core[w][:, 1 - y])
        mine[w][:, y] = add(mine[w][:, y], core[w][:, y])
        y_copy(w).start()

    def step_z(w):
        y_copy(w).wait_recv()
        mine[w][:, y] = add(mine[w][:, y], ybuf[w][...])
        for d in range(1, depth):
            z_copy(w, d).start()

    def step_x(w):
        total = mine[w][k, y].astype(F32)
        for d in range(1, depth):
            z_copy(w, d).wait_recv()
            total += zbuf[w][d - 1].astype(F32)
        xmine[w][...] = total.astype(BF16)
        x_copy(w).start()

    def step_p(w):
        x_copy(w).wait_recv()
        final[w][...] = xmine[w][...].astype(F32) + xbuf[w][...].astype(F32)
        p_copy(w).start()

    def small_sum():
        sm_own.wait()
        total = sm_buf[n - 1]
        for d in range(1, n):
            sm_copy(d).wait_recv()
            total += sm_buf[d - 1]
        sm_seq[me] = total
        for d in range(1, sources):
            ss_copy(d).start()

    @pl.when(u == 0)
    def _():
        greet(n, sources, i, me)
        for d in (1, 2, 3):
            g_copy(d).start()
        g_own.start()
        for w in range(3):
            c_copy(w).start()
            own_copy(w).start()
        sm_own.start()
        for d in range(1, n):
            sm_copy(d).start()
        dkT[...] = jnp.zeros_like(dkT)
        dvT[...] = jnp.zeros_like(dvT)
        row = lax.broadcasted_iota(jnp.int32, (HD, slot), 0)
        ones_rows = jnp.where(row < 2, 1.0, 0.0).astype(BF16)
        for h in range(heads):
            cols = slice(h * HD, (h + 1) * HD)
            vTe[h, 0:HD, :] = vT_ref[cols, :]
            vTe[h, HD:, :] = ones_rows
            kn[h] = k_ref[:, cols]
        g_own.wait()

    for d in range(1, sources):
        @pl.when(u == d)
        def _(d=d):
            g_copy(d).wait_recv()

    plan = {
        (0, 2): [(step_y, 0)], (0, 3): [(step_y, 1)], (0, 4): [(step_y, 2)],
        (1, 4): [(step_z, 0)], (2, 3): [(step_z, 1)], (2, 5): [(step_x, 0)],
        (3, 2): [(step_z, 2)], (3, 4): [(step_x, 1)], (3, 5): [(step_p, 0)],
    }

    lane = lax.broadcasted_iota(jnp.int32, (rows, HD), 1)
    j = sources - 1 - u
    for half in range(2):
        at = pl.multiple_of((j * 2 + half) * rows, rows)
        lanes = slice(half * gw, (half + 1) * gw)
        g = gc_buf[j, :, lanes].astype(F32) * linv_ref[0, half]
        g_low = g.astype(BF16)
        gT_low = g_low.T
        prod = g * ctx_ref[0, :, lanes].astype(F32)
        dqs = []
        for h in range(heads):
            for (when_u, point), actions in plan.items():
                if point == half * heads + h:
                    @pl.when(u == when_u)
                    def _(actions=actions):
                        for fn, w in actions:
                            fn(w)
            if half * heads + h == 1:
                @pl.when(u == 1)
                def _():
                    small_sum()
            cols = slice(h * HD, (h + 1) * HD)
            delta = -jnp.sum(prod[:, cols], axis=1, keepdims=True)
            d_hi = delta.astype(BF16)
            d_lo = (delta - d_hi.astype(F32)).astype(BF16)
            tail = jnp.where(lane == 0, d_hi, jnp.where(lane == 1, d_lo, jnp.zeros((), BF16)))
            ge = jnp.concatenate([g_low[:, cols], tail], axis=1)
            e = e_ref[h, half * rows : (half + 1) * rows, :]
            ds = (e.astype(F32) * mm(ge, vTe[h])).astype(BF16)
            dvT[cols, :] += mm(gT_low[cols, :], e)
            dkT[cols, :] += mm(qT_ref[cols, half * rows : (half + 1) * rows], ds)
            dqs.append((mm(ds, kn[h]) * (HD ** (-0.5))).astype(BF16))
        gT[0:gw, pl.ds(at, rows)] = jnp.concatenate(dqs, axis=1).T

    @pl.when(u == sources - 1)
    def _():
        gT[gw : 2 * gw, :] = (dkT[...] * (HD ** (-0.5))).astype(BF16)
        gT[2 * gw :, :] = dvT[...].astype(BF16)
        gb_buf[i] = mm_nt(jnp.ones((8, slot), BF16), gT[...])
        ready = 0
        for q in (1, 0, 2, 3):
            packed = [
                mm(w_ref[...], gT[:, (q * 2 + half) * rows : (q * 2 + half + 1) * rows]).T.astype(BF16)
                for half in range(2)
            ]
            block = jnp.concatenate(packed, axis=1)
            if ready:
                i_copy(ready).start()
            if q < sources - 1:
                gi_buf[q] = block
            else:
                gi_pos[me] = block
            ready = q + 1
        for d in range(1, n):
            b_copy(d).start()
        sums = [None, None]
        for q in range(sources):
            for half in range(2):
                part = mm(gT[:, (q * 2 + half) * rows : (q * 2 + half + 1) * rows], x_ref[q, :, window(half)])
                sums[half] = part if sums[half] is None else sums[half] + part
        gq = (sums[0][:, :gw] + sums[1][:, 64:]).T
        size = gw // parts_q
        for piece in range(parts_q):
            gq_buf[piece] = gq[piece * size : (piece + 1) * size].astype(BF16)
        step_x(2)
        for piece in range(parts_q):
            d, copy = q_copy(piece)

            @pl.when(d != 0)
            def _():
                copy.start()

        step_p(1)

        for d in range(1, n):
            b_copy(d).wait_recv()

        @pl.when(bias_owner)
        def _():
            total = gb_buf[0, 0:1, :]
            for d in range(1, n):
                total += gb_buf[d, 0:1, :]
            side = jnp.where(i < n // 2, total[:, :gw], total[:, 2 * gw :])
            piece = lax.rem(i, count)
            value = side[:, 0:per]
            for v in range(1, count):
                value = jnp.where(piece == v, side[:, v * per : (v + 1) * per], value)
            gqv_buf[0:1, 0:per] = value
            for d in range(1, sources):
                bs_copy(d).start()

        step_p(2)

        @pl.when(owner)
        def _():
            total = gq_buf[jnp.clip(i - me * parts_q, 0, parts_q - 1)].astype(F32)
            for d in range(1, n):
                remote(gq_buf.at[0], gq_got.at[d - 1], q_send.at[0], q_recv.at[d - 1], other(i), me).wait_recv()
                total += gq_got[d - 1].astype(F32)
            gq_fin[...] = total.astype(BF16)
            for d in range(1, sources):
                qs_copy(d).start()

        for d in range(1, sources):
            ss_copy(d).wait_recv()
        total = sm_seq[0]
        for v in range(1, sources):
            total += sm_seq[v]
        sm_ref[...] = total
        for w in range(3):
            p_copy(w).wait_recv()
            ref = outputs[w]
            for v in range(2):
                value = jnp.where(c == v, final[w][...], fbuf[w][...])
                if len(ref.shape) == 3:
                    ref[v] = value
                else:
                    half = ref.shape[1] // 2
                    ref[:, v * half : (v + 1) * half] = value

        for d in range(1, sources):
            i_copy(d).wait_recv()
        for half in range(2):
            r = slice(half * rows, (half + 1) * rows)
            lanes = slice(half * gw, (half + 1) * gw)
            for pair in range(GROUPS // 2):
                both = jnp.concatenate([gi_pos[2 * pair, :, lanes], gi_pos[2 * pair + 1, :, lanes]], axis=1)
                wide = slice(pair * 2 * gw, (pair + 1) * 2 * gw)
                gt_ref[r, wide] = (both.astype(F32) + gres_ref[r, wide]).astype(BF16)

        @pl.when(jnp.logical_not(bias_owner))
        def _():
            bs_copy(1).wait_recv()

        gqv_ref[...] = gqv_buf[0:1, 0:per]

        @pl.when(jnp.logical_not(owner))
        def _():
            qs_copy(1).wait_recv()

        gqkv_ref[...] = gq_fin[...].astype(F32)

        for d in range(1, sources):
            g_copy(d).wait_send()
            i_copy(d).wait_send()
            ss_copy(d).wait_send()

        @pl.when(bias_owner)
        def _():
            for d in range(1, sources):
                bs_copy(d).wait_send()

        @pl.when(owner)
        def _():
            for d in range(1, sources):
                qs_copy(d).wait_send()

        for piece in range(parts_q):
            d, copy = q_copy(piece)

            @pl.when(d != 0)
            def _():
                copy.wait_send()

        for d in range(1, n):
            sm_copy(d).wait_send()
            b_copy(d).wait_send()
        for w in range(3):
            c_copy(w).wait_send()
            y_copy(w).wait_send()
            for d in range(1, depth):
                z_copy(w, d).wait_send()
            x_copy(w).wait_send()
            p_copy(w).wait_send()


def revisit(n, per, e, ctx, linv, qT, vT, k, x, w, gres, gctx, gwo, gwu, gwd, small):
    sources, rows, _ = x.shape
    gw = w.shape[0]
    heads = gw // HD
    slot = sources * 2 * rows
    parts_q = n // GROUPS
    depth = n // 2
    last = sources - 1
    whole = lambda *shape: pl.BlockSpec(shape, lambda s: (0,) * len(shape), pipeline_mode=pl.Buffered(1))
    out_whole = lambda *shape: pl.BlockSpec(shape, lambda s: (0,) * len(shape))
    anywhere = pl.BlockSpec(memory_space=pl.ANY)
    dma = lambda *shape: pltpu.SemaphoreType.DMA(shape)

    def half_shape(a):
        return a.shape[3:] if len(a.shape) == 5 else (a.shape[2], a.shape[3] // 2)

    halves = [half_shape(a) for a in (gwo, gwu, gwd)]
    outs = [
        jax.ShapeDtypeStruct((2 * rows, GROUPS * gw), BF16),
        jax.ShapeDtypeStruct((gw // parts_q, 3 * gw), F32),
        jax.ShapeDtypeStruct((1, per), F32),
        jax.ShapeDtypeStruct(gwo.shape[2:], F32),
        jax.ShapeDtypeStruct(gwu.shape[2:], F32),
        jax.ShapeDtypeStruct(gwd.shape[2:], F32),
        jax.ShapeDtypeStruct(small.shape[1:], F32),
    ]
    vmem = pltpu.VMEM
    return pl.pallas_call(
        functools.partial(revisit_kernel, n, per),
        grid=(sources,),
        in_specs=[
            pl.BlockSpec((heads, 2 * rows, slot), lambda s: (0, last - s, 0)),
            pl.BlockSpec((1, rows, 2 * gw), lambda s: (last - s, 0, 0)),
            pl.BlockSpec((1, 2, rows, gw), lambda s: (last - s, 0, 0, 0)),
            pl.BlockSpec((gw, 2 * rows), lambda s: (0, last - s)),
            whole(*vT.shape), whole(*k.shape), whole(*x.shape), whole(*w.shape), whole(*gres.shape),
            anywhere, anywhere, anywhere, anywhere, anywhere,
        ],
        out_specs=[out_whole(*o.shape) for o in outs],
        out_shape=outs,
        scratch_shapes=[
            vmem((heads, 2 * HD, slot), BF16),
            vmem((heads, slot, HD), BF16),
            vmem((gw, slot), F32),
            vmem((gw, slot), F32),
            vmem((3 * gw, slot), BF16),
            vmem(x.shape, BF16), vmem((sources - 1,) + x.shape[1:], BF16), vmem(x.shape, BF16),
            vmem(small.shape, F32), vmem((sources,) + small.shape[1:], F32),
            vmem((n, 8, 3 * gw), F32), vmem((8, 256), F32),
            vmem((parts_q, gw // parts_q, 3 * gw), BF16),
            vmem((n - 1, gw // parts_q, 3 * gw), BF16),
            vmem((gw // parts_q, 3 * gw), BF16),
        ]
        + [vmem((depth, 2) + s, BF16) for s in halves]
        + [vmem((depth, 2) + s, BF16) for s in halves]
        + [vmem((depth,) + s, BF16) for s in halves]
        + [vmem((depth - 1,) + s, BF16) for s in halves]
        + [vmem(s, BF16) for s in halves]
        + [vmem(s, BF16) for s in halves]
        + [vmem(s, F32) for s in halves]
        + [vmem(s, F32) for s in halves]
        + [
            dma(3), dma(3), dma(3), dma(3), dma(n - 1), dma(n - 1), dma(3), dma(3), dma(n - 1), dma(n - 1),
            dma(3), pltpu.SemaphoreType.DMA, dma(parts_q), dma(n - 1), dma(3), pltpu.SemaphoreType.DMA,
            dma(3), dma(3), dma(3), dma(3), dma(3, depth - 1), dma(3, depth - 1), dma(3), dma(3), dma(3), dma(3), dma(3), dma(2),
        ],
        compiler_params=pltpu.CompilerParams(vmem_limit_bytes=62 << 20, collective_id=2, has_side_effects=True),
        name="revisit",
    )(e, ctx, linv, qT, vT, k, x, w, gres, gctx, gwo, gwu, gwd, small)


def split_rows(values):
    mean = jnp.mean(values, axis=-1, keepdims=True)
    centred = values - mean
    var = jnp.mean(centred * centred, axis=-1, keepdims=True)
    return centred, lax.rsqrt(var + epsilon)


def norm_back(grad, unit, inverse, gain):
    g = grad * gain
    m1 = jnp.mean(g, axis=-1, keepdims=True)
    m2 = jnp.mean(g * unit, axis=-1, keepdims=True)
    return inverse * (g - m1 - unit * m2)


def join_windows(parts):
    tiles = []
    for even, odd in zip(parts[0::2], parts[1::2]):
        tiles += [even[:, :128], even[:, 128:] + odd[:, :128], odd[:, 128:]]
    return jnp.concatenate(tiles, axis=1)


def group_window(g):
    at = (g // 2) * 384 + (g % 2) * 128
    return slice(at, at + 256)


def middle_kernel(
    n, pos_ref, ctx_ref, tok_ref, gout_ref, wo_ref, wu_ref, wd_ref, vec_ref,
    out_ref, gctx_ref, gres_ref, gwo_ref, gwu_ref, gwd_ref, small_ref, upad, dpad, awo, awu, awd, sums, usums,
):
    rows = ctx_ref.shape[1]
    gw = ctx_ref.shape[2] // 2
    width = tok_ref.shape[1]
    hidden = wu_ref.shape[1]
    share = width // n
    vec = join_lanes([vec_ref[d, :, 0:share] for d in range(n)])
    obias, gain1, shift1, dbias, gain2, shift2 = (vec[v : v + 1] for v in range(1, 7))
    count = n // GROUPS
    for g in range(GROUPS):
        upad[g] = pad_rows(wu_ref[g * gw : (g + 1) * gw, :], g % 2)
        dpad[g] = pad_lanes(wd_ref[g * hidden : (g + 1) * hidden, :], g % 2)
    packed = [[] for _ in range(GROUPS)]
    for half in range(2):
        first = half == 0

        def keep(ref, at, value):
            if first:
                ref[at] = value
            else:
                ref[at] += value

        r = slice(half * rows, (half + 1) * rows)
        x = tok_ref[r, :].astype(F32) + obias
        for g in range(GROUPS):
            x += mm(ctx_ref[g, :, window(half)], pad_rows(wo_ref[g * gw : (g + 1) * gw, :], half))
        c1, i1 = split_rows(x)
        n1 = c1 * i1
        mixed = n1 * gain1 + shift1
        low = mixed.astype(BF16)
        lowered = []
        slopes = []
        actives = []
        for g in range(GROUPS):
            ub = join_lanes([vec_ref[g * count + d, 7:8, 0 : hidden // count] for d in range(count)])
            u = mm(low[:, group_window(g)], upad[g]) + ub
            phi = 0.5 + 0.5 * lax.erf(u * (0.5 ** 0.5))
            slope = phi + u * (jnp.exp(u * u * -0.5) * 0.3989422804014327)
            act = (u * phi).astype(BF16)
            actives.append(act)
            slopes.append(slope)
            lowered.append(mm(act, dpad[g]))
        x = mixed + join_windows(lowered) + dbias
        c2, i2 = split_rows(x)
        n2 = c2 * i2
        row = lax.broadcasted_iota(jnp.int32, (rows, 1), 0) + (pos_ref[1] + half * rows)
        valid = jnp.where(row < pos_ref[0], 1.0, 0.0)
        out_ref[r, :] = (valid * (n2 * gain2 + shift2)).astype(BF16)
        gy = gout_ref[r, :].astype(F32) * valid
        d2 = norm_back(gy, n2, i2, gain2)
        keep(sums, slice(4, 5), jnp.sum(gy * n2, axis=0, keepdims=True))
        keep(sums, slice(5, 6), jnp.sum(gy, axis=0, keepdims=True))
        keep(sums, slice(3, 4), jnp.sum(d2, axis=0, keepdims=True))
        d2_low = d2.astype(BF16)
        backs = []
        for g in range(GROUPS):
            win = d2_low[:, group_window(g)]
            odd = 64 * (g % 2)
            part = mm_tn(actives[g], win)
            if first:
                awd[g] = part
            else:
                gwd_ref[g * hidden : (g + 1) * hidden, :] = (awd[g] + part)[:, odd : odd + gw].astype(BF16)
            gu = mm_nt(win, dpad[g]) * slopes[g]
            keep(usums, slice(g, g + 1), jnp.sum(gu, axis=0, keepdims=True))
            gu_low = gu.astype(BF16)
            part = mm_tn(low[:, group_window(g)], gu_low)[odd : odd + gw]
            if first:
                awu[g] = part
            else:
                gwu_ref[g * gw : (g + 1) * gw, :] = (awu[g] + part).astype(BF16)
            backs.append(mm_nt(gu_low, upad[g]))
        gm = join_windows(backs) + d2
        d1 = norm_back(gm, n1, i1, gain1)
        keep(sums, slice(1, 2), jnp.sum(gm * n1, axis=0, keepdims=True))
        keep(sums, slice(2, 3), jnp.sum(gm, axis=0, keepdims=True))
        keep(sums, slice(0, 1), jnp.sum(d1, axis=0, keepdims=True))
        gres_ref[r, :] = d1
        d1_low = d1.astype(BF16)
        for g in range(GROUPS):
            part = mm_tn(ctx_ref[g, :, window(half)], d1_low)[64 * half : 64 * half + gw]
            if first:
                awo[g] = part
            else:
                gwo_ref[g * gw : (g + 1) * gw, :] = (awo[g] + part).astype(BF16)
        back = mm_nt(d1_low, wo_ref[...]).astype(BF16)
        for g in range(GROUPS):
            packed[g].append(back[:, g * gw : (g + 1) * gw])
    for g in range(GROUPS):
        gctx_ref[g] = jnp.concatenate(packed[g], axis=1)
    sums[6:8, :] = jnp.zeros((2, width), F32)
    up_share = hidden // count
    for d in range(n):
        small_ref[d] = jnp.zeros(small_ref.shape[1:], F32)
        small_ref[d, 0:8, 0:share] = sums[0:8, d * share : (d + 1) * share]
        at = (d % count) * up_share
        for v in range(0, up_share, 128):
            size = min(128, up_share - v)
            small_ref[d, 8 + v // 128 : 9 + v // 128, 0:size] = usums[d // count : d // count + 1, at + v : at + v + size]


def middle(n, pos, ctx, tok, gout, wo, wu, wd, vec):
    hidden = wu.shape[1]
    width = tok.shape[1]
    gw = width // GROUPS
    vmem = pl.BlockSpec(memory_space=pltpu.VMEM)
    return pl.pallas_call(
        functools.partial(middle_kernel, n),
        in_specs=[pl.BlockSpec(memory_space=pltpu.SMEM)] + [vmem] * 7,
        out_specs=[vmem] * 7,
        out_shape=[
            jax.ShapeDtypeStruct(tok.shape, BF16),
            jax.ShapeDtypeStruct(ctx.shape, BF16),
            jax.ShapeDtypeStruct(tok.shape, F32),
            jax.ShapeDtypeStruct(wo.shape, BF16),
            jax.ShapeDtypeStruct(wu.shape, BF16),
            jax.ShapeDtypeStruct(wd.shape, BF16),
            jax.ShapeDtypeStruct((n, 16, 128), F32),
        ],
        scratch_shapes=[
            pltpu.VMEM((GROUPS, 256, hidden), BF16),
            pltpu.VMEM((GROUPS, hidden, 256), BF16),
            pltpu.VMEM((GROUPS, gw, width), F32),
            pltpu.VMEM((GROUPS, gw, hidden), F32),
            pltpu.VMEM((GROUPS, hidden, 256), F32),
            pltpu.VMEM((8, width), F32),
            pltpu.VMEM((8, hidden), F32),
        ],
        compiler_params=pltpu.CompilerParams(vmem_limit_bytes=62 << 20),
        name="middle",
    )(pos, ctx, tok, gout, wo, wu, wd, vec)


def on_device(
    tokens, lengths, qkv_weight, qv_bias, out_weight, out_bias, norm_gain, norm_shift,
    up_weight, up_bias, down_weight, down_bias, final_gain, final_shift, grad_output,
):
    n = lax.axis_size("dp")
    _, piece_rows, width = tokens.shape
    gw = width // GROUPS
    half = piece_rows // 2
    share, per, up_share = out_bias.shape[0], qv_bias.shape[0], up_bias.shape[0]
    me = lax.axis_index("seq")
    lanes = -(-max(up_share, per) // 128) * 128
    vec = jnp.stack([
        jnp.pad(a.astype(F32), (0, lanes - a.shape[0]))
        for a in (qv_bias, out_bias, norm_gain, norm_shift, down_bias, final_gain, final_shift, up_bias)
    ])
    x = tokens.reshape(2, half, GROUPS, gw).transpose(2, 1, 0, 3).reshape(GROUPS, half, 2 * gw)
    wd_halves = down_weight.reshape(2, down_weight.shape[0] // 2, gw)
    ctx, linv, e, k, qT, vT, w, vecs, x_all, ctx_pos, wo, wu, wd = attend(
        n, per, lengths, x, qkv_weight, vec, out_weight, up_weight, wd_halves
    )
    pos = jnp.stack([lengths[0], (me * piece_rows).astype(jnp.int32)])
    output, gctx, gres, gwo, gwu, gwd, small = middle(
        n, pos, ctx_pos, tokens[0], grad_output[0],
        wo.reshape(width, width), wu.reshape(width, -1), wd.reshape(-1, gw), vecs,
    )
    grad_tokens, gqkv, gqv, gwo, gwu, gwd, small = revisit(
        n, per, e, ctx, linv, qT, vT, k, x_all, w, gres, gctx,
        gwo.reshape(wo.shape), gwu.reshape(wu.shape), gwd.reshape(wd.shape), small,
    )
    return (
        output[None], grad_tokens[None], gqkv, gqv[0], gwo, small[0, :share],
        small[1, :share], small[2, :share], gwu, small[8:].reshape(-1)[:up_share], gwd.reshape(down_weight.shape),
        small[3, :share], small[4, :share], small[5, :share],
    )


def solution(mesh):
    rows = P("dp", "seq", None)
    mat = P("dp", None)
    vec = P("dp")
    in_specs = (rows, vec, mat, vec, mat, vec, vec, vec, mat, vec, mat, vec, vec, vec, rows)
    out_specs = (rows, rows, mat, vec, mat, vec, vec, vec, mat, vec, mat, vec, vec, vec)
    return jax.shard_map(on_device, mesh=mesh, in_specs=in_specs, out_specs=out_specs, check_vma=False)
```

```python
import functools

import jax
import jax.numpy as jnp
from jax import lax
from jax.experimental import pallas as pl
from jax.experimental.pallas import tpu as pltpu
from jax.sharding import PartitionSpec as P

H = 12
GROUPS = 4
HD = 64
epsilon = 1e-05
LOG2E = 1.4426950408889634
MASKED = -1e30
F32 = jnp.float32
BF16 = jnp.bfloat16


def mm(a, b):
    return jnp.dot(a, b, preferred_element_type=F32)


def mm_nt(a, b):
    return lax.dot_general(a, b, (((1,), (1,)), ((), ())), preferred_element_type=F32)


def mm_tn(a, b):
    return lax.dot_general(a, b, (((0,), (0,)), ((), ())), preferred_element_type=F32)


def pad_rows(w, half):
    zeros = jnp.zeros((64, w.shape[1]), w.dtype)
    return jnp.concatenate([w, zeros] if half == 0 else [zeros, w], axis=0)


def pad_lanes(w, half):
    zeros = jnp.zeros((w.shape[0], 64), w.dtype)
    return jnp.concatenate([w, zeros] if half == 0 else [zeros, w], axis=1)


def window(half):
    return slice(half * 128, half * 128 + 256)


MESH = pl.DeviceIdType.MESH


def remote(src, dst, send_sem, recv_sem, dp, seq):
    return pltpu.make_async_remote_copy(
        src_ref=src, dst_ref=dst, send_sem=send_sem, recv_sem=recv_sem,
        device_id={"dp": dp, "seq": seq}, device_id_type=MESH,
    )


def greet(n, group, i, s):
    barrier = pltpu.get_barrier_semaphore()
    for d in range(1, n):
        pl.semaphore_signal(barrier, inc=1, device_id={"dp": lax.rem(i + d, n), "seq": s}, device_id_type=MESH)
    for d in range(1, group):
        pl.semaphore_signal(barrier, inc=1, device_id={"dp": i, "seq": lax.rem(s + d, group)}, device_id_type=MESH)
    pl.semaphore_wait(barrier, n + group - 2)


def other(index):
    return index + 1 - 2 * lax.rem(index, 2)


def half_of(ref, lead, c):
    if len(ref.shape) == len(lead) + 3:
        return ref.at[lead + (c,)]
    lanes = ref.shape[-1] // 2
    at = pl.multiple_of(c * lanes, 128) if lanes % 128 == 0 else c * lanes
    return ref.at[lead + (slice(None), pl.ds(at, lanes))]


def stack_rows(pieces):
    if len(pieces) == 1:
        return pieces[0]
    if pieces[0].shape[0] % 16 == 0:
        return jnp.concatenate(pieces, axis=0)
    return jnp.concatenate([p.astype(F32) for p in pieces], axis=0).astype(pieces[0].dtype)


def join_lanes(pieces):
    return pieces[0] if len(pieces) == 1 else jnp.concatenate(pieces, axis=1)


def attend_kernel(
    n, len_ref, tok_ref, wq_in, wo_in, wu_in, wd_in, v0, v1, v2, v3, v4, v5, v6, v7,
    ctx_ref, linv_ref, e_ref, k_out, qT_out, vT_out, w_out, vec_out, x_out, ctx_pos, wo_out, wu_out, wd_out,
    qe, ke, ve, xp, x_buf, ctx_half, ctx_buf, q_part, wq_buf, vec_in, vec_buf,
    x_send, x_recv, c_send, c_recv, q_send, q_recv, r_send, r_recv, v_send, v_recv, z_send, z_recv, y_send, y_recv, p_send, p_recv, own, local,
):
    heads = qe.shape[0]
    sources, rows, _ = x_buf.shape
    gw = heads * HD
    slot = sources * 2 * rows
    per = v0.shape[-1]
    parts_q = wq_buf.shape[1]
    t = pl.program_id(0) // 2
    half_now = lax.rem(pl.program_id(0), 2)
    i = lax.axis_index("dp")
    me = lax.axis_index("seq")
    c = lax.rem(me, 2)
    y = lax.rem(i, 2)
    k = i // 2
    depth = n // 2
    weights = ((wo_in, wo_out), (wu_in, wu_out), (wd_in, wd_out))

    def x_copy(d):
        peer = lax.rem(me + d, sources)
        return remote(xp.at[peer], x_buf.at[sources - 1 - d], x_send.at[d - 1], x_recv.at[d - 1], i, peer)

    def ctx_copy(d):
        peer = lax.rem(me + d, sources)
        return remote(ctx_buf.at[d - 1], ctx_pos.at[me], c_send.at[d - 1], c_recv.at[d - 1], i, peer)

    def q_copy(d):
        return remote(wq_in.at[me], q_part.at[i], q_send.at[d - 1], q_recv.at[d - 1], lax.rem(i + d, n), me)

    def r_copy(d):
        peer = lax.rem(me + d, sources)
        return remote(
            q_part.at[pl.ds(peer * parts_q, parts_q)], wq_buf.at[me], r_send.at[d - 1], r_recv.at[d - 1], i, peer
        )

    def v_copy(d):
        return remote(vec_in, vec_buf.at[i], v_send.at[d - 1], v_recv.at[d - 1], lax.rem(i + d, n), me)

    def z_copy(w, d):
        src, dst = weights[w]
        to = lax.rem(k + d, depth)
        return remote(
            half_of(src, (), c), half_of(dst, (k, y), c), z_send.at[w, d - 1], z_recv.at[w, d - 1], to * 2 + y, me
        )

    def own_copy(w):
        src, dst = weights[w]
        return pltpu.make_async_copy(half_of(src, (), c), half_of(dst, (k, y), c), own.at[w])

    def y_copy(w):
        part = half_of(weights[w][1], (slice(None), y), c)
        return remote(part, part, y_send.at[w], y_recv.at[w], other(i), me)

    def p_copy(w):
        part = half_of(weights[w][1], (slice(None), slice(None)), c)
        return remote(part, part, p_send.at[w], p_recv.at[w], i, other(me))

    x_own = pltpu.make_async_copy(xp.at[me], x_buf.at[sources - 1], local.at[0])
    x_keep = pltpu.make_async_copy(x_buf, x_out, local.at[1])
    v_own = pltpu.make_async_copy(vec_in, vec_buf.at[i], local.at[2])
    ctx_own = pltpu.make_async_copy(ctx_buf.at[sources - 1], ctx_pos.at[me], local.at[3])
    q_own = pltpu.make_async_copy(wq_in.at[me], q_part.at[i], local.at[4])
    r_own = pltpu.make_async_copy(q_part.at[pl.ds(me * parts_q, parts_q)], wq_buf.at[me], local.at[5])

    def step_y(w):
        own_copy(w).wait()
        for d in range(1, depth):
            z_copy(w, d).wait_recv()
        y_copy(w).start()

    def step_p(w):
        y_copy(w).wait_recv()
        p_copy(w).start()

    @pl.when(pl.program_id(0) == 0)
    def _():
        for g in range(GROUPS):
            cols = slice(g * gw, (g + 1) * gw)
            xp[g] = jnp.concatenate([tok_ref[0:rows, cols], tok_ref[rows:, cols]], axis=1)
        vec_in[...] = jnp.zeros_like(vec_in)
        for v, ref in enumerate((v0, v1, v2, v3, v4, v5, v6, v7)):
            vec_in[v : v + 1, 0 : ref.shape[-1]] = ref[...].astype(F32).reshape(1, ref.shape[-1])
        greet(n, sources, i, me)
        for d in range(1, n):
            q_copy(d).start()
        q_own.start()
        x_copy(2).start()

        @pl.when(c == 0)
        def _():
            x_copy(1).start()

        @pl.when(c == 1)
        def _():
            x_copy(3).start()

        x_own.start()
        v_own.start()
        for d in range(1, n):
            v_copy(d).start()
        for w in range(3):
            for d in range(1, depth):
                z_copy(w, d).start()
            own_copy(w).start()

        scale = HD ** (-0.5) * LOG2E
        lane = lax.broadcasted_iota(jnp.int32, (slot, 128), 1)
        ones_lane = jnp.where(lane == 0, 1.0, 0.0).astype(BF16)
        key_row = lax.broadcasted_iota(jnp.int32, (128, 2 * rows), 0)
        for h in range(heads):
            qe[h, :, 128:256] = ones_lane
        for j in range(sources):
            first = lax.rem(me + 1 + j, sources) * (2 * rows)
            key_pos = lax.broadcasted_iota(jnp.int32, (128, 2 * rows), 1) + first
            bias = jnp.where((key_row == 0) & (key_pos >= len_ref[0]), MASKED, 0.0).astype(BF16)
            for h in range(heads):
                ke[h, 128:256, j * 2 * rows : (j + 1) * 2 * rows] = bias

        q_own.wait()
        for d in range(1, n):
            q_copy(d).wait_recv()
        for d in range(1, sources):
            r_copy(d).start()

        @pl.when(c == 0)
        def _():
            x_copy(3).start()

        @pl.when(c == 1)
        def _():
            x_copy(1).start()

        r_own.start()

        v_own.wait()
        for d in range(1, n):
            v_copy(d).wait_recv()
        vec_out[...] = vec_buf[...]
        count = gw // per
        q_bias = join_lanes([vec_buf[me * count + u, 0:1, 0:per] for u in range(count)])
        v_bias = join_lanes([vec_buf[(GROUPS + me) * count + u, 0:1, 0:per] for u in range(count)])
        b = jnp.concatenate([q_bias, jnp.zeros((1, gw), F32), v_bias], axis=1)
        r_own.wait()
        for d in range(1, sources):
            r_copy(d).wait_recv()
        weight = stack_rows([wq_buf[v, u] for u in range(parts_q) for v in range(sources)])
        w_out[...] = weight
        x_own.wait()
        for j in (3, 1, 2, 0):
            if j < sources - 1:
                x_copy(sources - 1 - j).wait_recv()
            for half in range(2):
                at = (j * 2 + half) * rows
                w = pad_rows(weight, half)
                qkv = (mm(x_buf[j, :, window(half)], w) + b).astype(BF16)
                q = qkv[:, :gw]
                kk = qkv[:, gw : 2 * gw]
                v = qkv[:, 2 * gw :]
                k_out[at : at + rows, :] = kk
                qT_out[:, at : at + rows] = q.T
                vT_out[:, at : at + rows] = v.T
                kT = kk.T
                scaled = q.astype(F32) * scale
                hi = scaled.astype(BF16)
                lo = (scaled - hi.astype(F32)).astype(BF16)
                ones = jnp.ones((rows, HD), BF16)
                for h in range(heads):
                    cols = slice(h * HD, (h + 1) * HD)
                    qe[h, at : at + rows, 0:128] = jnp.concatenate([hi[:, cols], lo[:, cols]], axis=1)
                    ke[h, 0:HD, at : at + rows] = kT[cols, :]
                    ke[h, HD : 2 * HD, at : at + rows] = kT[cols, :]
                    ve[h, at : at + rows, :] = jnp.concatenate([v[:, cols], ones], axis=1)
        x_keep.start()

    plan = {
        1: [(step_y, 0)], 3: [(step_y, 1)], 4: [(step_p, 0), (step_y, 2)], 6: [(step_p, 1)], 7: [(step_p, 2)],
    }
    for now, actions in plan.items():
        @pl.when(pl.program_id(0) == now)
        def _(actions=actions):
            for fn, w in actions:
                fn(w)

    parts = []
    inverse = []
    at = pl.multiple_of(pl.program_id(0) * rows, rows)
    for h in range(heads):
        scores = mm(qe[h, pl.ds(at, rows), :], ke[h])
        top = jnp.max(scores, axis=1, keepdims=True)
        e = jnp.exp2(scores - top).astype(BF16)
        e_ref[h] = e
        o = mm(e, ve[h])
        inv = 1.0 / o[:, HD:]
        inverse.append(inv)
        parts.append((o[:, :HD] * inv).astype(BF16))
    linv_ref[0, 0] = jnp.concatenate(inverse, axis=1)
    ctx_half[half_now] = jnp.concatenate(parts, axis=1)

    @pl.when(half_now == 1)
    def _():
        block = jnp.concatenate([ctx_half[0], ctx_half[1]], axis=1)
        ctx_ref[0] = block
        ctx_buf[t] = block
        for d in range(1, sources):
            @pl.when(t == d - 1)
            def _():
                ctx_copy(d).start()

    @pl.when(pl.program_id(0) == 2 * sources - 1)
    def _():
        ctx_own.start()
        for d in range(1, sources):
            x_copy(d).wait_send()
            r_copy(d).wait_send()
            ctx_copy(d).wait_send()
            ctx_copy(d).wait_recv()

        for d in range(1, n):
            q_copy(d).wait_send()
            v_copy(d).wait_send()
        for w in range(3):
            for d in range(1, depth):
                z_copy(w, d).wait_send()
            y_copy(w).wait_send()
            p_copy(w).wait()
        x_keep.wait()
        ctx_own.wait()


def attend(n, length, tok, wq, wo, wu, wd, vectors):
    sources, rows = GROUPS, tok.shape[0] // 2
    gw = 2 * wd.shape[1]
    heads = gw // HD
    slot = sources * 2 * rows
    depth = n // 2
    parts_q = n // GROUPS
    lanes = -(-max(v.shape[-1] for v in vectors) // 128) * 128
    block = (sources, rows, 2 * gw)
    whole = lambda *shape: pl.BlockSpec(shape, lambda s: (0,) * len(shape), pipeline_mode=pl.Buffered(1))
    out_whole = lambda *shape: pl.BlockSpec(shape, lambda s: (0,) * len(shape))
    anywhere = pl.BlockSpec(memory_space=pl.ANY)
    dma = lambda *shape: pltpu.SemaphoreType.DMA(shape)
    return pl.pallas_call(
        functools.partial(attend_kernel, n),
        grid=(2 * sources,),
        in_specs=[pl.BlockSpec(memory_space=pltpu.SMEM), whole(*tok.shape), anywhere]
        + [whole(*a.shape) for a in (wo, wu, wd) + vectors],
        out_specs=[
            pl.BlockSpec((1, rows, 2 * gw), lambda s: (s // 2, 0, 0)),
            pl.BlockSpec((1, 1, rows, gw), lambda s: (s // 2, lax.rem(s, 2), 0, 0)),
            pl.BlockSpec((heads, rows, slot), lambda s: (0, s, 0)),
            out_whole(slot, gw),
            out_whole(gw, slot),
            out_whole(gw, slot),
            out_whole(gw, 3 * gw),
            out_whole(n, 8, lanes),
            anywhere, anywhere, anywhere, anywhere, anywhere,
        ],
        out_shape=[
            jax.ShapeDtypeStruct(block, BF16),
            jax.ShapeDtypeStruct((sources, 2, rows, gw), F32),
            jax.ShapeDtypeStruct((heads, slot, slot), BF16),
            jax.ShapeDtypeStruct((slot, gw), BF16),
            jax.ShapeDtypeStruct((gw, slot), BF16),
            jax.ShapeDtypeStruct((gw, slot), BF16),
            jax.ShapeDtypeStruct((gw, 3 * gw), BF16),
            jax.ShapeDtypeStruct((n, 8, lanes), F32),
            jax.ShapeDtypeStruct(block, BF16),
            jax.ShapeDtypeStruct(block, BF16),
            jax.ShapeDtypeStruct((depth, 2) + wo.shape, BF16),
            jax.ShapeDtypeStruct((depth, 2) + wu.shape, BF16),
            jax.ShapeDtypeStruct((depth, 2) + wd.shape, BF16),
        ],
        scratch_shapes=[
            pltpu.VMEM((heads, slot, 256), BF16),
            pltpu.VMEM((heads, 256, slot), BF16),
            pltpu.VMEM((heads, slot, 128), BF16),
            pltpu.VMEM(block, BF16),
            pltpu.VMEM(block, BF16),
            pltpu.VMEM((2, rows, gw), BF16),
            pltpu.VMEM(block, BF16),
            pltpu.VMEM((n,) + wq.shape[1:], BF16),
            pltpu.VMEM((sources, parts_q) + wq.shape[1:], BF16),
            pltpu.VMEM((8, lanes), F32),
            pltpu.VMEM((n, 8, lanes), F32),
            dma(3), dma(3), dma(3), dma(3), dma(n - 1), dma(n - 1), dma(3), dma(3), dma(n - 1), dma(n - 1),
            dma(3, depth - 1), dma(3, depth - 1), dma(3), dma(3), dma(3), dma(3), dma(3), dma(6),
        ],
        compiler_params=pltpu.CompilerParams(vmem_limit_bytes=60 << 20, collective_id=1, has_side_effects=True),
        name="attend",
    )(length, tok, wq, wo, wu, wd, *vectors)


def revisit_kernel(
    n, per,
    e_ref, ctx_ref, linv_ref, qT_ref, vT_ref, k_ref, x_ref, w_ref, gctx_in, gwo_in, gwu_in, gwd_in, sm_in,
    gi_pos, gq_fin, gqv_out, gwo_out, gwu_out, gwd_out, sm_seq,
    vTe, kn, dkT, dvT, gT, gc_buf, gi_buf, sm_buf, sm_sum, gb_buf, gqv_buf, gq_buf, gq_got, gq_sum,
    mine0, mine1, mine2, core0, core1, core2, yb0, yb1, yb2, zb0, zb1, zb2, xm0, xm1, xm2, xb0, xb1, xb2, f0, f1, f2,
    g_send, g_recv, i_send, i_recv, sm_send, sm_recv, ss_send, ss_recv, b_send, b_recv, bs_send, bs_recv,
    q_send, q_recv, qs_send, qs_recv, c_send, c_recv, y_send, y_recv, z_send, z_recv, xs_send, xs_recv, p_send, p_recv, own, local,
):
    heads = kn.shape[0]
    sources, rows, _ = x_ref.shape
    gw = heads * HD
    slot = sources * 2 * rows
    parts_q = n // GROUPS
    u = pl.program_id(0)
    now = 2 * GROUPS - 1 - u
    half_now = lax.rem(now, 2)
    j = now // 2
    i = lax.axis_index("dp")
    me = lax.axis_index("seq")
    c = lax.rem(me, 2)
    y = lax.rem(i, 2)
    k = i // 2
    depth = n // 2
    across = lax.rem(me + 2, sources)
    every = slice(None)
    inputs = (gwo_in, gwu_in, gwd_in)
    outputs = (gwo_out, gwu_out, gwd_out)
    mine, core, ybuf, zbuf = (mine0, mine1, mine2), (core0, core1, core2), (yb0, yb1, yb2), (zb0, zb1, zb2)
    xmine, xbuf, final = (xm0, xm1, xm2), (xb0, xb1, xb2), (f0, f1, f2)

    def g_copy(d):
        peer = lax.rem(me + d, sources)
        return remote(gctx_in.at[peer], gc_buf.at[sources - 1 - d], g_send.at[d - 1], g_recv.at[d - 1], i, peer)

    def i_copy(d):
        return remote(gi_buf.at[d - 1], gi_pos.at[me], i_send.at[d - 1], i_recv.at[d - 1], i, lax.rem(me + d, sources))

    def sm_copy(d):
        to = lax.rem(i + d, n)
        return remote(sm_in.at[to], sm_buf.at[d - 1], sm_send.at[d - 1], sm_recv.at[d - 1], to, me)

    def ss_copy(d):
        return remote(sm_sum, sm_seq.at[me], ss_send.at[d - 1], ss_recv.at[d - 1], i, lax.rem(me + d, sources))

    def b_copy(d):
        return remote(gb_buf.at[i], gb_buf.at[i], b_send.at[d - 1], b_recv.at[d - 1], lax.rem(i + d, n), me)

    def bs_copy(d):
        return remote(gqv_buf, gqv_out, bs_send.at[d - 1], bs_recv, i, lax.rem(me + d, sources))

    def q_copy(d):
        to = lax.rem(i + d, n)
        return remote(gq_buf.at[to], gq_got.at[d - 1], q_send.at[d - 1], q_recv.at[d - 1], to, me)

    def qs_copy(d):
        spot = lax.rem(i, GROUPS)
        return remote(
            gq_sum, gq_fin.at[spot], qs_send.at[d], qs_recv.at[spot], me * parts_q + i // GROUPS, lax.rem(me + d, sources)
        )

    def own_copy(w):
        return pltpu.make_async_copy(half_of(inputs[w], (every, every), c), mine[w], own.at[w])

    def c_copy(w):
        return remote(half_of(inputs[w], (every, every), 1 - c), core[w], c_send.at[w], c_recv.at[w], i, other(me))

    def y_copy(w):
        return remote(mine[w].at[:, 1 - y], ybuf[w], y_send.at[w], y_recv.at[w], other(i), me)

    def z_copy(w, d):
        to = lax.rem(k + d, depth)
        return remote(mine[w].at[to, y], zbuf[w].at[d - 1], z_send.at[w, d - 1], z_recv.at[w, d - 1], to * 2 + y, me)

    def x_copy(w):
        return remote(xmine[w], xbuf[w], xs_send.at[w], xs_recv.at[w], i, across)

    def p_copy(w):
        return remote(final[w], outputs[w].at[c], p_send.at[w], p_recv.at[w], i, other(me))

    g_own = pltpu.make_async_copy(gctx_in.at[me], gc_buf.at[sources - 1], local.at[0])
    sm_own = pltpu.make_async_copy(sm_in.at[i], sm_buf.at[n - 1], local.at[1])
    ss_own = pltpu.make_async_copy(sm_sum, sm_seq.at[me], local.at[2])
    bs_own = pltpu.make_async_copy(gqv_buf, gqv_out, local.at[3])
    qs_own = pltpu.make_async_copy(gq_sum, gq_fin.at[lax.rem(i, GROUPS)], local.at[4])
    i_own = pltpu.make_async_copy(gi_buf.at[sources - 1], gi_pos.at[me], local.at[5])

    def p_own(w):
        return pltpu.make_async_copy(final[w], outputs[w].at[c], local.at[6 + w])

    stays = me * parts_q + i // GROUPS == i
    count = gw // per
    bias_owner = lax.rem(i // count, GROUPS) == me

    def step_y(w):
        own_copy(w).wait()
        c_copy(w).wait_recv()
        mine[w][...] += core[w][...]
        y_copy(w).start()

    def step_z(w):
        y_copy(w).wait_recv()
        mine[w][:, y] += ybuf[w][...]
        for d in range(1, depth):
            z_copy(w, d).start()

    def step_x(w):
        total = mine[w][k, y].astype(F32)
        for d in range(1, depth):
            z_copy(w, d).wait_recv()
            total += zbuf[w][d - 1].astype(F32)
        xmine[w][...] = total.astype(BF16)
        x_copy(w).start()

    def step_p(w):
        x_copy(w).wait_recv()
        final[w][...] = xmine[w][...].astype(F32) + xbuf[w][...].astype(F32)
        p_copy(w).start()
        p_own(w).start()

    def small_sum():
        sm_own.wait()
        total = sm_buf[n - 1]
        for d in range(1, n):
            sm_copy(d).wait_recv()
            total += sm_buf[d - 1]
        sm_sum[...] = total
        ss_own.start()
        for d in range(1, sources):
            ss_copy(d).start()

    @pl.when(u == 0)
    def _():
        greet(n, sources, i, me)
        for d in (1, 2, 3):
            g_copy(d).start()
        g_own.start()
        for w in range(3):
            c_copy(w).start()
            own_copy(w).start()
        sm_own.start()
        for d in range(1, n):
            sm_copy(d).start()
        dkT[...] = jnp.zeros_like(dkT)
        dvT[...] = jnp.zeros_like(dvT)
        row = lax.broadcasted_iota(jnp.int32, (HD, slot), 0)
        ones_rows = jnp.where(row < 2, 1.0, 0.0).astype(BF16)
        for h in range(heads):
            cols = slice(h * HD, (h + 1) * HD)
            vTe[h, 0:HD, :] = vT_ref[cols, :]
            vTe[h, HD:, :] = ones_rows
            kn[h] = k_ref[:, cols]
        g_own.wait()

    for d in range(1, sources):
        @pl.when(u == 2 * d)
        def _(d=d):
            g_copy(d).wait_recv()

    plan = {
        1: [(step_y, 0), (step_y, 1)], 2: [(step_y, 2)], 3: [(step_z, 0)], 5: [(step_z, 1)], 6: [(step_x, 0)],
        7: [(step_z, 2), (step_x, 1), (step_p, 0)],
    }
    for when_u, actions in plan.items():
        @pl.when(u == when_u)
        def _(actions=actions):
            for fn, w in actions:
                fn(w)

    @pl.when(u == 4)
    def _():
        small_sum()

    lane = lax.broadcasted_iota(jnp.int32, (rows, HD), 1)
    at = pl.multiple_of(now * rows, rows)
    both = gc_buf[j].astype(F32)
    g = jnp.where(half_now == 0, both[:, :gw], both[:, gw:]) * linv_ref[0, 0]
    g_low = g.astype(BF16)
    gT_low = g_low.T
    both = ctx_ref[0].astype(F32)
    prod = g * jnp.where(half_now == 0, both[:, :gw], both[:, gw:])
    dqs = []
    for h in range(heads):
        cols = slice(h * HD, (h + 1) * HD)
        delta = -jnp.sum(prod[:, cols], axis=1, keepdims=True)
        d_hi = delta.astype(BF16)
        d_lo = (delta - d_hi.astype(F32)).astype(BF16)
        tail = jnp.where(lane == 0, d_hi, jnp.where(lane == 1, d_lo, jnp.zeros((), BF16)))
        ge = jnp.concatenate([g_low[:, cols], tail], axis=1)
        e = e_ref[h]
        ds = (e.astype(F32) * mm(ge, vTe[h])).astype(BF16)
        dvT[cols, :] += mm(gT_low[cols, :], e)
        dkT[cols, :] += mm(qT_ref[cols, :], ds)
        dqs.append((mm(ds, kn[h]) * (HD ** (-0.5))).astype(BF16))
    gT[0:gw, pl.ds(at, rows)] = jnp.concatenate(dqs, axis=1).T

    @pl.when(u == 2 * sources - 1)
    def _():
        gT[gw : 2 * gw, :] = (dkT[...] * (HD ** (-0.5))).astype(BF16)
        gT[2 * gw :, :] = dvT[...].astype(BF16)
        sums = [None, None]
        for q in range(sources):
            for half in range(2):
                part = mm(gT[:, (q * 2 + half) * rows : (q * 2 + half + 1) * rows], x_ref[q, :, window(half)])
                sums[half] = part if sums[half] is None else sums[half] + part
        gq = (sums[0][:, :gw] + sums[1][:, 64:]).T
        size = gw // n
        for piece in range(n):
            gq_buf[piece] = gq[piece * size : (piece + 1) * size].astype(BF16)
        gb_buf[i] = mm_nt(jnp.ones((8, slot), BF16), gT[...])
        ready = 0
        for q in (1, 0, 2, 3):
            packed = [
                mm(w_ref[...], gT[:, (q * 2 + half) * rows : (q * 2 + half + 1) * rows]).T.astype(BF16)
                for half in range(2)
            ]
            block = jnp.concatenate(packed, axis=1)
            if ready:
                i_copy(ready).start()
            else:
                for d in range(1, n):
                    q_copy(d).start()
                for d in range(1, n):
                    b_copy(d).start()
            gi_buf[q] = block
            ready = q + 1
        i_own.start()
        step_x(2)
        step_p(1)
        total = gq_buf[i].astype(F32)
        for d in range(1, n):
            q_copy(d).wait_recv()
            total += gq_got[d - 1].astype(F32)
        gq_sum[...] = total.astype(BF16)
        for d in range(1, n):
            b_copy(d).wait_recv()

        @pl.when(bias_owner)
        def _():
            total = gb_buf[0, 0:1, :]
            for d in range(1, n):
                total += gb_buf[d, 0:1, :]
            side = jnp.where(i < n // 2, total[:, :gw], total[:, 2 * gw :])
            piece = lax.rem(i, count)
            value = side[:, 0:per]
            for v in range(1, count):
                value = jnp.where(piece == v, side[:, v * per : (v + 1) * per], value)
            gqv_buf[0:1, 0:per] = value
            bs_own.start()
            for d in range(1, sources):
                bs_copy(d).start()

        for d in range(1, sources):
            qs_copy(d).start()

        @pl.when(stays)
        def _():
            qs_own.start()

        @pl.when(jnp.logical_not(stays))
        def _():
            qs_copy(0).start()

        step_p(2)

        ss_own.wait()
        i_own.wait()
        for d in range(1, sources):
            ss_copy(d).wait_recv()
            i_copy(d).wait_recv()
        for w in range(3):
            p_copy(w).wait_recv()
            p_own(w).wait()

        @pl.when(jnp.logical_not(bias_owner))
        def _():
            bs_copy(1).wait_recv()

        for spot in range(GROUPS):
            source = lax.rem(i, parts_q) * GROUPS + spot

            @pl.when(jnp.logical_not(jnp.logical_and(i // parts_q == me, source == i)))
            def _():
                remote(gq_sum, gq_fin.at[spot], qs_send.at[0], qs_recv.at[spot], other(i), me).wait_recv()

        for d in range(1, sources):
            g_copy(d).wait_send()
            i_copy(d).wait_send()
            ss_copy(d).wait_send()

        @pl.when(bias_owner)
        def _():
            bs_own.wait()
            for d in range(1, sources):
                bs_copy(d).wait_send()

        for d in range(1, sources):
            qs_copy(d).wait_send()

        @pl.when(stays)
        def _():
            qs_own.wait()

        @pl.when(jnp.logical_not(stays))
        def _():
            qs_copy(0).wait_send()

        for d in range(1, n):
            q_copy(d).wait_send()
        for d in range(1, n):
            sm_copy(d).wait_send()
            b_copy(d).wait_send()
        for w in range(3):
            c_copy(w).wait_send()
            y_copy(w).wait_send()
            for d in range(1, depth):
                z_copy(w, d).wait_send()
            x_copy(w).wait_send()
            p_copy(w).wait_send()


def revisit(n, per, e, ctx, linv, qT, vT, k, x, w, gctx, gwo, gwu, gwd, small):
    sources, rows, _ = x.shape
    gw = w.shape[0]
    heads = gw // HD
    slot = sources * 2 * rows
    depth = n // 2
    last = 2 * sources - 1
    whole = lambda *shape: pl.BlockSpec(shape, lambda s: (0,) * len(shape), pipeline_mode=pl.Buffered(1))
    anywhere = pl.BlockSpec(memory_space=pl.ANY)
    dma = lambda *shape: pltpu.SemaphoreType.DMA(shape)

    def half_shape(a):
        return a.shape[3:] if len(a.shape) == 5 else (a.shape[2], a.shape[3] // 2)

    halves = [half_shape(a) for a in (gwo, gwu, gwd)]
    outs = [
        jax.ShapeDtypeStruct(x.shape, BF16),
        jax.ShapeDtypeStruct((GROUPS, gw // n, 3 * gw), BF16),
        jax.ShapeDtypeStruct((8, 256), F32),
        jax.ShapeDtypeStruct((2,) + halves[0], F32),
        jax.ShapeDtypeStruct((2,) + halves[1], F32),
        jax.ShapeDtypeStruct((2,) + halves[2], F32),
        jax.ShapeDtypeStruct((sources,) + small.shape[1:], F32),
    ]
    vmem = pltpu.VMEM
    return pl.pallas_call(
        functools.partial(revisit_kernel, n, per),
        grid=(2 * sources,),
        in_specs=[
            pl.BlockSpec((heads, rows, slot), lambda s: (0, last - s, 0)),
            pl.BlockSpec((1, rows, 2 * gw), lambda s: ((last - s) // 2, 0, 0)),
            pl.BlockSpec((1, 1, rows, gw), lambda s: ((last - s) // 2, lax.rem(last - s, 2), 0, 0)),
            pl.BlockSpec((gw, rows), lambda s: (0, last - s)),
            whole(*vT.shape), whole(*k.shape), whole(*x.shape), whole(*w.shape),
            anywhere, anywhere, anywhere, anywhere, anywhere,
        ],
        out_specs=[anywhere] * len(outs),
        out_shape=outs,
        scratch_shapes=[
            vmem((heads, 2 * HD, slot), BF16),
            vmem((heads, slot, HD), BF16),
            vmem((gw, slot), F32),
            vmem((gw, slot), F32),
            vmem((3 * gw, slot), BF16),
            vmem(x.shape, BF16), vmem(x.shape, BF16),
            vmem(small.shape, F32), vmem(small.shape[1:], F32),
            vmem((n, 8, 3 * gw), F32), vmem((8, 256), F32),
            vmem((n, gw // n, 3 * gw), BF16),
            vmem((n - 1, gw // n, 3 * gw), BF16),
            vmem((gw // n, 3 * gw), BF16),
        ]
        + [vmem((depth, 2) + s, BF16) for s in halves]
        + [vmem((depth, 2) + s, BF16) for s in halves]
        + [vmem((depth,) + s, BF16) for s in halves]
        + [vmem((depth - 1,) + s, BF16) for s in halves]
        + [vmem(s, BF16) for s in halves]
        + [vmem(s, BF16) for s in halves]
        + [vmem(s, F32) for s in halves]
        + [
            dma(3), dma(3), dma(3), dma(3), dma(n - 1), dma(n - 1), dma(3), dma(3), dma(n - 1), dma(n - 1),
            dma(3), pltpu.SemaphoreType.DMA, dma(n - 1), dma(n - 1), dma(4), dma(4),
            dma(3), dma(3), dma(3), dma(3), dma(3, depth - 1), dma(3, depth - 1), dma(3), dma(3), dma(3), dma(3), dma(3), dma(9),
        ],
        compiler_params=pltpu.CompilerParams(vmem_limit_bytes=62 << 20, collective_id=2, has_side_effects=True),
        name="revisit",
    )(e, ctx, linv, qT, vT, k, x, w, gctx, gwo, gwu, gwd, small)


def split_rows(values):
    mean = jnp.mean(values, axis=-1, keepdims=True)
    centred = values - mean
    var = jnp.mean(centred * centred, axis=-1, keepdims=True)
    return centred, lax.rsqrt(var + epsilon)


def norm_back(grad, unit, inverse, gain):
    g = grad * gain
    m1 = jnp.mean(g, axis=-1, keepdims=True)
    m2 = jnp.mean(g * unit, axis=-1, keepdims=True)
    return inverse * (g - m1 - unit * m2)


def join_windows(parts):
    tiles = []
    for even, odd in zip(parts[0::2], parts[1::2]):
        tiles += [even[:, :128], even[:, 128:] + odd[:, :128], odd[:, 128:]]
    return jnp.concatenate(tiles, axis=1)


def group_window(g):
    at = (g // 2) * 384 + (g % 2) * 128
    return slice(at, at + 256)


def middle_kernel(
    n, len_ref, ctx_ref, tok_ref, gout_ref, wo_ref, wu_ref, wd_ref, vec_ref,
    out_ref, gctx_ref, gres_ref, gwo_ref, gwu_ref, gwd_ref, small_ref, upad, dpad, awo, awu, awd, sums, usums,
):
    rows = ctx_ref.shape[1]
    gw = ctx_ref.shape[2] // 2
    width = tok_ref.shape[1]
    hidden = wu_ref.shape[1]
    share = width // n
    first_row = lax.axis_index("seq") * (2 * rows)
    vec = join_lanes([vec_ref[d, :, 0:share] for d in range(n)])
    obias, gain1, shift1, dbias, gain2, shift2 = (vec[v : v + 1] for v in range(1, 7))
    count = n // GROUPS
    for g in range(GROUPS):
        upad[g] = pad_rows(wu_ref[g * gw : (g + 1) * gw, :], g % 2)
        odd = 64 * (g % 2)
        dpad[g, 192 * (1 - g % 2) : 192 * (1 - g % 2) + 64, :] = jnp.zeros((64, hidden), BF16)
        size = hidden // count
        for d in range(count):
            for v in range(2):
                at = odd + v * (gw // 2)
                dpad[g, at : at + gw // 2, d * size : (d + 1) * size] = wd_ref[g * count + d, v]
    packed = [[] for _ in range(GROUPS)]
    for half in range(2):
        first = half == 0

        def keep(ref, at, value):
            if first:
                ref[at] = value
            else:
                ref[at] += value

        r = slice(half * rows, (half + 1) * rows)
        x = tok_ref[r, :].astype(F32) + obias
        for g in range(GROUPS):
            x += mm(ctx_ref[g, :, window(half)], pad_rows(wo_ref[g * gw : (g + 1) * gw, :], half))
        c1, i1 = split_rows(x)
        n1 = c1 * i1
        mixed = n1 * gain1 + shift1
        low = mixed.astype(BF16)
        lowered = []
        slopes = []
        actives = []
        for g in range(GROUPS):
            ub = join_lanes([vec_ref[g * count + d, 7:8, 0 : hidden // count] for d in range(count)])
            u = mm(low[:, group_window(g)], upad[g]) + ub
            phi = 0.5 + 0.5 * lax.erf(u * (0.5 ** 0.5))
            slope = phi + u * (jnp.exp(u * u * -0.5) * 0.3989422804014327)
            act = (u * phi).astype(BF16)
            actives.append(act)
            slopes.append(slope)
            lowered.append(mm_nt(act, dpad[g]))
        x = mixed + join_windows(lowered) + dbias
        c2, i2 = split_rows(x)
        n2 = c2 * i2
        row = lax.broadcasted_iota(jnp.int32, (rows, 1), 0) + (first_row + half * rows)
        valid = jnp.where(row < len_ref[0], 1.0, 0.0)
        out_ref[r, :] = (valid * (n2 * gain2 + shift2)).astype(BF16)
        gy = gout_ref[r, :].astype(F32) * valid
        d2 = norm_back(gy, n2, i2, gain2)
        keep(sums, slice(4, 5), jnp.sum(gy * n2, axis=0, keepdims=True))
        keep(sums, slice(5, 6), jnp.sum(gy, axis=0, keepdims=True))
        keep(sums, slice(3, 4), jnp.sum(d2, axis=0, keepdims=True))
        d2_low = d2.astype(BF16)
        backs = []
        for g in range(GROUPS):
            win = d2_low[:, group_window(g)]
            odd = 64 * (g % 2)
            part = mm_tn(win, actives[g])[odd : odd + gw]
            if first:
                awd[g] = part
            else:
                part = (awd[g] + part).astype(BF16)
                size = hidden // count
                for d in range(count):
                    for v in range(2):
                        gwd_ref[g * count + d, v] = part[v * (gw // 2) : (v + 1) * (gw // 2), d * size : (d + 1) * size]
            gu = mm(win, dpad[g]) * slopes[g]
            keep(usums, slice(g, g + 1), jnp.sum(gu, axis=0, keepdims=True))
            gu_low = gu.astype(BF16)
            part = mm_tn(low[:, group_window(g)], gu_low)[odd : odd + gw]
            if first:
                awu[g] = part
            else:
                gwu_ref[g * gw : (g + 1) * gw, :] = (awu[g] + part).astype(BF16)
            backs.append(mm_nt(gu_low, upad[g]))
        gm = join_windows(backs) + d2
        d1 = norm_back(gm, n1, i1, gain1)
        keep(sums, slice(1, 2), jnp.sum(gm * n1, axis=0, keepdims=True))
        keep(sums, slice(2, 3), jnp.sum(gm, axis=0, keepdims=True))
        keep(sums, slice(0, 1), jnp.sum(d1, axis=0, keepdims=True))
        gres_ref[r, :] = d1
        d1_low = d1.astype(BF16)
        for g in range(GROUPS):
            part = mm_tn(ctx_ref[g, :, window(half)], d1_low)[64 * half : 64 * half + gw]
            if first:
                awo[g] = part
            else:
                gwo_ref[g * gw : (g + 1) * gw, :] = (awo[g] + part).astype(BF16)
        back = mm_nt(d1_low, wo_ref[...]).astype(BF16)
        for g in range(GROUPS):
            packed[g].append(back[:, g * gw : (g + 1) * gw])
    for g in range(GROUPS):
        gctx_ref[g] = jnp.concatenate(packed[g], axis=1)
    sums[6:8, :] = jnp.zeros((2, width), F32)
    up_share = hidden // count
    for d in range(n):
        small_ref[d] = jnp.zeros(small_ref.shape[1:], F32)
        small_ref[d, 0:8, 0:share] = sums[0:8, d * share : (d + 1) * share]
        at = (d % count) * up_share
        for v in range(0, up_share, 128):
            size = min(128, up_share - v)
            small_ref[d, 8 + v // 128 : 9 + v // 128, 0:size] = usums[d // count : d // count + 1, at + v : at + v + size]


def middle(n, length, ctx, tok, gout, wo, wu, wd, vec):
    hidden = wu.shape[1]
    width = tok.shape[1]
    gw = width // GROUPS
    vmem = pl.BlockSpec(memory_space=pltpu.VMEM)
    return pl.pallas_call(
        functools.partial(middle_kernel, n),
        in_specs=[pl.BlockSpec(memory_space=pltpu.SMEM)] + [vmem] * 7,
        out_specs=[vmem] * 7,
        out_shape=[
            jax.ShapeDtypeStruct(tok.shape, BF16),
            jax.ShapeDtypeStruct(ctx.shape, BF16),
            jax.ShapeDtypeStruct(tok.shape, F32),
            jax.ShapeDtypeStruct(wo.shape, BF16),
            jax.ShapeDtypeStruct(wu.shape, BF16),
            jax.ShapeDtypeStruct(wd.shape, BF16),
            jax.ShapeDtypeStruct((n, 16, 128), F32),
        ],
        scratch_shapes=[
            pltpu.VMEM((GROUPS, 256, hidden), BF16),
            pltpu.VMEM((GROUPS, 256, hidden), BF16),
            pltpu.VMEM((GROUPS, gw, width), F32),
            pltpu.VMEM((GROUPS, gw, hidden), F32),
            pltpu.VMEM((GROUPS, gw, hidden), F32),
            pltpu.VMEM((8, width), F32),
            pltpu.VMEM((8, hidden), F32),
        ],
        compiler_params=pltpu.CompilerParams(vmem_limit_bytes=62 << 20),
        name="middle",
    )(length, ctx, tok, gout, wo, wu, wd, vec)


def finish_kernel(
    gi_ref, gres_ref, gq_ref, gqv_ref, gwo_ref, gwu_ref, gwd_ref, sm_ref,
    tok_out, qkv_out, qv_out, wo_out, b0_out, b1_out, b2_out, wu_out, up_out, wd_out, b3_out, b4_out, b5_out,
):
    rows = gi_ref.shape[1]
    gw = gi_ref.shape[2] // 2
    for half in range(2):
        r = slice(half * rows, (half + 1) * rows)
        lanes = slice(half * gw, (half + 1) * gw)
        for pair in range(GROUPS // 2):
            both = jnp.concatenate([gi_ref[2 * pair, :, lanes], gi_ref[2 * pair + 1, :, lanes]], axis=1)
            wide = slice(pair * 2 * gw, (pair + 1) * 2 * gw)
            tok_out[r, wide] = (both.astype(F32) + gres_ref[r, wide]).astype(BF16)
    qkv_out[...] = jnp.concatenate([gq_ref[v].astype(F32) for v in range(gq_ref.shape[0])], axis=0)
    qv_out[...] = gqv_ref[0:1, 0 : qv_out.shape[1]]
    for ref, out in ((gwo_ref, wo_out), (gwu_ref, wu_out)):
        out[...] = jnp.concatenate([ref[0], ref[1]], axis=1)
    size = gwd_ref.shape[1]
    for v in range(2):
        wd_out[v * size : (v + 1) * size, :] = gwd_ref[v]
    total = sm_ref[0] + sm_ref[1] + sm_ref[2] + sm_ref[3]
    for v, out in enumerate((b0_out, b1_out, b2_out, b3_out, b4_out, b5_out)):
        out[...] = total[v : v + 1, 0 : out.shape[1]]
    for v in range(0, up_out.shape[1], 128):
        step = min(128, up_out.shape[1] - v)
        up_out[:, v : v + step] = total[8 + v // 128 : 9 + v // 128, 0:step]


def finish(shapes, *args):
    vmem = pl.BlockSpec(memory_space=pltpu.VMEM)
    return pl.pallas_call(
        finish_kernel,
        in_specs=[vmem] * len(args),
        out_specs=[vmem] * len(shapes),
        out_shape=[jax.ShapeDtypeStruct(s, BF16 if v == 0 else F32) for v, s in enumerate(shapes)],
        compiler_params=pltpu.CompilerParams(vmem_limit_bytes=60 << 20),
        name="finish",
    )(*args)


def on_device(
    tokens, lengths, qkv_weight, qv_bias, out_weight, out_bias, norm_gain, norm_shift,
    up_weight, up_bias, down_weight, down_bias, final_gain, final_shift, grad_output,
):
    n = lax.axis_size("dp")
    width = tokens.shape[2]
    per = qv_bias.shape[0]
    vectors = tuple(
        a[None] if a.shape[0] <= 128 else a for a in (qv_bias, out_bias, norm_gain, norm_shift, down_bias, final_gain, final_shift, up_bias)
    )
    wq = qkv_weight.reshape(GROUPS, qkv_weight.shape[0] // GROUPS, qkv_weight.shape[1])
    wd_halves = down_weight.T.reshape(2, down_weight.shape[1] // 2, down_weight.shape[0])
    ctx, linv, e, k, qT, vT, w, vecs, x_all, ctx_pos, wo, wu, wd = attend(
        n, lengths, tokens[0], wq, out_weight, up_weight, wd_halves, vectors
    )
    output, gctx, gres, gwo, gwu, gwd, small = middle(
        n, lengths, ctx_pos, tokens[0], grad_output[0],
        wo.reshape(width, width), wu.reshape(width, -1), wd.reshape((n,) + wd.shape[2:]), vecs,
    )
    parts = revisit(
        n, per, e, ctx, linv, qT, vT, k, x_all, w, gctx,
        gwo.reshape(wo.shape), gwu.reshape(wu.shape), gwd.reshape(wd.shape), small,
    )
    one = lambda a: (1, a.shape[0])
    shapes = (
        tokens.shape[1:], qkv_weight.shape, one(qv_bias), out_weight.shape, one(out_bias), one(norm_gain),
        one(norm_shift), up_weight.shape, one(up_bias), down_weight.shape[::-1], one(down_bias), one(final_gain), one(final_shift),
    )
    outs = list(finish(shapes, parts[0], gres, *parts[1:]))
    outs[9] = outs[9].T
    flat = [a[0] if a.shape[0] == 1 else a for a in outs[1:]]
    return (output[None], outs[0][None], *flat)


def solution(mesh):
    rows = P("dp", "seq", None)
    mat = P("dp", None)
    vec = P("dp")
    in_specs = (rows, vec, mat, vec, mat, vec, vec, vec, mat, vec, mat, vec, vec, vec, rows)
    out_specs = (rows, rows, mat, vec, mat, vec, vec, vec, mat, vec, mat, vec, vec, vec)
    return jax.shard_map(on_device, mesh=mesh, in_specs=in_specs, out_specs=out_specs, check_vma=False)
```

```python
import functools

import jax
import jax.numpy as jnp
from jax import lax
from jax.experimental import pallas as pl
from jax.experimental.pallas import tpu as pltpu
from jax.sharding import PartitionSpec as P

H = 12
GROUPS = 4
HD = 64
epsilon = 1e-05
LOG2E = 1.4426950408889634
MASKED = -1e30
F32 = jnp.float32
BF16 = jnp.bfloat16


def mm(a, b):
    return jnp.dot(a, b, preferred_element_type=F32)


def mm_nt(a, b):
    return lax.dot_general(a, b, (((1,), (1,)), ((), ())), preferred_element_type=F32)


def mm_tn(a, b):
    return lax.dot_general(a, b, (((0,), (0,)), ((), ())), preferred_element_type=F32)


def pad_rows(w, half):
    zeros = jnp.zeros((64, w.shape[1]), w.dtype)
    return jnp.concatenate([w, zeros] if half == 0 else [zeros, w], axis=0)


def pad_lanes(w, half):
    zeros = jnp.zeros((w.shape[0], 64), w.dtype)
    return jnp.concatenate([w, zeros] if half == 0 else [zeros, w], axis=1)


def window(half):
    return slice(half * 128, half * 128 + 256)


MESH = pl.DeviceIdType.MESH


def remote(src, dst, send_sem, recv_sem, dp, seq):
    return pltpu.make_async_remote_copy(
        src_ref=src, dst_ref=dst, send_sem=send_sem, recv_sem=recv_sem,
        device_id={"dp": dp, "seq": seq}, device_id_type=MESH,
    )


def greet(n, group, i, s):
    barrier = pltpu.get_barrier_semaphore()
    for d in range(1, n):
        pl.semaphore_signal(barrier, inc=1, device_id={"dp": lax.rem(i + d, n), "seq": s}, device_id_type=MESH)
    for d in range(1, group):
        pl.semaphore_signal(barrier, inc=1, device_id={"dp": i, "seq": lax.rem(s + d, group)}, device_id_type=MESH)
    pl.semaphore_wait(barrier, n + group - 2)


def other(index):
    return index + 1 - 2 * lax.rem(index, 2)


def half_of(ref, lead, c):
    if len(ref.shape) == len(lead) + 3:
        return ref.at[lead + (c,)]
    lanes = ref.shape[-1] // 2
    at = pl.multiple_of(c * lanes, 128) if lanes % 128 == 0 else c * lanes
    return ref.at[lead + (slice(None), pl.ds(at, lanes))]


def stack_rows(pieces):
    if len(pieces) == 1:
        return pieces[0]
    if pieces[0].shape[0] % 16 == 0:
        return jnp.concatenate(pieces, axis=0)
    return jnp.concatenate([p.astype(F32) for p in pieces], axis=0).astype(pieces[0].dtype)


def join_lanes(pieces):
    return pieces[0] if len(pieces) == 1 else jnp.concatenate(pieces, axis=1)


def attend_kernel(
    n, len_ref, tok_ref, wq_in, wo_in, wu_in, wd_in, v0, v1, v2, v3, v4, v5, v6, v7,
    ctx_ref, linv_ref, e_ref, k_out, qT_out, vT_out, w_out, vec_out, x_out, ctx_pos, wo_out, wu_out, wd_out,
    qe, ke, ve, xp, x_buf, ctx_half, ctx_buf, q_part, wq_buf, vec_in, vec_buf,
    x_send, x_recv, c_send, c_recv, q_send, q_recv, r_send, r_recv, v_send, v_recv, z_send, z_recv, y_send, y_recv, p_send, p_recv, own, local,
):
    heads = qe.shape[0]
    sources, rows, _ = x_buf.shape
    gw = heads * HD
    slot = sources * 2 * rows
    per = v0.shape[-1]
    parts_q = wq_buf.shape[1]
    t = pl.program_id(0) // 2
    half_now = lax.rem(pl.program_id(0), 2)
    i = lax.axis_index("dp")
    me = lax.axis_index("seq")
    c = lax.rem(me, 2)
    y = lax.rem(i, 2)
    k = i // 2
    depth = n // 2
    weights = ((wo_in, wo_out), (wu_in, wu_out), (wd_in, wd_out))

    def x_copy(d):
        peer = lax.rem(me + d, sources)
        return remote(xp.at[peer], x_buf.at[sources - 1 - d], x_send.at[d - 1], x_recv.at[d - 1], i, peer)

    def ctx_copy(d):
        peer = lax.rem(me + d, sources)
        return remote(ctx_buf.at[d - 1], ctx_pos.at[me], c_send.at[d - 1], c_recv.at[d - 1], i, peer)

    def q_copy(d):
        return remote(wq_in.at[me], q_part.at[i], q_send.at[d - 1], q_recv.at[d - 1], lax.rem(i + d, n), me)

    def r_copy(d):
        peer = lax.rem(me + d, sources)
        return remote(
            q_part.at[pl.ds(peer * parts_q, parts_q)], wq_buf.at[me], r_send.at[d - 1], r_recv.at[d - 1], i, peer
        )

    def v_copy(d):
        return remote(vec_in, vec_buf.at[i], v_send.at[d - 1], v_recv.at[d - 1], lax.rem(i + d, n), me)

    def z_copy(w, d):
        src, dst = weights[w]
        to = lax.rem(k + d, depth)
        return remote(
            half_of(src, (), c), half_of(dst, (k, y), c), z_send.at[w, d - 1], z_recv.at[w, d - 1], to * 2 + y, me
        )

    def own_copy(w):
        src, dst = weights[w]
        return pltpu.make_async_copy(half_of(src, (), c), half_of(dst, (k, y), c), own.at[w])

    def y_copy(w):
        part = half_of(weights[w][1], (slice(None), y), c)
        return remote(part, part, y_send.at[w], y_recv.at[w], other(i), me)

    def p_copy(w):
        part = half_of(weights[w][1], (slice(None), slice(None)), c)
        return remote(part, part, p_send.at[w], p_recv.at[w], i, other(me))

    x_own = pltpu.make_async_copy(xp.at[me], x_buf.at[sources - 1], local.at[0])
    x_keep = pltpu.make_async_copy(x_buf, x_out, local.at[1])
    v_own = pltpu.make_async_copy(vec_in, vec_buf.at[i], local.at[2])
    ctx_own = pltpu.make_async_copy(ctx_buf.at[sources - 1], ctx_pos.at[me], local.at[3])
    q_own = pltpu.make_async_copy(wq_in.at[me], q_part.at[i], local.at[4])
    r_own = pltpu.make_async_copy(q_part.at[pl.ds(me * parts_q, parts_q)], wq_buf.at[me], local.at[5])

    def step_y(w):
        own_copy(w).wait()
        for d in range(1, depth):
            z_copy(w, d).wait_recv()
        y_copy(w).start()

    def step_p(w):
        y_copy(w).wait_recv()
        p_copy(w).start()

    @pl.when(pl.program_id(0) == 0)
    def _():
        for g in range(GROUPS):
            cols = slice(g * gw, (g + 1) * gw)
            xp[g] = jnp.concatenate([tok_ref[0:rows, cols], tok_ref[rows:, cols]], axis=1)
        vec_in[...] = jnp.zeros_like(vec_in)
        for v, ref in enumerate((v0, v1, v2, v3, v4, v5, v6, v7)):
            vec_in[v : v + 1, 0 : ref.shape[-1]] = ref[...].astype(F32).reshape(1, ref.shape[-1])
        greet(n, sources, i, me)
        for d in range(1, n):
            q_copy(d).start()
        q_own.start()
        x_copy(2).start()

        @pl.when(c == 0)
        def _():
            x_copy(1).start()

        @pl.when(c == 1)
        def _():
            x_copy(3).start()

        x_own.start()
        v_own.start()
        for d in range(1, n):
            v_copy(d).start()

        scale = HD ** (-0.5) * LOG2E
        lane = lax.broadcasted_iota(jnp.int32, (slot, 128), 1)
        ones_lane = jnp.where(lane == 0, 1.0, 0.0).astype(BF16)
        key_row = lax.broadcasted_iota(jnp.int32, (128, 2 * rows), 0)
        for h in range(heads):
            qe[h, :, 128:256] = ones_lane
        for j in range(sources):
            first = lax.rem(me + 1 + j, sources) * (2 * rows)
            key_pos = lax.broadcasted_iota(jnp.int32, (128, 2 * rows), 1) + first
            bias = jnp.where((key_row == 0) & (key_pos >= len_ref[0]), MASKED, 0.0).astype(BF16)
            for h in range(heads):
                ke[h, 128:256, j * 2 * rows : (j + 1) * 2 * rows] = bias

        q_own.wait()
        for d in range(1, n):
            q_copy(d).wait_recv()
        for d in range(1, sources):
            r_copy(d).start()
        for w in range(3):
            for d in range(1, depth):
                z_copy(w, d).start()
            own_copy(w).start()

        @pl.when(c == 0)
        def _():
            x_copy(3).start()

        @pl.when(c == 1)
        def _():
            x_copy(1).start()

        r_own.start()

        v_own.wait()
        for d in range(1, n):
            v_copy(d).wait_recv()
        vec_out[...] = vec_buf[...]
        count = gw // per
        q_bias = join_lanes([vec_buf[me * count + u, 0:1, 0:per] for u in range(count)])
        v_bias = join_lanes([vec_buf[(GROUPS + me) * count + u, 0:1, 0:per] for u in range(count)])
        b = jnp.concatenate([q_bias, jnp.zeros((1, gw), F32), v_bias], axis=1)
        r_own.wait()
        for d in range(1, sources):
            r_copy(d).wait_recv()
        weight = stack_rows([wq_buf[v, u] for u in range(parts_q) for v in range(sources)])
        w_out[...] = weight
        x_own.wait()
        for j in (3, 1, 2, 0):
            if j < sources - 1:
                x_copy(sources - 1 - j).wait_recv()
            for half in range(2):
                at = (j * 2 + half) * rows
                w = pad_rows(weight, half)
                qkv = (mm(x_buf[j, :, window(half)], w) + b).astype(BF16)
                q = qkv[:, :gw]
                kk = qkv[:, gw : 2 * gw]
                v = qkv[:, 2 * gw :]
                k_out[at : at + rows, :] = kk
                qT_out[:, at : at + rows] = q.T
                vT_out[:, at : at + rows] = v.T
                kT = kk.T
                scaled = q.astype(F32) * scale
                hi = scaled.astype(BF16)
                lo = (scaled - hi.astype(F32)).astype(BF16)
                ones = jnp.ones((rows, HD), BF16)
                for h in range(heads):
                    cols = slice(h * HD, (h + 1) * HD)
                    qe[h, at : at + rows, 0:128] = jnp.concatenate([hi[:, cols], lo[:, cols]], axis=1)
                    ke[h, 0:HD, at : at + rows] = kT[cols, :]
                    ke[h, HD : 2 * HD, at : at + rows] = kT[cols, :]
                    ve[h, at : at + rows, :] = jnp.concatenate([v[:, cols], ones], axis=1)
        x_keep.start()

    plan = {
        0: [(step_y, 0)], 1: [(step_y, 1)], 3: [(step_p, 0), (step_y, 2)], 5: [(step_p, 1)], 7: [(step_p, 2)],
    }
    for now, actions in plan.items():
        @pl.when(pl.program_id(0) == now)
        def _(actions=actions):
            for fn, w in actions:
                fn(w)

    parts = []
    inverse = []
    at = pl.multiple_of(pl.program_id(0) * rows, rows)
    for h in range(heads):
        scores = mm(qe[h, pl.ds(at, rows), :], ke[h])
        top = jnp.max(scores, axis=1, keepdims=True)
        e = jnp.exp2(scores - top).astype(BF16)
        e_ref[h] = e
        o = mm(e, ve[h])
        inv = 1.0 / o[:, HD:]
        inverse.append(inv)
        parts.append((o[:, :HD] * inv).astype(BF16))
    linv_ref[0, 0] = jnp.concatenate(inverse, axis=1)
    ctx_half[half_now] = jnp.concatenate(parts, axis=1)

    @pl.when(half_now == 1)
    def _():
        block = jnp.concatenate([ctx_half[0], ctx_half[1]], axis=1)
        ctx_ref[0] = block
        ctx_buf[t] = block
        for d in range(1, sources):
            @pl.when(t == d - 1)
            def _():
                ctx_copy(d).start()

    @pl.when(pl.program_id(0) == 2 * sources - 1)
    def _():
        ctx_own.start()
        for d in range(1, sources):
            x_copy(d).wait_send()
            r_copy(d).wait_send()
            ctx_copy(d).wait_send()
            ctx_copy(d).wait_recv()

        for d in range(1, n):
            q_copy(d).wait_send()
            v_copy(d).wait_send()
        for w in range(3):
            for d in range(1, depth):
                z_copy(w, d).wait_send()
            y_copy(w).wait_send()
            p_copy(w).wait()
        x_keep.wait()
        ctx_own.wait()


def attend(n, length, tok, wq, wo, wu, wd, vectors):
    sources, rows = GROUPS, tok.shape[0] // 2
    gw = 2 * wd.shape[1]
    heads = gw // HD
    slot = sources * 2 * rows
    depth = n // 2
    parts_q = n // GROUPS
    lanes = -(-max(v.shape[-1] for v in vectors) // 128) * 128
    block = (sources, rows, 2 * gw)
    whole = lambda *shape: pl.BlockSpec(shape, lambda s: (0,) * len(shape), pipeline_mode=pl.Buffered(1))
    out_whole = lambda *shape: pl.BlockSpec(shape, lambda s: (0,) * len(shape))
    anywhere = pl.BlockSpec(memory_space=pl.ANY)
    dma = lambda *shape: pltpu.SemaphoreType.DMA(shape)
    return pl.pallas_call(
        functools.partial(attend_kernel, n),
        grid=(2 * sources,),
        in_specs=[pl.BlockSpec(memory_space=pltpu.SMEM), whole(*tok.shape), anywhere]
        + [whole(*a.shape) for a in (wo, wu, wd) + vectors],
        out_specs=[
            pl.BlockSpec((1, rows, 2 * gw), lambda s: (s // 2, 0, 0)),
            pl.BlockSpec((1, 1, rows, gw), lambda s: (s // 2, lax.rem(s, 2), 0, 0)),
            pl.BlockSpec((heads, rows, slot), lambda s: (0, s, 0)),
            out_whole(slot, gw),
            out_whole(gw, slot),
            out_whole(gw, slot),
            out_whole(gw, 3 * gw),
            out_whole(n, 8, lanes),
            anywhere, anywhere, anywhere, anywhere, anywhere,
        ],
        out_shape=[
            jax.ShapeDtypeStruct(block, BF16),
            jax.ShapeDtypeStruct((sources, 2, rows, gw), F32),
            jax.ShapeDtypeStruct((heads, slot, slot), BF16),
            jax.ShapeDtypeStruct((slot, gw), BF16),
            jax.ShapeDtypeStruct((gw, slot), BF16),
            jax.ShapeDtypeStruct((gw, slot), BF16),
            jax.ShapeDtypeStruct((gw, 3 * gw), BF16),
            jax.ShapeDtypeStruct((n, 8, lanes), F32),
            jax.ShapeDtypeStruct(block, BF16),
            jax.ShapeDtypeStruct(block, BF16),
            jax.ShapeDtypeStruct((depth, 2) + wo.shape, BF16),
            jax.ShapeDtypeStruct((depth, 2) + wu.shape, BF16),
            jax.ShapeDtypeStruct((depth, 2) + wd.shape, BF16),
        ],
        scratch_shapes=[
            pltpu.VMEM((heads, slot, 256), BF16),
            pltpu.VMEM((heads, 256, slot), BF16),
            pltpu.VMEM((heads, slot, 128), BF16),
            pltpu.VMEM(block, BF16),
            pltpu.VMEM(block, BF16),
            pltpu.VMEM((2, rows, gw), BF16),
            pltpu.VMEM(block, BF16),
            pltpu.VMEM((n,) + wq.shape[1:], BF16),
            pltpu.VMEM((sources, parts_q) + wq.shape[1:], BF16),
            pltpu.VMEM((8, lanes), F32),
            pltpu.VMEM((n, 8, lanes), F32),
            dma(3), dma(3), dma(3), dma(3), dma(n - 1), dma(n - 1), dma(3), dma(3), dma(n - 1), dma(n - 1),
            dma(3, depth - 1), dma(3, depth - 1), dma(3), dma(3), dma(3), dma(3), dma(3), dma(6),
        ],
        compiler_params=pltpu.CompilerParams(vmem_limit_bytes=60 << 20, collective_id=1, has_side_effects=True),
        name="attend",
    )(length, tok, wq, wo, wu, wd, *vectors)


def revisit_kernel(
    n, per,
    e_ref, ctx_ref, linv_ref, qT_ref, vT_ref, k_ref, x_ref, w_ref, gctx_in, gwo_in, gwu_in, gwd_in, sm_in,
    gi_pos, gq_fin, gqv_out, gwo_out, gwu_out, gwd_out, sm_seq,
    vTe, kn, dkT, dvT, gT, gc_buf, gi_buf, sm_buf, sm_sum, gb_buf, gqv_buf, gq_buf, gq_got, gq_sum,
    mine0, mine1, mine2, core0, core1, core2, yb0, yb1, yb2, zb0, zb1, zb2, xm0, xm1, xm2, xb0, xb1, xb2, f0, f1, f2,
    g_send, g_recv, i_send, i_recv, sm_send, sm_recv, ss_send, ss_recv, b_send, b_recv, bs_send, bs_recv,
    q_send, q_recv, qs_send, qs_recv, c_send, c_recv, y_send, y_recv, z_send, z_recv, xs_send, xs_recv, p_send, p_recv, own, local,
):
    heads = kn.shape[0]
    sources, rows, _ = x_ref.shape
    gw = heads * HD
    slot = sources * 2 * rows
    parts_q = n // GROUPS
    u = pl.program_id(0)
    now = 2 * GROUPS - 1 - u
    half_now = lax.rem(now, 2)
    j = now // 2
    i = lax.axis_index("dp")
    me = lax.axis_index("seq")
    c = lax.rem(me, 2)
    y = lax.rem(i, 2)
    k = i // 2
    depth = n // 2
    across = lax.rem(me + 2, sources)
    every = slice(None)
    inputs = (gwo_in, gwu_in, gwd_in)
    outputs = (gwo_out, gwu_out, gwd_out)
    mine, core, ybuf, zbuf = (mine0, mine1, mine2), (core0, core1, core2), (yb0, yb1, yb2), (zb0, zb1, zb2)
    xmine, xbuf, final = (xm0, xm1, xm2), (xb0, xb1, xb2), (f0, f1, f2)

    def g_copy(d):
        peer = lax.rem(me + d, sources)
        return remote(gctx_in.at[peer], gc_buf.at[sources - 1 - d], g_send.at[d - 1], g_recv.at[d - 1], i, peer)

    def i_copy(d):
        return remote(gi_buf.at[d - 1], gi_pos.at[me], i_send.at[d - 1], i_recv.at[d - 1], i, lax.rem(me + d, sources))

    def sm_copy(d):
        to = lax.rem(i + d, n)
        return remote(sm_in.at[to], sm_buf.at[d - 1], sm_send.at[d - 1], sm_recv.at[d - 1], to, me)

    def ss_copy(d):
        return remote(sm_sum, sm_seq.at[me], ss_send.at[d - 1], ss_recv.at[d - 1], i, lax.rem(me + d, sources))

    def b_copy(d):
        return remote(gb_buf.at[i], gb_buf.at[i], b_send.at[d - 1], b_recv.at[d - 1], lax.rem(i + d, n), me)

    def bs_copy(d):
        return remote(gqv_buf, gqv_out, bs_send.at[d - 1], bs_recv, i, lax.rem(me + d, sources))

    def q_copy(d):
        to = lax.rem(i + d, n)
        return remote(gq_buf.at[to], gq_got.at[d - 1], q_send.at[d - 1], q_recv.at[d - 1], to, me)

    def qs_copy(d):
        spot = lax.rem(i, GROUPS)
        return remote(
            gq_sum, gq_fin.at[spot], qs_send.at[d], qs_recv.at[spot], me * parts_q + i // GROUPS, lax.rem(me + d, sources)
        )

    def own_copy(w):
        return pltpu.make_async_copy(half_of(inputs[w], (every, every), c), mine[w], own.at[w])

    def c_copy(w):
        return remote(half_of(inputs[w], (every, every), 1 - c), core[w], c_send.at[w], c_recv.at[w], i, other(me))

    def y_copy(w):
        return remote(mine[w].at[:, 1 - y], ybuf[w], y_send.at[w], y_recv.at[w], other(i), me)

    def z_copy(w, d):
        to = lax.rem(k + d, depth)
        return remote(mine[w].at[to, y], zbuf[w].at[d - 1], z_send.at[w, d - 1], z_recv.at[w, d - 1], to * 2 + y, me)

    def x_copy(w):
        return remote(xmine[w], xbuf[w], xs_send.at[w], xs_recv.at[w], i, across)

    def p_copy(w):
        return remote(final[w], outputs[w].at[c], p_send.at[w], p_recv.at[w], i, other(me))

    g_own = pltpu.make_async_copy(gctx_in.at[me], gc_buf.at[sources - 1], local.at[0])
    sm_own = pltpu.make_async_copy(sm_in.at[i], sm_buf.at[n - 1], local.at[1])
    ss_own = pltpu.make_async_copy(sm_sum, sm_seq.at[me], local.at[2])
    bs_own = pltpu.make_async_copy(gqv_buf, gqv_out, local.at[3])
    qs_own = pltpu.make_async_copy(gq_sum, gq_fin.at[lax.rem(i, GROUPS)], local.at[4])
    i_own = pltpu.make_async_copy(gi_buf.at[sources - 1], gi_pos.at[me], local.at[5])

    def p_own(w):
        return pltpu.make_async_copy(final[w], outputs[w].at[c], local.at[6 + w])

    stays = me * parts_q + i // GROUPS == i
    count = gw // per
    bias_owner = lax.rem(i // count, GROUPS) == me

    def step_y(w):
        own_copy(w).wait()
        c_copy(w).wait_recv()
        mine[w][...] += core[w][...]
        y_copy(w).start()

    def step_z(w):
        y_copy(w).wait_recv()
        mine[w][:, y] += ybuf[w][...]
        for d in range(1, depth):
            z_copy(w, d).start()

    def step_x(w):
        total = mine[w][k, y].astype(F32)
        for d in range(1, depth):
            z_copy(w, d).wait_recv()
            total += zbuf[w][d - 1].astype(F32)
        xmine[w][...] = total.astype(BF16)
        x_copy(w).start()

    def step_p(w):
        x_copy(w).wait_recv()
        final[w][...] = xmine[w][...].astype(F32) + xbuf[w][...].astype(F32)
        p_copy(w).start()
        p_own(w).start()

    def small_sum():
        sm_own.wait()
        total = sm_buf[n - 1]
        for d in range(1, n):
            sm_copy(d).wait_recv()
            total += sm_buf[d - 1]
        sm_sum[...] = total
        ss_own.start()
        for d in range(1, sources):
            ss_copy(d).start()

    @pl.when(u == 0)
    def _():
        greet(n, sources, i, me)
        for d in (1, 2, 3):
            g_copy(d).start()
        g_own.start()
        for w in range(3):
            c_copy(w).start()
            own_copy(w).start()
        sm_own.start()
        for d in range(1, n):
            sm_copy(d).start()
        dkT[...] = jnp.zeros_like(dkT)
        dvT[...] = jnp.zeros_like(dvT)
        row = lax.broadcasted_iota(jnp.int32, (HD, slot), 0)
        ones_rows = jnp.where(row < 2, 1.0, 0.0).astype(BF16)
        for h in range(heads):
            cols = slice(h * HD, (h + 1) * HD)
            vTe[h, 0:HD, :] = vT_ref[cols, :]
            vTe[h, HD:, :] = ones_rows
            kn[h] = k_ref[:, cols]
        g_own.wait()

    for d in range(1, sources):
        @pl.when(u == 2 * d)
        def _(d=d):
            g_copy(d).wait_recv()

    plan = {
        1: [(step_y, 0), (step_y, 1)], 2: [(step_y, 2)], 3: [(step_z, 0)], 5: [(step_z, 1)], 6: [(step_x, 0)],
        7: [(step_z, 2), (step_x, 1), (step_p, 0)],
    }
    for when_u, actions in plan.items():
        @pl.when(u == when_u)
        def _(actions=actions):
            for fn, w in actions:
                fn(w)

    @pl.when(u == 4)
    def _():
        small_sum()

    lane = lax.broadcasted_iota(jnp.int32, (rows, HD), 1)
    at = pl.multiple_of(now * rows, rows)
    both = gc_buf[j].astype(F32)
    g = jnp.where(half_now == 0, both[:, :gw], both[:, gw:]) * linv_ref[0, 0]
    g_low = g.astype(BF16)
    gT_low = g_low.T
    both = ctx_ref[0].astype(F32)
    prod = g * jnp.where(half_now == 0, both[:, :gw], both[:, gw:])
    dqs = []
    for h in range(heads):
        cols = slice(h * HD, (h + 1) * HD)
        delta = -jnp.sum(prod[:, cols], axis=1, keepdims=True)
        d_hi = delta.astype(BF16)
        d_lo = (delta - d_hi.astype(F32)).astype(BF16)
        tail = jnp.where(lane == 0, d_hi, jnp.where(lane == 1, d_lo, jnp.zeros((), BF16)))
        ge = jnp.concatenate([g_low[:, cols], tail], axis=1)
        e = e_ref[h]
        ds = (e.astype(F32) * mm(ge, vTe[h])).astype(BF16)
        dvT[cols, :] += mm(gT_low[cols, :], e)
        dkT[cols, :] += mm(qT_ref[cols, :], ds)
        dqs.append((mm(ds, kn[h]) * (HD ** (-0.5))).astype(BF16))
    gT[0:gw, pl.ds(at, rows)] = jnp.concatenate(dqs, axis=1).T

    @pl.when(u == 2 * sources - 1)
    def _():
        gT[gw : 2 * gw, :] = (dkT[...] * (HD ** (-0.5))).astype(BF16)
        gT[2 * gw :, :] = dvT[...].astype(BF16)
        sums = [None, None]
        for q in range(sources):
            for half in range(2):
                part = mm(gT[:, (q * 2 + half) * rows : (q * 2 + half + 1) * rows], x_ref[q, :, window(half)])
                sums[half] = part if sums[half] is None else sums[half] + part
        gq = (sums[0][:, :gw] + sums[1][:, 64:]).T
        size = gw // n
        for piece in range(n):
            gq_buf[piece] = gq[piece * size : (piece + 1) * size].astype(BF16)
        gb_buf[i] = mm_nt(jnp.ones((8, slot), BF16), gT[...])
        ready = 0
        for q in (1, 0, 2, 3):
            packed = [
                mm(w_ref[...], gT[:, (q * 2 + half) * rows : (q * 2 + half + 1) * rows]).T.astype(BF16)
                for half in range(2)
            ]
            block = jnp.concatenate(packed, axis=1)
            if ready:
                i_copy(ready).start()
            else:
                for d in range(1, n):
                    q_copy(d).start()
                for d in range(1, n):
                    b_copy(d).start()
            gi_buf[q] = block
            ready = q + 1
        i_own.start()
        step_x(2)
        step_p(1)
        total = gq_buf[i].astype(F32)
        for d in range(1, n):
            q_copy(d).wait_recv()
            total += gq_got[d - 1].astype(F32)
        gq_sum[...] = total.astype(BF16)
        for d in range(1, n):
            b_copy(d).wait_recv()

        @pl.when(bias_owner)
        def _():
            total = gb_buf[0, 0:1, :]
            for d in range(1, n):
                total += gb_buf[d, 0:1, :]
            side = jnp.where(i < n // 2, total[:, :gw], total[:, 2 * gw :])
            piece = lax.rem(i, count)
            value = side[:, 0:per]
            for v in range(1, count):
                value = jnp.where(piece == v, side[:, v * per : (v + 1) * per], value)
            gqv_buf[0:1, 0:per] = value
            bs_own.start()
            for d in range(1, sources):
                bs_copy(d).start()

        for d in range(1, sources):
            qs_copy(d).start()

        @pl.when(stays)
        def _():
            qs_own.start()

        @pl.when(jnp.logical_not(stays))
        def _():
            qs_copy(0).start()

        step_p(2)

        ss_own.wait()
        i_own.wait()
        for d in range(1, sources):
            ss_copy(d).wait_recv()
            i_copy(d).wait_recv()
        for w in range(3):
            p_copy(w).wait_recv()
            p_own(w).wait()

        @pl.when(jnp.logical_not(bias_owner))
        def _():
            bs_copy(1).wait_recv()

        for spot in range(GROUPS):
            source = lax.rem(i, parts_q) * GROUPS + spot

            @pl.when(jnp.logical_not(jnp.logical_and(i // parts_q == me, source == i)))
            def _():
                remote(gq_sum, gq_fin.at[spot], qs_send.at[0], qs_recv.at[spot], other(i), me).wait_recv()

        for d in range(1, sources):
            g_copy(d).wait_send()
            i_copy(d).wait_send()
            ss_copy(d).wait_send()

        @pl.when(bias_owner)
        def _():
            bs_own.wait()
            for d in range(1, sources):
                bs_copy(d).wait_send()

        for d in range(1, sources):
            qs_copy(d).wait_send()

        @pl.when(stays)
        def _():
            qs_own.wait()

        @pl.when(jnp.logical_not(stays))
        def _():
            qs_copy(0).wait_send()

        for d in range(1, n):
            q_copy(d).wait_send()
        for d in range(1, n):
            sm_copy(d).wait_send()
            b_copy(d).wait_send()
        for w in range(3):
            c_copy(w).wait_send()
            y_copy(w).wait_send()
            for d in range(1, depth):
                z_copy(w, d).wait_send()
            x_copy(w).wait_send()
            p_copy(w).wait_send()


def revisit(n, per, e, ctx, linv, qT, vT, k, x, w, gctx, gwo, gwu, gwd, small):
    sources, rows, _ = x.shape
    gw = w.shape[0]
    heads = gw // HD
    slot = sources * 2 * rows
    depth = n // 2
    last = 2 * sources - 1
    whole = lambda *shape: pl.BlockSpec(shape, lambda s: (0,) * len(shape), pipeline_mode=pl.Buffered(1))
    anywhere = pl.BlockSpec(memory_space=pl.ANY)
    dma = lambda *shape: pltpu.SemaphoreType.DMA(shape)

    def half_shape(a):
        return a.shape[3:] if len(a.shape) == 5 else (a.shape[2], a.shape[3] // 2)

    halves = [half_shape(a) for a in (gwo, gwu, gwd)]
    outs = [
        jax.ShapeDtypeStruct(x.shape, BF16),
        jax.ShapeDtypeStruct((GROUPS, gw // n, 3 * gw), BF16),
        jax.ShapeDtypeStruct((8, 256), F32),
        jax.ShapeDtypeStruct((2,) + halves[0], F32),
        jax.ShapeDtypeStruct((2,) + halves[1], F32),
        jax.ShapeDtypeStruct((2,) + halves[2], F32),
        jax.ShapeDtypeStruct((sources,) + small.shape[1:], F32),
    ]
    vmem = pltpu.VMEM
    return pl.pallas_call(
        functools.partial(revisit_kernel, n, per),
        grid=(2 * sources,),
        in_specs=[
            pl.BlockSpec((heads, rows, slot), lambda s: (0, last - s, 0)),
            pl.BlockSpec((1, rows, 2 * gw), lambda s: ((last - s) // 2, 0, 0)),
            pl.BlockSpec((1, 1, rows, gw), lambda s: ((last - s) // 2, lax.rem(last - s, 2), 0, 0)),
            pl.BlockSpec((gw, rows), lambda s: (0, last - s)),
            whole(*vT.shape), whole(*k.shape), whole(*x.shape), whole(*w.shape),
            anywhere, anywhere, anywhere, anywhere, anywhere,
        ],
        out_specs=[anywhere] * len(outs),
        out_shape=outs,
        scratch_shapes=[
            vmem((heads, 2 * HD, slot), BF16),
            vmem((heads, slot, HD), BF16),
            vmem((gw, slot), F32),
            vmem((gw, slot), F32),
            vmem((3 * gw, slot), BF16),
            vmem(x.shape, BF16), vmem(x.shape, BF16),
            vmem(small.shape, F32), vmem(small.shape[1:], F32),
            vmem((n, 8, 3 * gw), F32), vmem((8, 256), F32),
            vmem((n, gw // n, 3 * gw), BF16),
            vmem((n - 1, gw // n, 3 * gw), BF16),
            vmem((gw // n, 3 * gw), BF16),
        ]
        + [vmem((depth, 2) + s, BF16) for s in halves]
        + [vmem((depth, 2) + s, BF16) for s in halves]
        + [vmem((depth,) + s, BF16) for s in halves]
        + [vmem((depth - 1,) + s, BF16) for s in halves]
        + [vmem(s, BF16) for s in halves]
        + [vmem(s, BF16) for s in halves]
        + [vmem(s, F32) for s in halves]
        + [
            dma(3), dma(3), dma(3), dma(3), dma(n - 1), dma(n - 1), dma(3), dma(3), dma(n - 1), dma(n - 1),
            dma(3), pltpu.SemaphoreType.DMA, dma(n - 1), dma(n - 1), dma(4), dma(4),
            dma(3), dma(3), dma(3), dma(3), dma(3, depth - 1), dma(3, depth - 1), dma(3), dma(3), dma(3), dma(3), dma(3), dma(9),
        ],
        compiler_params=pltpu.CompilerParams(vmem_limit_bytes=62 << 20, collective_id=2, has_side_effects=True),
        name="revisit",
    )(e, ctx, linv, qT, vT, k, x, w, gctx, gwo, gwu, gwd, small)


def split_rows(values):
    mean = jnp.mean(values, axis=-1, keepdims=True)
    centred = values - mean
    var = jnp.mean(centred * centred, axis=-1, keepdims=True)
    return centred, lax.rsqrt(var + epsilon)


def norm_back(grad, unit, inverse, gain):
    g = grad * gain
    m1 = jnp.mean(g, axis=-1, keepdims=True)
    m2 = jnp.mean(g * unit, axis=-1, keepdims=True)
    return inverse * (g - m1 - unit * m2)


def join_windows(parts):
    tiles = []
    for even, odd in zip(parts[0::2], parts[1::2]):
        tiles += [even[:, :128], even[:, 128:] + odd[:, :128], odd[:, 128:]]
    return jnp.concatenate(tiles, axis=1)


def group_window(g):
    at = (g // 2) * 384 + (g % 2) * 128
    return slice(at, at + 256)


def middle_kernel(
    n, len_ref, ctx_ref, tok_ref, gout_ref, wo_ref, wu_ref, wd_ref, vec_ref,
    out_ref, gctx_ref, gres_ref, gwo_ref, gwu_ref, gwd_ref, small_ref, upad, dpad, awo, awu, awd, sums, usums,
):
    rows = ctx_ref.shape[1]
    gw = ctx_ref.shape[2] // 2
    width = tok_ref.shape[1]
    hidden = wu_ref.shape[1]
    share = width // n
    first_row = lax.axis_index("seq") * (2 * rows)
    vec = join_lanes([vec_ref[d, :, 0:share] for d in range(n)])
    obias, gain1, shift1, dbias, gain2, shift2 = (vec[v : v + 1] for v in range(1, 7))
    count = n // GROUPS
    for g in range(GROUPS):
        upad[g] = pad_rows(wu_ref[g * gw : (g + 1) * gw, :], g % 2)
        odd = 64 * (g % 2)
        dpad[g, 192 * (1 - g % 2) : 192 * (1 - g % 2) + 64, :] = jnp.zeros((64, hidden), BF16)
        size = hidden // count
        for d in range(count):
            for v in range(2):
                at = odd + v * (gw // 2)
                dpad[g, at : at + gw // 2, d * size : (d + 1) * size] = wd_ref[g * count + d, v]
    packed = [[] for _ in range(GROUPS)]
    for half in range(2):
        first = half == 0

        def keep(ref, at, value):
            if first:
                ref[at] = value
            else:
                ref[at] += value

        r = slice(half * rows, (half + 1) * rows)
        x = tok_ref[r, :].astype(F32) + obias
        for g in range(GROUPS):
            x += mm(ctx_ref[g, :, window(half)], pad_rows(wo_ref[g * gw : (g + 1) * gw, :], half))
        c1, i1 = split_rows(x)
        n1 = c1 * i1
        mixed = n1 * gain1 + shift1
        low = mixed.astype(BF16)
        lowered = []
        slopes = []
        actives = []
        for g in range(GROUPS):
            ub = join_lanes([vec_ref[g * count + d, 7:8, 0 : hidden // count] for d in range(count)])
            u = mm(low[:, group_window(g)], upad[g]) + ub
            phi = 0.5 + 0.5 * lax.erf(u * (0.5 ** 0.5))
            slope = phi + u * (jnp.exp(u * u * -0.5) * 0.3989422804014327)
            act = (u * phi).astype(BF16)
            actives.append(act)
            slopes.append(slope)
            lowered.append(mm_nt(act, dpad[g]))
        x = mixed + join_windows(lowered) + dbias
        c2, i2 = split_rows(x)
        n2 = c2 * i2
        row = lax.broadcasted_iota(jnp.int32, (rows, 1), 0) + (first_row + half * rows)
        valid = jnp.where(row < len_ref[0], 1.0, 0.0)
        out_ref[r, :] = (valid * (n2 * gain2 + shift2)).astype(BF16)
        gy = gout_ref[r, :].astype(F32) * valid
        d2 = norm_back(gy, n2, i2, gain2)
        keep(sums, slice(4, 5), jnp.sum(gy * n2, axis=0, keepdims=True))
        keep(sums, slice(5, 6), jnp.sum(gy, axis=0, keepdims=True))
        keep(sums, slice(3, 4), jnp.sum(d2, axis=0, keepdims=True))
        d2_low = d2.astype(BF16)
        backs = []
        for g in range(GROUPS):
            win = d2_low[:, group_window(g)]
            odd = 64 * (g % 2)
            part = mm_tn(win, actives[g])[odd : odd + gw]
            if first:
                awd[g] = part
            else:
                part = (awd[g] + part).astype(BF16)
                size = hidden // count
                for d in range(count):
                    for v in range(2):
                        gwd_ref[g * count + d, v] = part[v * (gw // 2) : (v + 1) * (gw // 2), d * size : (d + 1) * size]
            gu = mm(win, dpad[g]) * slopes[g]
            keep(usums, slice(g, g + 1), jnp.sum(gu, axis=0, keepdims=True))
            gu_low = gu.astype(BF16)
            part = mm_tn(low[:, group_window(g)], gu_low)[odd : odd + gw]
            if first:
                awu[g] = part
            else:
                gwu_ref[g * gw : (g + 1) * gw, :] = (awu[g] + part).astype(BF16)
            backs.append(mm_nt(gu_low, upad[g]))
        gm = join_windows(backs) + d2
        d1 = norm_back(gm, n1, i1, gain1)
        keep(sums, slice(1, 2), jnp.sum(gm * n1, axis=0, keepdims=True))
        keep(sums, slice(2, 3), jnp.sum(gm, axis=0, keepdims=True))
        keep(sums, slice(0, 1), jnp.sum(d1, axis=0, keepdims=True))
        gres_ref[r, :] = d1
        d1_low = d1.astype(BF16)
        for g in range(GROUPS):
            part = mm_tn(ctx_ref[g, :, window(half)], d1_low)[64 * half : 64 * half + gw]
            if first:
                awo[g] = part
            else:
                gwo_ref[g * gw : (g + 1) * gw, :] = (awo[g] + part).astype(BF16)
        back = mm_nt(d1_low, wo_ref[...]).astype(BF16)
        for g in range(GROUPS):
            packed[g].append(back[:, g * gw : (g + 1) * gw])
    for g in range(GROUPS):
        gctx_ref[g] = jnp.concatenate(packed[g], axis=1)
    sums[6:8, :] = jnp.zeros((2, width), F32)
    up_share = hidden // count
    for d in range(n):
        small_ref[d] = jnp.zeros(small_ref.shape[1:], F32)
        small_ref[d, 0:8, 0:share] = sums[0:8, d * share : (d + 1) * share]
        at = (d % count) * up_share
        for v in range(0, up_share, 128):
            size = min(128, up_share - v)
            small_ref[d, 8 + v // 128 : 9 + v // 128, 0:size] = usums[d // count : d // count + 1, at + v : at + v + size]


def middle(n, length, ctx, tok, gout, wo, wu, wd, vec):
    hidden = wu.shape[1]
    width = tok.shape[1]
    gw = width // GROUPS
    vmem = pl.BlockSpec(memory_space=pltpu.VMEM)
    return pl.pallas_call(
        functools.partial(middle_kernel, n),
        in_specs=[pl.BlockSpec(memory_space=pltpu.SMEM)] + [vmem] * 7,
        out_specs=[vmem] * 7,
        out_shape=[
            jax.ShapeDtypeStruct(tok.shape, BF16),
            jax.ShapeDtypeStruct(ctx.shape, BF16),
            jax.ShapeDtypeStruct(tok.shape, F32),
            jax.ShapeDtypeStruct(wo.shape, BF16),
            jax.ShapeDtypeStruct(wu.shape, BF16),
            jax.ShapeDtypeStruct(wd.shape, BF16),
            jax.ShapeDtypeStruct((n, 16, 128), F32),
        ],
        scratch_shapes=[
            pltpu.VMEM((GROUPS, 256, hidden), BF16),
            pltpu.VMEM((GROUPS, 256, hidden), BF16),
            pltpu.VMEM((GROUPS, gw, width), F32),
            pltpu.VMEM((GROUPS, gw, hidden), F32),
            pltpu.VMEM((GROUPS, gw, hidden), F32),
            pltpu.VMEM((8, width), F32),
            pltpu.VMEM((8, hidden), F32),
        ],
        compiler_params=pltpu.CompilerParams(vmem_limit_bytes=62 << 20),
        name="middle",
    )(length, ctx, tok, gout, wo, wu, wd, vec)


def finish_kernel(
    gi_ref, gres_ref, gq_ref, gqv_ref, gwo_ref, gwu_ref, gwd_ref, sm_ref,
    tok_out, qkv_out, qv_out, wo_out, b0_out, b1_out, b2_out, wu_out, up_out, wd_out, b3_out, b4_out, b5_out,
):
    rows = gi_ref.shape[1]
    gw = gi_ref.shape[2] // 2
    for half in range(2):
        r = slice(half * rows, (half + 1) * rows)
        lanes = slice(half * gw, (half + 1) * gw)
        for pair in range(GROUPS // 2):
            both = jnp.concatenate([gi_ref[2 * pair, :, lanes], gi_ref[2 * pair + 1, :, lanes]], axis=1)
            wide = slice(pair * 2 * gw, (pair + 1) * 2 * gw)
            tok_out[r, wide] = (both.astype(F32) + gres_ref[r, wide]).astype(BF16)
    qkv_out[...] = jnp.concatenate([gq_ref[v].astype(F32) for v in range(gq_ref.shape[0])], axis=0)
    qv_out[...] = gqv_ref[0:1, 0 : qv_out.shape[1]]
    for ref, out in ((gwo_ref, wo_out), (gwu_ref, wu_out)):
        out[...] = jnp.concatenate([ref[0], ref[1]], axis=1)
    size = gwd_ref.shape[1]
    for v in range(2):
        wd_out[v * size : (v + 1) * size, :] = gwd_ref[v]
    total = sm_ref[0] + sm_ref[1] + sm_ref[2] + sm_ref[3]
    for v, out in enumerate((b0_out, b1_out, b2_out, b3_out, b4_out, b5_out)):
        out[...] = total[v : v + 1, 0 : out.shape[1]]
    for v in range(0, up_out.shape[1], 128):
        step = min(128, up_out.shape[1] - v)
        up_out[:, v : v + step] = total[8 + v // 128 : 9 + v // 128, 0:step]


def finish(shapes, *args):
    vmem = pl.BlockSpec(memory_space=pltpu.VMEM)
    return pl.pallas_call(
        finish_kernel,
        in_specs=[vmem] * len(args),
        out_specs=[vmem] * len(shapes),
        out_shape=[jax.ShapeDtypeStruct(s, BF16 if v == 0 else F32) for v, s in enumerate(shapes)],
        compiler_params=pltpu.CompilerParams(vmem_limit_bytes=60 << 20),
        name="finish",
    )(*args)


def on_device(
    tokens, lengths, qkv_weight, qv_bias, out_weight, out_bias, norm_gain, norm_shift,
    up_weight, up_bias, down_weight, down_bias, final_gain, final_shift, grad_output,
):
    n = lax.axis_size("dp")
    width = tokens.shape[2]
    per = qv_bias.shape[0]
    vectors = tuple(
        a[None] if a.shape[0] <= 128 else a for a in (qv_bias, out_bias, norm_gain, norm_shift, down_bias, final_gain, final_shift, up_bias)
    )
    wq = qkv_weight.reshape(GROUPS, qkv_weight.shape[0] // GROUPS, qkv_weight.shape[1])
    wd_halves = down_weight.T.reshape(2, down_weight.shape[1] // 2, down_weight.shape[0])
    ctx, linv, e, k, qT, vT, w, vecs, x_all, ctx_pos, wo, wu, wd = attend(
        n, lengths, tokens[0], wq, out_weight, up_weight, wd_halves, vectors
    )
    output, gctx, gres, gwo, gwu, gwd, small = middle(
        n, lengths, ctx_pos, tokens[0], grad_output[0],
        wo.reshape(width, width), wu.reshape(width, -1), wd.reshape((n,) + wd.shape[2:]), vecs,
    )
    parts = revisit(
        n, per, e, ctx, linv, qT, vT, k, x_all, w, gctx,
        gwo.reshape(wo.shape), gwu.reshape(wu.shape), gwd.reshape(wd.shape), small,
    )
    one = lambda a: (1, a.shape[0])
    shapes = (
        tokens.shape[1:], qkv_weight.shape, one(qv_bias), out_weight.shape, one(out_bias), one(norm_gain),
        one(norm_shift), up_weight.shape, one(up_bias), down_weight.shape[::-1], one(down_bias), one(final_gain), one(final_shift),
    )
    outs = list(finish(shapes, parts[0], gres, *parts[1:]))
    outs[9] = outs[9].T
    flat = [a[0] if a.shape[0] == 1 else a for a in outs[1:]]
    return (output[None], outs[0][None], *flat)


def solution(mesh):
    rows = P("dp", "seq", None)
    mat = P("dp", None)
    vec = P("dp")
    in_specs = (rows, vec, mat, vec, mat, vec, vec, vec, mat, vec, mat, vec, vec, vec, rows)
    out_specs = (rows, rows, mat, vec, mat, vec, vec, vec, mat, vec, mat, vec, vec, vec)
    return jax.shard_map(on_device, mesh=mesh, in_specs=in_specs, out_specs=out_specs, check_vma=False)
```

```python
import functools

import jax
import jax.numpy as jnp
from jax import lax
from jax.experimental import pallas as pl
from jax.experimental.pallas import tpu as pltpu
from jax.sharding import PartitionSpec as P

H = 12
GROUPS = 4
HD = 64
epsilon = 1e-05
LOG2E = 1.4426950408889634
MASKED = -1e30
F32 = jnp.float32
BF16 = jnp.bfloat16


def mm(a, b):
    return jnp.dot(a, b, preferred_element_type=F32)


def mm_nt(a, b):
    return lax.dot_general(a, b, (((1,), (1,)), ((), ())), preferred_element_type=F32)


def mm_tn(a, b):
    return lax.dot_general(a, b, (((0,), (0,)), ((), ())), preferred_element_type=F32)


def pad_rows(w, half):
    zeros = jnp.zeros((64, w.shape[1]), w.dtype)
    return jnp.concatenate([w, zeros] if half == 0 else [zeros, w], axis=0)


def pad_lanes(w, half):
    zeros = jnp.zeros((w.shape[0], 64), w.dtype)
    return jnp.concatenate([w, zeros] if half == 0 else [zeros, w], axis=1)


def window(half):
    return slice(half * 128, half * 128 + 256)


MESH = pl.DeviceIdType.MESH


def remote(src, dst, send_sem, recv_sem, dp, seq):
    return pltpu.make_async_remote_copy(
        src_ref=src, dst_ref=dst, send_sem=send_sem, recv_sem=recv_sem,
        device_id={"dp": dp, "seq": seq}, device_id_type=MESH,
    )


def greet(n, group, i, s):
    barrier = pltpu.get_barrier_semaphore()
    for d in range(1, n):
        pl.semaphore_signal(barrier, inc=1, device_id={"dp": lax.rem(i + d, n), "seq": s}, device_id_type=MESH)
    for d in range(1, group):
        pl.semaphore_signal(barrier, inc=1, device_id={"dp": i, "seq": lax.rem(s + d, group)}, device_id_type=MESH)
    pl.semaphore_wait(barrier, n + group - 2)


def other(index):
    return index + 1 - 2 * lax.rem(index, 2)


def half_of(ref, lead, c):
    if len(ref.shape) == len(lead) + 3:
        return ref.at[lead + (c,)]
    lanes = ref.shape[-1] // 2
    at = pl.multiple_of(c * lanes, 128) if lanes % 128 == 0 else c * lanes
    return ref.at[lead + (slice(None), pl.ds(at, lanes))]


def stack_rows(pieces):
    if len(pieces) == 1:
        return pieces[0]
    if pieces[0].shape[0] % 16 == 0:
        return jnp.concatenate(pieces, axis=0)
    return jnp.concatenate([p.astype(F32) for p in pieces], axis=0).astype(pieces[0].dtype)


def join_lanes(pieces):
    return pieces[0] if len(pieces) == 1 else jnp.concatenate(pieces, axis=1)


def attend_kernel(
    n, len_ref, tok_ref, wq_in, wo_in, wu_in, wd_in, v0, v1, v2, v3, v4, v5, v6, v7,
    ctx_ref, linv_ref, e_ref, k_out, qT_out, vT_out, w_out, vec_out, x_out, ctx_pos, wo_out, wu_out, wd_out,
    qe, ke, ve, xp, x_buf, ctx_half, ctx_buf, q_part, wq_buf, vec_in, vec_buf,
    x_send, x_recv, c_send, c_recv, q_send, q_recv, r_send, r_recv, v_send, v_recv, z_send, z_recv, y_send, y_recv, p_send, p_recv, own, local,
):
    heads = qe.shape[0]
    sources, rows, _ = x_buf.shape
    gw = heads * HD
    slot = sources * 2 * rows
    per = v0.shape[-1]
    parts_q = wq_buf.shape[1]
    t = pl.program_id(0) // 2
    half_now = lax.rem(pl.program_id(0), 2)
    i = lax.axis_index("dp")
    me = lax.axis_index("seq")
    c = lax.rem(me, 2)
    y = lax.rem(i, 2)
    k = i // 2
    depth = n // 2
    weights = ((wo_in, wo_out), (wu_in, wu_out), (wd_in, wd_out))

    def x_copy(d):
        peer = lax.rem(me + d, sources)
        return remote(xp.at[peer], x_buf.at[sources - 1 - d], x_send.at[d - 1], x_recv.at[d - 1], i, peer)

    def ctx_copy(d):
        peer = lax.rem(me + d, sources)
        return remote(ctx_buf.at[d - 1], ctx_pos.at[me], c_send.at[d - 1], c_recv.at[d - 1], i, peer)

    def q_copy(d):
        return remote(wq_in.at[me], q_part.at[i], q_send.at[d - 1], q_recv.at[d - 1], lax.rem(i + d, n), me)

    def r_copy(d):
        peer = lax.rem(me + d, sources)
        return remote(
            q_part.at[pl.ds(peer * parts_q, parts_q)], wq_buf.at[me], r_send.at[d - 1], r_recv.at[d - 1], i, peer
        )

    def v_copy(d):
        return remote(vec_in, vec_buf.at[i], v_send.at[d - 1], v_recv.at[d - 1], lax.rem(i + d, n), me)

    def z_copy(w, d):
        src, dst = weights[w]
        to = lax.rem(k + d, depth)
        return remote(
            half_of(src, (), c), half_of(dst, (k, y), c), z_send.at[w, d - 1], z_recv.at[w, d - 1], to * 2 + y, me
        )

    def own_copy(w):
        src, dst = weights[w]
        return pltpu.make_async_copy(half_of(src, (), c), half_of(dst, (k, y), c), own.at[w])

    def y_copy(w):
        part = half_of(weights[w][1], (slice(None), y), c)
        return remote(part, part, y_send.at[w], y_recv.at[w], other(i), me)

    def p_copy(w):
        part = half_of(weights[w][1], (slice(None), slice(None)), c)
        return remote(part, part, p_send.at[w], p_recv.at[w], i, other(me))

    x_own = pltpu.make_async_copy(xp.at[me], x_buf.at[sources - 1], local.at[0])
    x_keep = pltpu.make_async_copy(x_buf, x_out, local.at[1])
    v_own = pltpu.make_async_copy(vec_in, vec_buf.at[i], local.at[2])
    ctx_own = pltpu.make_async_copy(ctx_buf.at[sources - 1], ctx_pos.at[me], local.at[3])
    q_own = pltpu.make_async_copy(wq_in.at[me], q_part.at[i], local.at[4])
    r_own = pltpu.make_async_copy(q_part.at[pl.ds(me * parts_q, parts_q)], wq_buf.at[me], local.at[5])

    def step_y(w):
        own_copy(w).wait()
        for d in range(1, depth):
            z_copy(w, d).wait_recv()
        y_copy(w).start()

    def step_p(w):
        y_copy(w).wait_recv()
        p_copy(w).start()

    @pl.when(pl.program_id(0) == 0)
    def _():
        for g in range(GROUPS):
            cols = slice(g * gw, (g + 1) * gw)
            xp[g] = jnp.concatenate([tok_ref[0:rows, cols], tok_ref[rows:, cols]], axis=1)
        vec_in[...] = jnp.zeros_like(vec_in)
        for v, ref in enumerate((v0, v1, v2, v3, v4, v5, v6, v7)):
            vec_in[v : v + 1, 0 : ref.shape[-1]] = ref[...].astype(F32).reshape(1, ref.shape[-1])
        greet(n, sources, i, me)
        for d in range(1, n):
            q_copy(d).start()
        q_own.start()
        x_copy(2).start()

        @pl.when(c == 0)
        def _():
            x_copy(1).start()

        @pl.when(c == 1)
        def _():
            x_copy(3).start()

        x_own.start()
        v_own.start()
        for d in range(1, n):
            v_copy(d).start()

        scale = HD ** (-0.5) * LOG2E
        lane = lax.broadcasted_iota(jnp.int32, (slot, 128), 1)
        ones_lane = jnp.where(lane == 0, 1.0, 0.0).astype(BF16)
        key_row = lax.broadcasted_iota(jnp.int32, (128, 2 * rows), 0)
        for h in range(heads):
            qe[h, :, 128:256] = ones_lane
        for j in range(sources):
            first = lax.rem(me + 1 + j, sources) * (2 * rows)
            key_pos = lax.broadcasted_iota(jnp.int32, (128, 2 * rows), 1) + first
            bias = jnp.where((key_row == 0) & (key_pos >= len_ref[0]), MASKED, 0.0).astype(BF16)
            for h in range(heads):
                ke[h, 128:256, j * 2 * rows : (j + 1) * 2 * rows] = bias

        q_own.wait()
        for d in range(1, n):
            q_copy(d).wait_recv()
        for d in range(1, sources):
            r_copy(d).start()
        for w in range(3):
            for d in range(1, depth):
                z_copy(w, d).start()
            own_copy(w).start()

        @pl.when(c == 0)
        def _():
            x_copy(3).start()

        @pl.when(c == 1)
        def _():
            x_copy(1).start()

        r_own.start()

        v_own.wait()
        for d in range(1, n):
            v_copy(d).wait_recv()
        vec_out[...] = vec_buf[...]
        count = gw // per
        q_bias = join_lanes([vec_buf[me * count + u, 0:1, 0:per] for u in range(count)])
        v_bias = join_lanes([vec_buf[(GROUPS + me) * count + u, 0:1, 0:per] for u in range(count)])
        b = jnp.concatenate([q_bias, jnp.zeros((1, gw), F32), v_bias], axis=1)
        r_own.wait()
        for d in range(1, sources):
            r_copy(d).wait_recv()
        weight = stack_rows([wq_buf[v, u] for u in range(parts_q) for v in range(sources)])
        w_out[...] = weight
        x_own.wait()
        for j in (3, 1, 2, 0):
            if j < sources - 1:
                x_copy(sources - 1 - j).wait_recv()
            for half in range(2):
                at = (j * 2 + half) * rows
                w = pad_rows(weight, half)
                qkv = (mm(x_buf[j, :, window(half)], w) + b).astype(BF16)
                q = qkv[:, :gw]
                kk = qkv[:, gw : 2 * gw]
                v = qkv[:, 2 * gw :]
                k_out[at : at + rows, :] = kk
                qT_out[:, at : at + rows] = q.T
                vT_out[:, at : at + rows] = v.T
                kT = kk.T
                scaled = q.astype(F32) * scale
                hi = scaled.astype(BF16)
                lo = (scaled - hi.astype(F32)).astype(BF16)
                ones = jnp.ones((rows, HD), BF16)
                for h in range(heads):
                    cols = slice(h * HD, (h + 1) * HD)
                    qe[h, at : at + rows, 0:128] = jnp.concatenate([hi[:, cols], lo[:, cols]], axis=1)
                    ke[h, 0:HD, at : at + rows] = kT[cols, :]
                    ke[h, HD : 2 * HD, at : at + rows] = kT[cols, :]
                    ve[h, at : at + rows, :] = jnp.concatenate([v[:, cols], ones], axis=1)
        x_keep.start()

    plan = {
        0: [(step_y, 0)], 1: [(step_y, 1)], 3: [(step_p, 0), (step_y, 2)], 5: [(step_p, 1)], 7: [(step_p, 2)],
    }
    for now, actions in plan.items():
        @pl.when(pl.program_id(0) == now)
        def _(actions=actions):
            for fn, w in actions:
                fn(w)

    parts = []
    inverse = []
    at = pl.multiple_of(pl.program_id(0) * rows, rows)
    for h in range(heads):
        scores = mm(qe[h, pl.ds(at, rows), :], ke[h])
        top = jnp.max(scores, axis=1, keepdims=True)
        e = jnp.exp2(scores - top).astype(BF16)
        e_ref[h] = e
        o = mm(e, ve[h])
        inv = 1.0 / o[:, HD:]
        inverse.append(inv)
        parts.append((o[:, :HD] * inv).astype(BF16))
    linv_ref[0, 0] = jnp.concatenate(inverse, axis=1)
    ctx_half[half_now] = jnp.concatenate(parts, axis=1)

    @pl.when(half_now == 1)
    def _():
        block = jnp.concatenate([ctx_half[0], ctx_half[1]], axis=1)
        ctx_ref[0] = block
        ctx_buf[t] = block
        for d in range(1, sources):
            @pl.when(t == d - 1)
            def _():
                ctx_copy(d).start()

    @pl.when(pl.program_id(0) == 2 * sources - 1)
    def _():
        ctx_own.start()
        for d in range(1, sources):
            x_copy(d).wait_send()
            r_copy(d).wait_send()
            ctx_copy(d).wait_send()
            ctx_copy(d).wait_recv()

        for d in range(1, n):
            q_copy(d).wait_send()
            v_copy(d).wait_send()
        for w in range(3):
            for d in range(1, depth):
                z_copy(w, d).wait_send()
            y_copy(w).wait_send()
            p_copy(w).wait()
        x_keep.wait()
        ctx_own.wait()


def attend(n, length, tok, wq, wo, wu, wd, vectors):
    sources, rows = GROUPS, tok.shape[0] // 2
    gw = 2 * wd.shape[1]
    heads = gw // HD
    slot = sources * 2 * rows
    depth = n // 2
    parts_q = n // GROUPS
    lanes = -(-max(v.shape[-1] for v in vectors) // 128) * 128
    block = (sources, rows, 2 * gw)
    whole = lambda *shape: pl.BlockSpec(shape, lambda s: (0,) * len(shape), pipeline_mode=pl.Buffered(1))
    out_whole = lambda *shape: pl.BlockSpec(shape, lambda s: (0,) * len(shape))
    anywhere = pl.BlockSpec(memory_space=pl.ANY)
    dma = lambda *shape: pltpu.SemaphoreType.DMA(shape)
    return pl.pallas_call(
        functools.partial(attend_kernel, n),
        grid=(2 * sources,),
        in_specs=[pl.BlockSpec(memory_space=pltpu.SMEM), whole(*tok.shape), anywhere]
        + [whole(*a.shape) for a in (wo, wu, wd) + vectors],
        out_specs=[
            pl.BlockSpec((1, rows, 2 * gw), lambda s: (s // 2, 0, 0)),
            pl.BlockSpec((1, 1, rows, gw), lambda s: (s // 2, lax.rem(s, 2), 0, 0)),
            pl.BlockSpec((heads, rows, slot), lambda s: (0, s, 0)),
            out_whole(slot, gw),
            out_whole(gw, slot),
            out_whole(gw, slot),
            out_whole(gw, 3 * gw),
            out_whole(n, 8, lanes),
            anywhere, anywhere, anywhere, anywhere, anywhere,
        ],
        out_shape=[
            jax.ShapeDtypeStruct(block, BF16),
            jax.ShapeDtypeStruct((sources, 2, rows, gw), F32),
            jax.ShapeDtypeStruct((heads, slot, slot), BF16),
            jax.ShapeDtypeStruct((slot, gw), BF16),
            jax.ShapeDtypeStruct((gw, slot), BF16),
            jax.ShapeDtypeStruct((gw, slot), BF16),
            jax.ShapeDtypeStruct((gw, 3 * gw), BF16),
            jax.ShapeDtypeStruct((n, 8, lanes), F32),
            jax.ShapeDtypeStruct(block, BF16),
            jax.ShapeDtypeStruct(block, BF16),
            jax.ShapeDtypeStruct((depth, 2) + wo.shape, BF16),
            jax.ShapeDtypeStruct((depth, 2) + wu.shape, BF16),
            jax.ShapeDtypeStruct((depth, 2) + wd.shape, BF16),
        ],
        scratch_shapes=[
            pltpu.VMEM((heads, slot, 256), BF16),
            pltpu.VMEM((heads, 256, slot), BF16),
            pltpu.VMEM((heads, slot, 128), BF16),
            pltpu.VMEM(block, BF16),
            pltpu.VMEM(block, BF16),
            pltpu.VMEM((2, rows, gw), BF16),
            pltpu.VMEM(block, BF16),
            pltpu.VMEM((n,) + wq.shape[1:], BF16),
            pltpu.VMEM((sources, parts_q) + wq.shape[1:], BF16),
            pltpu.VMEM((8, lanes), F32),
            pltpu.VMEM((n, 8, lanes), F32),
            dma(3), dma(3), dma(3), dma(3), dma(n - 1), dma(n - 1), dma(3), dma(3), dma(n - 1), dma(n - 1),
            dma(3, depth - 1), dma(3, depth - 1), dma(3), dma(3), dma(3), dma(3), dma(3), dma(6),
        ],
        compiler_params=pltpu.CompilerParams(vmem_limit_bytes=60 << 20, collective_id=1, has_side_effects=True),
        name="attend",
    )(length, tok, wq, wo, wu, wd, *vectors)


def revisit_kernel(
    n, per,
    e_ref, ctx_ref, linv_ref, qT_ref, vT_ref, k_ref, x_ref, w_ref, gctx_in, gwo_in, gwu_in, gwd_in, sm_in,
    gi_pos, gq_fin, gqv_out, gwo_out, gwu_out, gwd_out, sm_seq,
    vTe, kn, dkT, dvT, gT, gc_buf, gi_buf, sm_buf, sm_sum, gb_buf, gqv_buf, gq_buf, gq_got, gq_sum,
    mine0, mine1, mine2, core0, core1, core2, yb0, yb1, yb2, zb0, zb1, zb2, xm0, xm1, xm2, xb0, xb1, xb2, f0, f1, f2,
    g_send, g_recv, i_send, i_recv, sm_send, sm_recv, ss_send, ss_recv, b_send, b_recv, bs_send, bs_recv,
    q_send, q_recv, qs_send, qs_recv, c_send, c_recv, y_send, y_recv, z_send, z_recv, xs_send, xs_recv, p_send, p_recv, own, local,
):
    heads = kn.shape[0]
    sources, rows, _ = x_ref.shape
    gw = heads * HD
    slot = sources * 2 * rows
    parts_q = n // GROUPS
    u = pl.program_id(0)
    now = 2 * GROUPS - 1 - u
    half_now = lax.rem(now, 2)
    j = now // 2
    i = lax.axis_index("dp")
    me = lax.axis_index("seq")
    c = lax.rem(me, 2)
    y = lax.rem(i, 2)
    k = i // 2
    depth = n // 2
    across = lax.rem(me + 2, sources)
    every = slice(None)
    inputs = (gwo_in, gwu_in, gwd_in)
    outputs = (gwo_out, gwu_out, gwd_out)
    mine, core, ybuf, zbuf = (mine0, mine1, mine2), (core0, core1, core2), (yb0, yb1, yb2), (zb0, zb1, zb2)
    xmine, xbuf, final = (xm0, xm1, xm2), (xb0, xb1, xb2), (f0, f1, f2)

    def g_copy(d):
        peer = lax.rem(me + d, sources)
        return remote(gctx_in.at[peer], gc_buf.at[sources - 1 - d], g_send.at[d - 1], g_recv.at[d - 1], i, peer)

    def i_copy(d):
        return remote(gi_buf.at[d - 1], gi_pos.at[me], i_send.at[d - 1], i_recv.at[d - 1], i, lax.rem(me + d, sources))

    def sm_copy(d):
        to = lax.rem(i + d, n)
        return remote(sm_in.at[to], sm_buf.at[d - 1], sm_send.at[d - 1], sm_recv.at[d - 1], to, me)

    def ss_copy(d):
        return remote(sm_sum, sm_seq.at[me], ss_send.at[d - 1], ss_recv.at[d - 1], i, lax.rem(me + d, sources))

    def b_copy(d):
        return remote(gb_buf.at[i], gb_buf.at[i], b_send.at[d - 1], b_recv.at[d - 1], lax.rem(i + d, n), me)

    def bs_copy(d):
        return remote(gqv_buf, gqv_out, bs_send.at[d - 1], bs_recv, i, lax.rem(me + d, sources))

    def q_copy(d):
        to = lax.rem(i + d, n)
        return remote(gq_buf.at[to], gq_got.at[d - 1], q_send.at[d - 1], q_recv.at[d - 1], to, me)

    def qs_copy(d):
        spot = lax.rem(i, GROUPS)
        return remote(
            gq_sum, gq_fin.at[spot], qs_send.at[d], qs_recv.at[spot], me * parts_q + i // GROUPS, lax.rem(me + d, sources)
        )

    def own_copy(w):
        return pltpu.make_async_copy(half_of(inputs[w], (every, every), c), mine[w], own.at[w])

    def c_copy(w):
        return remote(half_of(inputs[w], (every, every), 1 - c), core[w], c_send.at[w], c_recv.at[w], i, other(me))

    def y_copy(w):
        return remote(mine[w].at[:, 1 - y], ybuf[w], y_send.at[w], y_recv.at[w], other(i), me)

    def z_copy(w, d):
        to = lax.rem(k + d, depth)
        return remote(mine[w].at[to, y], zbuf[w].at[d - 1], z_send.at[w, d - 1], z_recv.at[w, d - 1], to * 2 + y, me)

    def x_copy(w):
        return remote(xmine[w], xbuf[w], xs_send.at[w], xs_recv.at[w], i, across)

    def p_copy(w):
        return remote(final[w], outputs[w].at[c], p_send.at[w], p_recv.at[w], i, other(me))

    g_own = pltpu.make_async_copy(gctx_in.at[me], gc_buf.at[sources - 1], local.at[0])
    sm_own = pltpu.make_async_copy(sm_in.at[i], sm_buf.at[n - 1], local.at[1])
    ss_own = pltpu.make_async_copy(sm_sum, sm_seq.at[me], local.at[2])
    bs_own = pltpu.make_async_copy(gqv_buf, gqv_out, local.at[3])
    qs_own = pltpu.make_async_copy(gq_sum, gq_fin.at[lax.rem(i, GROUPS)], local.at[4])
    i_own = pltpu.make_async_copy(gi_buf.at[sources - 1], gi_pos.at[me], local.at[5])

    def p_own(w):
        return pltpu.make_async_copy(final[w], outputs[w].at[c], local.at[6 + w])

    stays = me * parts_q + i // GROUPS == i
    count = gw // per
    bias_owner = lax.rem(i // count, GROUPS) == me

    def step_y(w):
        own_copy(w).wait()
        c_copy(w).wait_recv()
        mine[w][...] += core[w][...]
        y_copy(w).start()

    def step_z(w):
        y_copy(w).wait_recv()
        mine[w][:, y] += ybuf[w][...]
        for d in range(1, depth):
            z_copy(w, d).start()

    def step_x(w):
        total = mine[w][k, y].astype(F32)
        for d in range(1, depth):
            z_copy(w, d).wait_recv()
            total += zbuf[w][d - 1].astype(F32)
        xmine[w][...] = total.astype(BF16)
        x_copy(w).start()

    def step_p(w):
        x_copy(w).wait_recv()
        final[w][...] = xmine[w][...].astype(F32) + xbuf[w][...].astype(F32)
        p_copy(w).start()
        p_own(w).start()

    def small_sum():
        sm_own.wait()
        total = sm_buf[n - 1]
        for d in range(1, n):
            sm_copy(d).wait_recv()
            total += sm_buf[d - 1]
        sm_sum[...] = total
        ss_own.start()
        for d in range(1, sources):
            ss_copy(d).start()

    @pl.when(u == 0)
    def _():
        greet(n, sources, i, me)
        for d in (1, 2, 3):
            g_copy(d).start()
        g_own.start()
        for w in range(3):
            c_copy(w).start()
            own_copy(w).start()
        sm_own.start()
        for d in range(1, n):
            sm_copy(d).start()
        dkT[...] = jnp.zeros_like(dkT)
        dvT[...] = jnp.zeros_like(dvT)
        row = lax.broadcasted_iota(jnp.int32, (HD, slot), 0)
        ones_rows = jnp.where(row < 2, 1.0, 0.0).astype(BF16)
        for h in range(heads):
            cols = slice(h * HD, (h + 1) * HD)
            vTe[h, 0:HD, :] = vT_ref[cols, :]
            vTe[h, HD:, :] = ones_rows
            kn[h] = k_ref[:, cols]
        g_own.wait()

    for d in range(1, sources):
        @pl.when(u == 2 * d)
        def _(d=d):
            g_copy(d).wait_recv()

    plan = {
        1: [(step_y, 0), (step_y, 1)], 2: [(step_y, 2)], 3: [(step_z, 0)], 5: [(step_z, 1)], 6: [(step_x, 0)],
        7: [(step_z, 2), (step_x, 1), (step_p, 0)],
    }
    for when_u, actions in plan.items():
        @pl.when(u == when_u)
        def _(actions=actions):
            for fn, w in actions:
                fn(w)

    @pl.when(u == 4)
    def _():
        small_sum()

    lane = lax.broadcasted_iota(jnp.int32, (rows, HD), 1)
    at = pl.multiple_of(now * rows, rows)
    both = gc_buf[j].astype(F32)
    g = jnp.where(half_now == 0, both[:, :gw], both[:, gw:]) * linv_ref[0, 0]
    g_low = g.astype(BF16)
    gT_low = g_low.T
    both = ctx_ref[0].astype(F32)
    prod = g * jnp.where(half_now == 0, both[:, :gw], both[:, gw:])
    dqs = []
    for h in range(heads):
        cols = slice(h * HD, (h + 1) * HD)
        delta = -jnp.sum(prod[:, cols], axis=1, keepdims=True)
        d_hi = delta.astype(BF16)
        d_lo = (delta - d_hi.astype(F32)).astype(BF16)
        tail = jnp.where(lane == 0, d_hi, jnp.where(lane == 1, d_lo, jnp.zeros((), BF16)))
        ge = jnp.concatenate([g_low[:, cols], tail], axis=1)
        e = e_ref[h]
        ds = (e.astype(F32) * mm(ge, vTe[h])).astype(BF16)
        dvT[cols, :] += mm(gT_low[cols, :], e)
        dkT[cols, :] += mm(qT_ref[cols, :], ds)
        dqs.append((mm(ds, kn[h]) * (HD ** (-0.5))).astype(BF16))
    gT[0:gw, pl.ds(at, rows)] = jnp.concatenate(dqs, axis=1).T

    @pl.when(u == 2 * sources - 1)
    def _():
        gT[gw : 2 * gw, :] = (dkT[...] * (HD ** (-0.5))).astype(BF16)
        gT[2 * gw :, :] = dvT[...].astype(BF16)
        sums = [None, None]
        for q in range(sources):
            for half in range(2):
                part = mm(gT[:, (q * 2 + half) * rows : (q * 2 + half + 1) * rows], x_ref[q, :, window(half)])
                sums[half] = part if sums[half] is None else sums[half] + part
        gq = (sums[0][:, :gw] + sums[1][:, 64:]).T
        size = gw // n
        for piece in range(n):
            gq_buf[piece] = gq[piece * size : (piece + 1) * size].astype(BF16)
        gb_buf[i] = mm_nt(jnp.ones((8, slot), BF16), gT[...])
        ready = 0
        for q in (1, 0, 2, 3):
            packed = [
                mm(w_ref[...], gT[:, (q * 2 + half) * rows : (q * 2 + half + 1) * rows]).T.astype(BF16)
                for half in range(2)
            ]
            block = jnp.concatenate(packed, axis=1)
            if ready:
                i_copy(ready).start()
            else:
                for d in range(1, n):
                    q_copy(d).start()
                for d in range(1, n):
                    b_copy(d).start()
            gi_buf[q] = block
            ready = q + 1
        i_own.start()
        step_x(2)
        step_p(1)
        total = gq_buf[i].astype(F32)
        for d in range(1, n):
            q_copy(d).wait_recv()
            total += gq_got[d - 1].astype(F32)
        gq_sum[...] = total.astype(BF16)
        for d in range(1, n):
            b_copy(d).wait_recv()

        @pl.when(bias_owner)
        def _():
            total = gb_buf[0, 0:1, :]
            for d in range(1, n):
                total += gb_buf[d, 0:1, :]
            side = jnp.where(i < n // 2, total[:, :gw], total[:, 2 * gw :])
            piece = lax.rem(i, count)
            value = side[:, 0:per]
            for v in range(1, count):
                value = jnp.where(piece == v, side[:, v * per : (v + 1) * per], value)
            gqv_buf[0:1, 0:per] = value
            bs_own.start()
            for d in range(1, sources):
                bs_copy(d).start()

        for d in range(1, sources):
            qs_copy(d).start()

        @pl.when(stays)
        def _():
            qs_own.start()

        @pl.when(jnp.logical_not(stays))
        def _():
            qs_copy(0).start()

        step_p(2)

        ss_own.wait()
        i_own.wait()
        for d in range(1, sources):
            ss_copy(d).wait_recv()
            i_copy(d).wait_recv()
        for w in range(3):
            p_copy(w).wait_recv()
            p_own(w).wait()

        @pl.when(jnp.logical_not(bias_owner))
        def _():
            bs_copy(1).wait_recv()

        for spot in range(GROUPS):
            source = lax.rem(i, parts_q) * GROUPS + spot

            @pl.when(jnp.logical_not(jnp.logical_and(i // parts_q == me, source == i)))
            def _():
                remote(gq_sum, gq_fin.at[spot], qs_send.at[0], qs_recv.at[spot], other(i), me).wait_recv()

        for d in range(1, sources):
            g_copy(d).wait_send()
            i_copy(d).wait_send()
            ss_copy(d).wait_send()

        @pl.when(bias_owner)
        def _():
            bs_own.wait()
            for d in range(1, sources):
                bs_copy(d).wait_send()

        for d in range(1, sources):
            qs_copy(d).wait_send()

        @pl.when(stays)
        def _():
            qs_own.wait()

        @pl.when(jnp.logical_not(stays))
        def _():
            qs_copy(0).wait_send()

        for d in range(1, n):
            q_copy(d).wait_send()
        for d in range(1, n):
            sm_copy(d).wait_send()
            b_copy(d).wait_send()
        for w in range(3):
            c_copy(w).wait_send()
            y_copy(w).wait_send()
            for d in range(1, depth):
                z_copy(w, d).wait_send()
            x_copy(w).wait_send()
            p_copy(w).wait_send()


def revisit(n, per, e, ctx, linv, qT, vT, k, x, w, gctx, gwo, gwu, gwd, small):
    sources, rows, _ = x.shape
    gw = w.shape[0]
    heads = gw // HD
    slot = sources * 2 * rows
    depth = n // 2
    last = 2 * sources - 1
    whole = lambda *shape: pl.BlockSpec(shape, lambda s: (0,) * len(shape), pipeline_mode=pl.Buffered(1))
    anywhere = pl.BlockSpec(memory_space=pl.ANY)
    dma = lambda *shape: pltpu.SemaphoreType.DMA(shape)

    def half_shape(a):
        return a.shape[3:] if len(a.shape) == 5 else (a.shape[2], a.shape[3] // 2)

    halves = [half_shape(a) for a in (gwo, gwu, gwd)]
    outs = [
        jax.ShapeDtypeStruct(x.shape, BF16),
        jax.ShapeDtypeStruct((GROUPS, gw // n, 3 * gw), BF16),
        jax.ShapeDtypeStruct((8, 256), F32),
        jax.ShapeDtypeStruct((2,) + halves[0], F32),
        jax.ShapeDtypeStruct((2,) + halves[1], F32),
        jax.ShapeDtypeStruct((2,) + halves[2], F32),
        jax.ShapeDtypeStruct((sources,) + small.shape[1:], F32),
    ]
    vmem = pltpu.VMEM
    return pl.pallas_call(
        functools.partial(revisit_kernel, n, per),
        grid=(2 * sources,),
        in_specs=[
            pl.BlockSpec((heads, rows, slot), lambda s: (0, last - s, 0)),
            pl.BlockSpec((1, rows, 2 * gw), lambda s: ((last - s) // 2, 0, 0)),
            pl.BlockSpec((1, 1, rows, gw), lambda s: ((last - s) // 2, lax.rem(last - s, 2), 0, 0)),
            pl.BlockSpec((gw, rows), lambda s: (0, last - s)),
            whole(*vT.shape), whole(*k.shape), whole(*x.shape), whole(*w.shape),
            anywhere, anywhere, anywhere, anywhere, anywhere,
        ],
        out_specs=[anywhere] * len(outs),
        out_shape=outs,
        scratch_shapes=[
            vmem((heads, 2 * HD, slot), BF16),
            vmem((heads, slot, HD), BF16),
            vmem((gw, slot), F32),
            vmem((gw, slot), F32),
            vmem((3 * gw, slot), BF16),
            vmem(x.shape, BF16), vmem(x.shape, BF16),
            vmem(small.shape, F32), vmem(small.shape[1:], F32),
            vmem((n, 8, 3 * gw), F32), vmem((8, 256), F32),
            vmem((n, gw // n, 3 * gw), BF16),
            vmem((n - 1, gw // n, 3 * gw), BF16),
            vmem((gw // n, 3 * gw), BF16),
        ]
        + [vmem((depth, 2) + s, BF16) for s in halves]
        + [vmem((depth, 2) + s, BF16) for s in halves]
        + [vmem((depth,) + s, BF16) for s in halves]
        + [vmem((depth - 1,) + s, BF16) for s in halves]
        + [vmem(s, BF16) for s in halves]
        + [vmem(s, BF16) for s in halves]
        + [vmem(s, F32) for s in halves]
        + [
            dma(3), dma(3), dma(3), dma(3), dma(n - 1), dma(n - 1), dma(3), dma(3), dma(n - 1), dma(n - 1),
            dma(3), pltpu.SemaphoreType.DMA, dma(n - 1), dma(n - 1), dma(4), dma(4),
            dma(3), dma(3), dma(3), dma(3), dma(3, depth - 1), dma(3, depth - 1), dma(3), dma(3), dma(3), dma(3), dma(3), dma(9),
        ],
        compiler_params=pltpu.CompilerParams(vmem_limit_bytes=62 << 20, collective_id=2, has_side_effects=True),
        name="revisit",
    )(e, ctx, linv, qT, vT, k, x, w, gctx, gwo, gwu, gwd, small)


def split_rows(values):
    mean = jnp.mean(values, axis=-1, keepdims=True)
    centred = values - mean
    var = jnp.mean(centred * centred, axis=-1, keepdims=True)
    return centred, lax.rsqrt(var + epsilon)


def norm_back(grad, unit, inverse, gain):
    g = grad * gain
    m1 = jnp.mean(g, axis=-1, keepdims=True)
    m2 = jnp.mean(g * unit, axis=-1, keepdims=True)
    return inverse * (g - m1 - unit * m2)


def join_windows(parts):
    tiles = []
    for even, odd in zip(parts[0::2], parts[1::2]):
        tiles += [even[:, :128], even[:, 128:] + odd[:, :128], odd[:, 128:]]
    return jnp.concatenate(tiles, axis=1)


def group_window(g):
    at = (g // 2) * 384 + (g % 2) * 128
    return slice(at, at + 256)


def middle_kernel(
    n, len_ref, ctx_ref, tok_ref, gout_ref, wo_ref, wu_ref, wd_ref, vec_ref,
    out_ref, gctx_ref, gres_ref, gwo_ref, gwu_ref, gwd_ref, small_ref, upad, dpad, awo, awu, awd, sums, usums,
):
    rows = ctx_ref.shape[1]
    gw = ctx_ref.shape[2] // 2
    width = tok_ref.shape[1]
    hidden = wu_ref.shape[1]
    share = width // n
    first_row = lax.axis_index("seq") * (2 * rows)
    vec = join_lanes([vec_ref[d, :, 0:share] for d in range(n)])
    obias, gain1, shift1, dbias, gain2, shift2 = (vec[v : v + 1] for v in range(1, 7))
    count = n // GROUPS
    for g in range(GROUPS):
        upad[g] = pad_rows(wu_ref[g * gw : (g + 1) * gw, :], g % 2)
        odd = 64 * (g % 2)
        dpad[g, 192 * (1 - g % 2) : 192 * (1 - g % 2) + 64, :] = jnp.zeros((64, hidden), BF16)
        size = hidden // count
        for d in range(count):
            for v in range(2):
                at = odd + v * (gw // 2)
                dpad[g, at : at + gw // 2, d * size : (d + 1) * size] = wd_ref[g * count + d, v]
    packed = [[] for _ in range(GROUPS)]
    for half in range(2):
        first = half == 0

        def keep(ref, at, value):
            if first:
                ref[at] = value
            else:
                ref[at] += value

        r = slice(half * rows, (half + 1) * rows)
        x = tok_ref[r, :].astype(F32) + obias
        for g in range(GROUPS):
            x += mm(ctx_ref[g, :, window(half)], pad_rows(wo_ref[g * gw : (g + 1) * gw, :], half))
        c1, i1 = split_rows(x)
        n1 = c1 * i1
        mixed = n1 * gain1 + shift1
        low = mixed.astype(BF16)
        lowered = []
        slopes = []
        actives = []
        for g in range(GROUPS):
            ub = join_lanes([vec_ref[g * count + d, 7:8, 0 : hidden // count] for d in range(count)])
            u = mm(low[:, group_window(g)], upad[g]) + ub
            phi = 0.5 + 0.5 * lax.erf(u * (0.5 ** 0.5))
            slope = phi + u * (jnp.exp(u * u * -0.5) * 0.3989422804014327)
            act = (u * phi).astype(BF16)
            actives.append(act)
            slopes.append(slope)
            lowered.append(mm_nt(act, dpad[g]))
        x = mixed + join_windows(lowered) + dbias
        c2, i2 = split_rows(x)
        n2 = c2 * i2
        row = lax.broadcasted_iota(jnp.int32, (rows, 1), 0) + (first_row + half * rows)
        valid = jnp.where(row < len_ref[0], 1.0, 0.0)
        out_ref[r, :] = (valid * (n2 * gain2 + shift2)).astype(BF16)
        gy = gout_ref[r, :].astype(F32) * valid
        d2 = norm_back(gy, n2, i2, gain2)
        keep(sums, slice(4, 5), jnp.sum(gy * n2, axis=0, keepdims=True))
        keep(sums, slice(5, 6), jnp.sum(gy, axis=0, keepdims=True))
        keep(sums, slice(3, 4), jnp.sum(d2, axis=0, keepdims=True))
        d2_low = d2.astype(BF16)
        backs = []
        for g in range(GROUPS):
            win = d2_low[:, group_window(g)]
            odd = 64 * (g % 2)
            part = mm_tn(win, actives[g])[odd : odd + gw]
            if first:
                awd[g] = part
            else:
                part = (awd[g] + part).astype(BF16)
                size = hidden // count
                for d in range(count):
                    for v in range(2):
                        gwd_ref[g * count + d, v] = part[v * (gw // 2) : (v + 1) * (gw // 2), d * size : (d + 1) * size]
            gu = mm(win, dpad[g]) * slopes[g]
            keep(usums, slice(g, g + 1), jnp.sum(gu, axis=0, keepdims=True))
            gu_low = gu.astype(BF16)
            part = mm_tn(low[:, group_window(g)], gu_low)[odd : odd + gw]
            if first:
                awu[g] = part
            else:
                gwu_ref[g * gw : (g + 1) * gw, :] = (awu[g] + part).astype(BF16)
            backs.append(mm_nt(gu_low, upad[g]))
        gm = join_windows(backs) + d2
        d1 = norm_back(gm, n1, i1, gain1)
        keep(sums, slice(1, 2), jnp.sum(gm * n1, axis=0, keepdims=True))
        keep(sums, slice(2, 3), jnp.sum(gm, axis=0, keepdims=True))
        keep(sums, slice(0, 1), jnp.sum(d1, axis=0, keepdims=True))
        gres_ref[r, :] = d1
        d1_low = d1.astype(BF16)
        for g in range(GROUPS):
            part = mm_tn(ctx_ref[g, :, window(half)], d1_low)[64 * half : 64 * half + gw]
            if first:
                awo[g] = part
            else:
                gwo_ref[g * gw : (g + 1) * gw, :] = (awo[g] + part).astype(BF16)
        back = mm_nt(d1_low, wo_ref[...]).astype(BF16)
        for g in range(GROUPS):
            packed[g].append(back[:, g * gw : (g + 1) * gw])
    for g in range(GROUPS):
        gctx_ref[g] = jnp.concatenate(packed[g], axis=1)
    sums[6:8, :] = jnp.zeros((2, width), F32)
    up_share = hidden // count
    for d in range(n):
        small_ref[d] = jnp.zeros(small_ref.shape[1:], F32)
        small_ref[d, 0:8, 0:share] = sums[0:8, d * share : (d + 1) * share]
        at = (d % count) * up_share
        for v in range(0, up_share, 128):
            size = min(128, up_share - v)
            small_ref[d, 8 + v // 128 : 9 + v // 128, 0:size] = usums[d // count : d // count + 1, at + v : at + v + size]


def middle(n, length, ctx, tok, gout, wo, wu, wd, vec):
    hidden = wu.shape[1]
    width = tok.shape[1]
    gw = width // GROUPS
    vmem = pl.BlockSpec(memory_space=pltpu.VMEM)
    return pl.pallas_call(
        functools.partial(middle_kernel, n),
        in_specs=[pl.BlockSpec(memory_space=pltpu.SMEM)] + [vmem] * 7,
        out_specs=[vmem] * 7,
        out_shape=[
            jax.ShapeDtypeStruct(tok.shape, BF16),
            jax.ShapeDtypeStruct(ctx.shape, BF16),
            jax.ShapeDtypeStruct(tok.shape, F32),
            jax.ShapeDtypeStruct(wo.shape, BF16),
            jax.ShapeDtypeStruct(wu.shape, BF16),
            jax.ShapeDtypeStruct(wd.shape, BF16),
            jax.ShapeDtypeStruct((n, 16, 128), F32),
        ],
        scratch_shapes=[
            pltpu.VMEM((GROUPS, 256, hidden), BF16),
            pltpu.VMEM((GROUPS, 256, hidden), BF16),
            pltpu.VMEM((GROUPS, gw, width), F32),
            pltpu.VMEM((GROUPS, gw, hidden), F32),
            pltpu.VMEM((GROUPS, gw, hidden), F32),
            pltpu.VMEM((8, width), F32),
            pltpu.VMEM((8, hidden), F32),
        ],
        compiler_params=pltpu.CompilerParams(vmem_limit_bytes=62 << 20),
        name="middle",
    )(length, ctx, tok, gout, wo, wu, wd, vec)


def finish_kernel(
    gi_ref, gres_ref, gq_ref, gqv_ref, gwo_ref, gwu_ref, gwd_ref, sm_ref,
    tok_out, qkv_out, qv_out, wo_out, b0_out, b1_out, b2_out, wu_out, up_out, wd_out, b3_out, b4_out, b5_out,
):
    rows = gi_ref.shape[1]
    gw = gi_ref.shape[2] // 2
    for half in range(2):
        r = slice(half * rows, (half + 1) * rows)
        lanes = slice(half * gw, (half + 1) * gw)
        for pair in range(GROUPS // 2):
            both = jnp.concatenate([gi_ref[2 * pair, :, lanes], gi_ref[2 * pair + 1, :, lanes]], axis=1)
            wide = slice(pair * 2 * gw, (pair + 1) * 2 * gw)
            tok_out[r, wide] = (both.astype(F32) + gres_ref[r, wide]).astype(BF16)
    qkv_out[...] = jnp.concatenate([gq_ref[v].astype(F32) for v in range(gq_ref.shape[0])], axis=0)
    qv_out[...] = gqv_ref[0:1, 0 : qv_out.shape[-1]].reshape(qv_out.shape)
    for ref, out in ((gwo_ref, wo_out), (gwu_ref, wu_out)):
        out[...] = jnp.concatenate([ref[0], ref[1]], axis=1)
    size = gwd_ref.shape[1]
    for v in range(2):
        wd_out[v * size : (v + 1) * size, :] = gwd_ref[v]
    total = sm_ref[0] + sm_ref[1] + sm_ref[2] + sm_ref[3]
    for v, out in enumerate((b0_out, b1_out, b2_out, b3_out, b4_out, b5_out)):
        out[...] = total[v : v + 1, 0 : out.shape[1]]
    size = up_out.shape[-1]
    pieces = [total[8 + v // 128 : 9 + v // 128, 0 : min(128, size - v)] for v in range(0, size, 128)]
    up_out[...] = join_lanes(pieces).reshape(up_out.shape)


def finish(shapes, *args):
    vmem = pl.BlockSpec(memory_space=pltpu.VMEM)
    return pl.pallas_call(
        finish_kernel,
        in_specs=[vmem] * len(args),
        out_specs=[vmem] * len(shapes),
        out_shape=[jax.ShapeDtypeStruct(s, BF16 if v == 0 else F32) for v, s in enumerate(shapes)],
        compiler_params=pltpu.CompilerParams(vmem_limit_bytes=60 << 20),
        name="finish",
    )(*args)


def on_device(
    tokens, lengths, qkv_weight, qv_bias, out_weight, out_bias, norm_gain, norm_shift,
    up_weight, up_bias, down_weight, down_bias, final_gain, final_shift, grad_output,
):
    n = lax.axis_size("dp")
    width = tokens.shape[2]
    per = qv_bias.shape[0]
    vectors = tuple(
        a[None] if a.shape[0] <= 128 else a for a in (qv_bias, out_bias, norm_gain, norm_shift, down_bias, final_gain, final_shift, up_bias)
    )
    wq = qkv_weight.reshape(GROUPS, qkv_weight.shape[0] // GROUPS, qkv_weight.shape[1])
    wd_halves = down_weight.T.reshape(2, down_weight.shape[1] // 2, down_weight.shape[0])
    ctx, linv, e, k, qT, vT, w, vecs, x_all, ctx_pos, wo, wu, wd = attend(
        n, lengths, tokens[0], wq, out_weight, up_weight, wd_halves, vectors
    )
    output, gctx, gres, gwo, gwu, gwd, small = middle(
        n, lengths, ctx_pos, tokens[0], grad_output[0],
        wo.reshape(width, width), wu.reshape(width, -1), wd.reshape((n,) + wd.shape[2:]), vecs,
    )
    parts = revisit(
        n, per, e, ctx, linv, qT, vT, k, x_all, w, gctx,
        gwo.reshape(wo.shape), gwu.reshape(wu.shape), gwd.reshape(wd.shape), small,
    )
    one = lambda a: (1, a.shape[0]) if a.shape[0] <= 128 else a.shape
    shapes = (
        tokens.shape[1:], qkv_weight.shape, one(qv_bias), out_weight.shape, one(out_bias), one(norm_gain),
        one(norm_shift), up_weight.shape, one(up_bias), down_weight.shape[::-1], one(down_bias), one(final_gain), one(final_shift),
    )
    outs = list(finish(shapes, parts[0], gres, *parts[1:]))
    outs[9] = outs[9].T
    flat = [a[0] if a.shape[0] == 1 else a for a in outs[1:]]
    return (output[None], outs[0][None], *flat)


def solution(mesh):
    rows = P("dp", "seq", None)
    mat = P("dp", None)
    vec = P("dp")
    in_specs = (rows, vec, mat, vec, mat, vec, vec, vec, mat, vec, mat, vec, vec, vec, rows)
    out_specs = (rows, rows, mat, vec, mat, vec, vec, vec, mat, vec, mat, vec, vec, vec)
    return jax.shard_map(on_device, mesh=mesh, in_specs=in_specs, out_specs=out_specs, check_vma=False)
```
